32 devices in a mesh: groups: 2 (over y), chan: 8 (over z, x), win: 2 (over core).
Axes of the slice: x: 2, y: 2, z: 4, core: 2. Of those that a mesh axis runs over, the one named last changes fastest.
Arguments:
- records: bfloat16 [8192, 512], P(('groups', 'chan', 'win')), parts along dimension 0
- record_channel: int32 [8192], P(('groups', 'chan', 'win')), parts along dimension 0, may hold values from 0 to 127, as said below
- record_piece: int32 [8192], P(('groups', 'chan', 'win')), parts along dimension 0, may hold values from 0 to 15
- fir_taps: bfloat16 [32], replicated, may hold values from -1 to 1
- window_starts: int32 [32], P(('groups', 'win')), parts along dimension 0, may hold values from 0 to 1024, as said below
- source_slot: int32 [16], P(('groups', 'chan')), parts along dimension 0, may hold values from 0 to 15
Outputs:
- correlations: float32 [16, 128, 256], P(('groups', 'win'), 'chan'), parts along dimension 0
The draws below stay inside these ranges and needn't reach their ends.
There are 2 independent parts, one for each index of `groups`. The reference program is written for one: setup_inputs(seed, part) draws one part's arguments, and reference() takes and returns one part's arrays. A program takes and returns all parts, laid end to end along the dimension named above; an argument that names none is the same for every part. Nothing has to cross between parts.
Inputs may be any that keep to these rules, and one draw needn't show every extreme that they name: `record_channel`: record r sits on the device r // 256 of chan and win joined, chan slowest. Among the records of one time span each pair of a channel and a piece occurs exactly once. The records of one device hold at most 64 records whose channels lie in any one block of 16 consecutive channels, and in every span some device holds exactly 64 of one block. `window_starts`: window w belongs to span w // 8; the first window of the minute starts at 0 and the last at 1024.
All inputs are finite; a program needn't handle non-finite values.
Results may differ from the reference program's by a relative error of at most 0.0041.
Values may be sent and summed in bfloat16 or wider, within the bound.
No kernel may reach another device: no remote copies, remote signals or barrier semaphores. Data moves between devices by JAX's collectives and lax.ppermute only.
A program may use at most 64 MiB of HBM per device.

```python
import math
import jax
import jax.numpy as jnp
from jax import lax

CH_DEV = 16
SPAN = 2048
WIN_DEV = 8
WL = 1024
NF = 512
DEC = 4
TAPS = 32
SPILL = 7
SEG = 512
PIECES = 16
BAND = 64
LAGS = 256
CHANNELS = 128
SOURCES = 8
WINDOWS = 16
RECORDS = 4096


def spread_rows(base_key):
    block_total = CHANNELS // CH_DEV
    span_total = WINDOWS // WIN_DEV
    per_device = CH_DEV * PIECES
    average = per_device // block_total
    swing = average // 2

    def one_span(span_key):
        subkeys = jax.random.split(span_key, 5)
        positions = jnp.arange(block_total, dtype=jnp.int32)
        pattern = jnp.where(positions < 2, 2, 1) * jnp.where(positions % 2 == 0, 1, -1)
        levels = jax.random.permutation(subkeys[0], pattern)
        sender_shift = jax.random.permutation(subkeys[1], block_total)
        owner_shift = jax.random.permutation(subkeys[2], block_total)
        counts = average + swing * levels[(sender_shift[:, None] + owner_shift[None, :]) % block_total]
        orders = jax.vmap(lambda subkey: jax.random.permutation(subkey, block_total))(jax.random.split(subkeys[3], block_total))
        ranks = jnp.argsort(orders, axis=1, stable=True).T
        earlier = ranks[None, :, :] < ranks[:, None, :]
        offsets = jnp.sum(jnp.where(earlier, counts[None, :, :], 0), axis=1)
        run_ends = jnp.cumsum(counts, axis=1)
        run_begins = run_ends - counts
        row_index = jnp.arange(per_device, dtype=jnp.int32)
        owners = jnp.sum((run_ends[:, None, :] <= row_index[None, :, None]).astype(jnp.int32), axis=2)
        begin_chosen = jnp.take_along_axis(run_begins, owners, axis=1)
        offset_chosen = jnp.take_along_axis(offsets, owners, axis=1)
        item_index = offset_chosen + row_index[None, :] - begin_chosen
        channel_ids = owners * CH_DEV + item_index % CH_DEV
        piece_ids = item_index // CH_DEV
        shuffles = jax.vmap(lambda subkey: jax.random.permutation(subkey, per_device))(jax.random.split(subkeys[4], block_total))
        channel_ids = jnp.take_along_axis(channel_ids, shuffles, axis=1)
        piece_ids = jnp.take_along_axis(piece_ids, shuffles, axis=1)
        return (channel_ids, piece_ids)
    channel_ids, piece_ids = jax.vmap(one_span)(jax.random.split(base_key, span_total))
    channel_ids = jnp.transpose(channel_ids, (1, 0, 2)).reshape(-1).astype(jnp.int32)
    piece_ids = jnp.transpose(piece_ids, (1, 0, 2)).reshape(-1).astype(jnp.int32)
    return (channel_ids, piece_ids)


def draw_record_channel(key, part):
    channel_ids, piece_ids = spread_rows(jax.random.fold_in(key, 11))
    return channel_ids


def draw_record_piece(key, part):
    channel_ids, piece_ids = spread_rows(jax.random.fold_in(key, 11))
    return piece_ids


def draw_records(key, part):
    channel_ids, piece_ids = spread_rows(jax.random.fold_in(key, 11))
    levels = jax.random.uniform(jax.random.fold_in(key, 12), (CHANNELS,), jnp.float32)
    gains = jnp.exp(math.log(10.0) * levels)
    row_gain = gains[channel_ids]
    values = row_gain[:, None] * jax.random.normal(jax.random.fold_in(key, 13), (RECORDS, SEG), jnp.float32)
    return values.astype(jnp.bfloat16)


def draw_window_starts(key, part):
    chosen_starts = jax.random.randint(jax.random.fold_in(key, 21), (WINDOWS,), 0, SPAN - WL + 1)
    position = jnp.arange(WINDOWS, dtype=jnp.int32)
    chosen_starts = jnp.where(position == 0, 0, jnp.where(position == WINDOWS - 1, SPAN - WL, chosen_starts))
    return chosen_starts.astype(jnp.int32)


def with_ends(values, rng, low, high):
    longest = values.shape.index(max(values.shape))
    spots = []
    for shift in (0, 1):
        where = [jax.random.randint(jax.random.fold_in(rng, axis), (), 0, length) for axis, length in enumerate(values.shape)]
        where[longest] = (where[longest] + shift) % values.shape[longest]
        spots.append(tuple(where))
    return values.at[spots[0]].set(low).at[spots[1]].set(high)


def normal_values(rng, shape, width, limit, held_as=jnp.bfloat16):
    values = width * jax.random.normal(rng, shape, jnp.float32)
    return jnp.clip(values, min=-limit, max=limit).astype(held_as)


def setup_inputs(seed: int = 0, part: int = 0) -> dict:
    key_list = jax.random.split(jax.random.key(seed), 7)
    own_keys = jax.random.split(jax.random.fold_in(key_list[6], part), 7)
    return {
        "records": draw_records(jax.random.fold_in(jax.random.fold_in(key_list[6], part), 71), part),
        "record_channel": draw_record_channel(jax.random.fold_in(jax.random.fold_in(key_list[6], part), 71), part),
        "record_piece": draw_record_piece(jax.random.fold_in(jax.random.fold_in(key_list[6], part), 71), part),
        "fir_taps": normal_values(key_list[3], (TAPS,), TAPS ** -0.5, 1.0),
        "window_starts": draw_window_starts(jax.random.fold_in(jax.random.fold_in(key_list[6], part), 71), part),
        "source_slot": with_ends(jax.random.randint(own_keys[5], (SOURCES,), 0, CH_DEV), jax.random.fold_in(own_keys[5], 1), 0, CH_DEV - 1).astype(jnp.int32),
    }


EPSILON = 1e-06

def make_filter(fir_taps):
    outputs_per = SEG // DEC
    sample_index = jnp.arange(SEG, dtype=jnp.int32)[:, None]
    column_index = jnp.arange(outputs_per + SPILL, dtype=jnp.int32)[None, :]
    tap_index = jnp.where(column_index < outputs_per, DEC * column_index + DEC - 1 - sample_index, DEC * (column_index - outputs_per) + DEC - 1 + SEG - sample_index)
    match_table = (tap_index[:, :, None] == jnp.arange(TAPS, dtype=jnp.int32)[None, None, :]).astype(jnp.float32)
    return lax.optimization_barrier(jnp.sum(match_table * fir_taps.astype(jnp.float32)[None, None, :], axis=2)).astype(jnp.bfloat16)

def make_fourier():
    sample_index = jnp.arange(WL, dtype=jnp.int32)[:, None]
    freq_index = jnp.arange(NF, dtype=jnp.int32)[None, :]
    phase = 2.0 * math.pi * (sample_index * freq_index % WL).astype(jnp.float32) / WL
    return jnp.concatenate([jnp.cos(phase), -jnp.sin(phase)], axis=1).astype(jnp.bfloat16)

def make_taper():
    sample_index = jnp.arange(WL, dtype=jnp.int32).astype(jnp.float32)
    return 0.5 - 0.5 * jnp.cos(2.0 * math.pi * sample_index / WL)

def make_lags():
    freq_index = jnp.arange(NF, dtype=jnp.int32)[:, None]
    lag_index = jnp.arange(LAGS, dtype=jnp.int32)[None, :] - LAGS // 2
    phase = 2.0 * math.pi * (freq_index * lag_index % WL).astype(jnp.float32) / WL
    scale = 1.0 / math.sqrt(WL * WIN_DEV)
    return (jnp.concatenate([jnp.cos(phase), -jnp.sin(phase)], axis=0) * scale).astype(jnp.bfloat16)

def whiten(spectra):
    freq_index = jnp.arange(NF, dtype=jnp.int32)
    band_table = (jnp.abs(freq_index[:, None] - freq_index[None, :]) <= BAND).astype(jnp.float32)
    band_count = lax.optimization_barrier(jnp.sum(band_table, axis=0))
    real_part = spectra[..., :NF]
    imag_part = spectra[..., NF:]
    energy = real_part * real_part + imag_part * imag_part
    smooth = jnp.dot(energy.reshape(-1, NF), band_table, precision=lax.Precision.HIGHEST) / band_count[None, :]
    amplitude = jnp.sqrt(smooth + EPSILON).reshape(energy.shape)
    return (spectra / jnp.concatenate([amplitude, amplitude], axis=-1)).astype(jnp.bfloat16)

def cross_spectrum(source_block, local_block):
    src_real = source_block[..., :NF].astype(jnp.float32)
    src_imag = source_block[..., NF:].astype(jnp.float32)
    loc_real = local_block[..., :NF].astype(jnp.float32)
    loc_imag = local_block[..., NF:].astype(jnp.float32)
    real_sum = jnp.einsum('bwf,cwf->bcf', src_real, loc_real) + jnp.einsum('bwf,cwf->bcf', src_imag, loc_imag)
    imag_sum = jnp.einsum('bwf,cwf->bcf', src_imag, loc_real) - jnp.einsum('bwf,cwf->bcf', src_real, loc_imag)
    return jnp.concatenate([real_sum, imag_sum], axis=-1).astype(jnp.bfloat16)

def reference(records, record_channel, record_piece, fir_taps, window_starts, source_slot):
    span_total = WINDOWS // WIN_DEV
    per_device = CH_DEV * PIECES
    outputs_per = SEG // DEC
    record_index = jnp.arange(RECORDS, dtype=jnp.int32)
    span_of = record_index // per_device % span_total
    target = (span_of * CHANNELS + record_channel) * PIECES + record_piece
    traces = jnp.zeros((span_total * CHANNELS * PIECES, SEG), jnp.bfloat16).at[target].set(records)
    filtered = jnp.dot(traces, make_filter(fir_taps), preferred_element_type=jnp.float32)
    main_part = filtered[:, :outputs_per].reshape(span_total, CHANNELS, PIECES, outputs_per)
    spill_part = filtered[:, outputs_per:].reshape(span_total, CHANNELS, PIECES, SPILL)
    carried = jnp.pad(spill_part[:, :, :-1, :], ((0, 0), (0, 0), (1, 0), (0, outputs_per - SPILL)))
    decimated = (main_part + carried).reshape(span_total, CHANNELS, SPAN)
    starts = window_starts.reshape(span_total, WIN_DEV)
    taper_window = make_taper()

    def cut_span(trace_span, start_span):

        def window_cut(window_start):
            return lax.dynamic_slice_in_dim(trace_span, window_start, WL, 1)
        return jax.vmap(window_cut, out_axes=1)(start_span)
    segments = (jax.vmap(cut_span)(decimated, starts) * taper_window).astype(jnp.bfloat16)
    spectra = jnp.dot(segments.reshape(-1, WL), make_fourier(), preferred_element_type=jnp.float32)
    whitened = whiten(spectra).reshape(span_total, CHANNELS, WIN_DEV, WL)
    source_channels = jnp.arange(SOURCES, dtype=jnp.int32) * CH_DEV + source_slot
    sources = whitened[:, source_channels]
    lag_table = make_lags()
    block_size = math.gcd(SOURCES, 16)
    block_count = SOURCES // block_size
    grouped = jnp.transpose(sources.reshape(span_total, block_count, block_size, WIN_DEV, WL), (1, 0, 2, 3, 4))

    def one_block(source_block):
        accumulated = jnp.zeros((block_size * CHANNELS, LAGS), jnp.float32)
        for span_number in range(span_total):
            cross_spectra = cross_spectrum(source_block[span_number], whitened[span_number])
            accumulated = accumulated + jnp.dot(cross_spectra.reshape(-1, WL), lag_table, preferred_element_type=jnp.float32)
        return accumulated.reshape(block_size, CHANNELS, LAGS)
    return lax.map(one_block, grouped).reshape(SOURCES, CHANNELS, LAGS)
```

```python
import math

import jax
import jax.numpy as jnp
import ml_dtypes
import numpy as np
from jax import lax
from jax.experimental import pallas as pl
from jax.experimental.pallas import tpu as pltpu
from jax.sharding import PartitionSpec as P

CH_DEV = 16
SPAN = 2048
WIN_DEV = 8
WL = 1024
NF = 512
DEC = 4
TAPS = 32
SPILL = 7
SEG = 512
PIECES = 16
BAND = 64
LAGS = 256


EPSILON = 1e-06

LANES = 128
OUTS = SEG // DEC
AUX = 16
SCALE_ROW = SPILL
KEY_ROW = SPILL + 1
SLOT_ROW = SPILL + 2
FILTER_VMEM = 62 << 20
CORRELATE_VMEM = 53 << 20
LOCAL_ROWS = 16384
LAST_HOP = {1: 1, 2: 2, 4: 4, 6: 6, 3: 3, 5: 1, 7: 1}
ORDER = (3, 6, 1, 4, 2, 7, 5)
CODE = 23000.0


def fourier_table():
    sample_index = np.arange(WL)[:, None]
    freq_index = np.arange(NF)[None, :]
    phase = 2.0 * np.pi * (sample_index * freq_index % WL) / WL
    return np.concatenate([np.cos(phase), -np.sin(phase)], axis=1).astype(ml_dtypes.bfloat16)


def lag_table():
    freq_index = np.arange(NF)[:, None]
    lag_index = np.arange(LAGS)[None, :] - LAGS // 2
    phase = 2.0 * np.pi * (freq_index * lag_index % WL) / WL
    scale = 1.0 / math.sqrt(WL * WIN_DEV)
    return (np.concatenate([np.cos(phase), -np.sin(phase)], axis=0) * scale).astype(
        ml_dtypes.bfloat16
    )


def band_table():
    freq_index = np.arange(NF)
    return (np.abs(freq_index[:, None] - freq_index[None, :]) <= BAND).astype(ml_dtypes.bfloat16)


def split_rows(row):
    rows = []
    for _ in range(3):
        rows.append(row.astype(ml_dtypes.bfloat16))
        row = row - rows[-1].astype(np.float32)
    return rows


def wide_table():
    freq_index = np.arange(NF)
    band = np.abs(freq_index[:, None] - freq_index[None, :]) <= BAND
    taper = (0.5 - 0.5 * np.cos(2.0 * np.pi * np.arange(WL) / WL)).astype(np.float32)
    inverse = np.zeros(WL, np.float32)
    inverse[:NF] = 1.0 / band.sum(axis=0)
    empty = [np.zeros(WL, ml_dtypes.bfloat16)] * 10
    rows = np.stack(split_rows(taper) + split_rows(inverse) + empty)
    return np.concatenate([fourier_table(), rows], axis=0)


def filter_kernel(
    records_hbm, channel_hbm, piece_hbm, taps_hbm, slot_hbm, starts_hbm, unit_hbm, local_hbm, *scratch
):
    records_ref, channel_ref, piece_ref, taps_ref, slot_ref, starts_ref = scratch[:6]
    unit_ref, local_ref, arrived = scratch[6:]
    f32 = jnp.float32
    count = records_ref.shape[0]
    size = unit_ref.shape[0]
    pairs = (
        (taps_hbm, taps_ref),
        (records_hbm, records_ref),
        (channel_hbm, channel_ref),
        (piece_hbm, piece_ref),
        (slot_hbm, slot_ref),
        (starts_hbm, starts_ref),
    )
    copies = [
        pltpu.make_async_copy(source, target, arrived.at[number])
        for number, (source, target) in enumerate(pairs)
    ]
    for copy in copies:
        copy.start()
    tap = lax.broadcasted_iota(jnp.int32, (TAPS, SEG), 0)
    sample = lax.broadcasted_iota(jnp.int32, (TAPS, SEG), 1)
    place = (((DEC - 1 - tap) & (SEG - 1)) == sample).astype(f32).astype(jnp.bfloat16)
    copies[0].wait()
    taps = jnp.broadcast_to(taps_ref[...].reshape(1, TAPS), (16, TAPS))
    first = jnp.dot(taps, place, preferred_element_type=f32)
    circulant = pltpu.roll(
        jnp.broadcast_to(first[0:1], (OUTS, SEG)), 0, 1, stride=DEC, stride_axis=0
    )
    output = lax.broadcasted_iota(jnp.int32, (OUTS, SEG), 0)
    sample = lax.broadcasted_iota(jnp.int32, (OUTS, SEG), 1)
    inside = sample <= DEC * output + DEC - 1
    main_filter = jnp.where(inside, circulant, 0.0)
    spill_filter = jnp.where(inside, 0.0, circulant)[:AUX]
    filters = jnp.concatenate([main_filter, spill_filter], axis=0).astype(jnp.bfloat16)
    copies[1].wait()
    filtered = lax.dot_general(
        filters, records_ref[...], (((1,), (1,)), ((), ())), preferred_element_type=f32
    )
    absolute = jnp.abs(filtered)
    largest = jnp.maximum(jnp.max(absolute, axis=0, keepdims=True), 1e-30)
    power = jnp.minimum(jnp.floor(jnp.log2(largest)) + 1.0, 126.0)
    root = jnp.sqrt(jnp.sqrt(absolute * jnp.exp2(-power)))
    code = jnp.floor(root * CODE + 0.5)
    code = jnp.where(filtered < 0.0, -code, code)
    main = jnp.transpose(code[:OUTS]).astype(jnp.int32)
    local_ref[:count] = main
    unit_ref[:count] = main.astype(jnp.int16)
    for copy in copies[2:]:
        copy.wait()
    row = lax.broadcasted_iota(jnp.int32, (AUX, count), 0)
    key = channel_ref[...].reshape(1, count) * PIECES + piece_ref[...].reshape(1, count)
    side = jnp.where(row < SPILL, code[OUTS:].astype(jnp.int32), 0)
    side = jnp.where(row == SCALE_ROW, power.astype(jnp.int32), side)
    side = jnp.where(row == KEY_ROW, key, side)
    side = jnp.where(row == SLOT_ROW, slot_ref[0], side)
    for block in range(count // LANES):
        to = slice(count + block * AUX, count + (block + 1) * AUX)
        part = side[:, block * LANES : (block + 1) * LANES]
        local_ref[to] = part
        unit_ref[to] = part.astype(jnp.int16)
    lane = lax.broadcasted_iota(jnp.int32, (8, OUTS), 1)
    starts = jnp.zeros((8, OUTS), jnp.int32)
    for window in range(WIN_DEV):
        starts = jnp.where(lane == window, starts_ref[window], starts)
    local_ref[size:] = starts
    here = local_hbm.at[pl.ds(0, size + 8)]
    out = pltpu.make_async_copy(unit_ref, unit_hbm, arrived.at[0])
    local = pltpu.make_async_copy(local_ref, here, arrived.at[1])
    out.start()
    local.start()
    out.wait()
    local.wait()


def halves(code):
    first = (code >> 8).astype(jnp.float32).astype(jnp.bfloat16)
    return first, (code & 255).astype(jnp.float32).astype(jnp.bfloat16)


def decoded(code, scale):
    root = code * (1.0 / CODE)
    return (root * root) * (root * jnp.abs(root)) * scale


def correlate_kernel(block_total, span_total, *refs):
    units_ref = refs[1:block_total]
    local_hbm, wide_hbm, band_hbm, lags_hbm = (refs[0],) + refs[block_total : block_total + 3]
    keep_ref, send_ref = refs[block_total + 3 : block_total + 5]
    pick_ref, dec_ref, seg_ref, white_ref, cross_ref, out_ref = refs[
        block_total + 5 : block_total + 11
    ]
    unit_ref, starts_ref, wide_ref, band_ref, lags_ref, arrived = refs[block_total + 11 :]
    size = unit_ref.shape[0]
    pairs = (
        (local_hbm.at[pl.ds(0, size)], unit_ref),
        (local_hbm.at[pl.ds(size, 8)], starts_ref),
        (wide_hbm, wide_ref),
        (band_hbm, band_ref),
        (lags_hbm, lags_ref),
    )
    copies = [
        pltpu.make_async_copy(source, target, arrived.at[number])
        for number, (source, target) in enumerate(pairs)
    ]
    for copy in copies:
        copy.start()
    f32 = jnp.float32
    me = lax.axis_index("chan")
    half = lax.axis_index("win")
    rows = CH_DEV + block_total
    count = unit_ref.shape[0] * LANES // (LANES + AUX)
    copies[0].wait()
    units = dict(zip(ORDER, units_ref))
    units = [unit_ref] + [units[step] for step in range(1, block_total)]
    side = jnp.concatenate(
        [
            unit[count + block * AUX : count + (block + 1) * AUX].astype(jnp.int32)
            for unit in units
            for block in range(count // LANES)
        ],
        axis=1,
    )
    row = lax.broadcasted_iota(jnp.int32, (2 * rows, LANES), 0)
    odd = (row >= rows).astype(jnp.int32)
    row = row - odd * rows
    source = row - CH_DEV
    channel = me * CH_DEV + row
    for step in range(block_total):
        slot = side[SLOT_ROW : SLOT_ROW + 1, step * count : step * count + LANES]
        slot = jnp.broadcast_to(slot, (2 * rows, LANES))
        channel = jnp.where(source == (me ^ step), source * CH_DEV + slot, channel)
    wanted = channel * PIECES + odd
    total = block_total * count
    wanted = jnp.concatenate([wanted] * (total // LANES), axis=1)
    key = jnp.broadcast_to(side[KEY_ROW : KEY_ROW + 1], (2 * rows, total))
    for pair in range(PIECES // 2):
        pick_ref[pair * 2 * rows : (pair + 1) * 2 * rows] = jnp.where(
            wanted + 2 * pair == key, 1.0, 0.0
        ).astype(jnp.bfloat16)
    codes = jnp.concatenate([unit[:count].astype(jnp.int32) for unit in units], axis=0)
    picked = jnp.dot(
        pick_ref[...], jnp.concatenate(halves(codes), axis=1), preferred_element_type=f32
    )
    beside = lax.dot_general(
        pick_ref[...],
        jnp.concatenate(halves(side), axis=0),
        (((1,), (1,)), ((), ())),
        preferred_element_type=f32,
    )
    beside = beside[:, :AUX] * 256.0 + beside[:, AUX:]
    scale = jnp.exp2(beside[:, SCALE_ROW : SCALE_ROW + 1])
    main_part = decoded(picked[:, :OUTS] * 256.0 + picked[:, OUTS:], scale)
    column = lax.broadcasted_iota(jnp.int32, beside.shape, 1)
    spill_part = jnp.where(column < SPILL, decoded(beside, scale), 0.0)
    for piece in range(PIECES):
        dec_ref[:, piece * OUTS : (piece + 1) * OUTS] = main_part[
            piece * rows : (piece + 1) * rows
        ]
        if piece:
            dec_ref[:, piece * OUTS : piece * OUTS + AUX] += spill_part[
                (piece - 1) * rows : piece * rows
            ]
    dec_ref[:, SPAN:] = jnp.zeros((rows, LANES), f32)
    lane = lax.broadcasted_iota(jnp.int32, (rows, LANES), 1)
    copies[1].wait()
    copies[2].wait()
    extra = wide_ref[WL:].astype(f32)
    taper = extra[0:1] + extra[1:2] + extra[2:3]
    inverse = (extra[3:4] + extra[4:5] + extra[5:6])[:, :NF]

    def cut(window, carry):
        start = starts_ref[0, window]
        base = pl.multiple_of((start >> 7) * LANES, LANES)
        offset = start & (LANES - 1)
        shift = (LANES - offset) & (LANES - 1)
        chunks = [
            pltpu.roll(dec_ref[:, pl.ds(base + tile * LANES, LANES)], shift, 1)
            for tile in range(WL // LANES + 1)
        ]
        here = lane < LANES - offset
        to = pl.ds(pl.multiple_of(window * rows, 8), rows)
        for tile in range(WL // LANES):
            at = slice(tile * LANES, (tile + 1) * LANES)
            seg_ref[to, at] = (
                jnp.where(here, chunks[tile], chunks[tile + 1]) * taper[:, at]
            )
        return carry

    lax.fori_loop(0, WIN_DEV, cut, 0)
    spectra = jnp.dot(
        seg_ref[...].astype(jnp.bfloat16), wide_ref[:WL], preferred_element_type=f32
    )
    real = spectra[:, :NF]
    imag = spectra[:, NF:]
    energy = real * real + imag * imag
    high = energy.astype(jnp.bfloat16)
    rest = energy - high.astype(f32)
    middle = rest.astype(jnp.bfloat16)
    low = (rest - middle.astype(f32)).astype(jnp.bfloat16)
    copies[3].wait()
    band = band_ref[...]
    smooth = (
        jnp.dot(high, band, preferred_element_type=f32)
        + jnp.dot(middle, band, preferred_element_type=f32)
        + jnp.dot(low, band, preferred_element_type=f32)
    ) * inverse
    scale = lax.rsqrt(smooth + EPSILON)
    white_ref[:, :NF] = (real * scale).astype(jnp.bfloat16).astype(f32)
    white_ref[:, NF:] = (imag * scale).astype(jnp.bfloat16).astype(f32)

    def cross(tile, carry):
        re = pl.ds(pl.multiple_of(tile * LANES, LANES), LANES)
        im = pl.ds(pl.multiple_of(NF + tile * LANES, LANES), LANES)
        real_sums = [jnp.zeros((CH_DEV, LANES), f32)] * block_total
        imag_sums = [jnp.zeros((CH_DEV, LANES), f32)] * block_total
        for window in range(WIN_DEV):
            own = slice(window * rows, window * rows + CH_DEV)
            loc_real = white_ref[own, re]
            loc_imag = white_ref[own, im]
            for number in range(block_total):
                at = window * rows + CH_DEV + number
                src_real = jnp.broadcast_to(white_ref[at : at + 1, re], (CH_DEV, LANES))
                src_imag = jnp.broadcast_to(white_ref[at : at + 1, im], (CH_DEV, LANES))
                real_sums[number] += src_real * loc_real + src_imag * loc_imag
                imag_sums[number] += src_imag * loc_real - src_real * loc_imag
        for number in range(block_total):
            to = slice(number * CH_DEV, (number + 1) * CH_DEV)
            cross_ref[to, re] = real_sums[number].astype(jnp.bfloat16)
            cross_ref[to, im] = imag_sums[number].astype(jnp.bfloat16)
        return carry

    lax.fori_loop(0, NF // LANES, cross, 0)
    copies[4].wait()
    out_ref[...] = jnp.dot(cross_ref[...], lags_ref[...], preferred_element_type=f32)
    part = keep_ref.shape[0]
    keep_ref[...] = out_ref[pl.ds(pl.multiple_of(half * part, 8), part)]
    send_ref[...] = out_ref[pl.ds(pl.multiple_of((span_total - 1 - half) * part, 8), part)]


def gathered_body(records, record_channel, record_piece, fir_taps, window_starts, source_slot):
    block_total = lax.axis_size("chan")
    span_total = lax.axis_size("win")
    vmem = pl.BlockSpec(memory_space=pltpu.VMEM)
    hbm = pl.BlockSpec(memory_space=pl.ANY)
    count = records.shape[0]
    size = count + count // LANES * AUX
    unit, local = pl.pallas_call(
        filter_kernel,
        out_shape=(
            jax.ShapeDtypeStruct((size, OUTS), jnp.int16),
            jax.ShapeDtypeStruct((LOCAL_ROWS, OUTS), jnp.int32),
        ),
        in_specs=[hbm] * 6,
        out_specs=(hbm, hbm),
        scratch_shapes=[
            pltpu.VMEM(records.shape, records.dtype),
            pltpu.VMEM(record_channel.shape, jnp.int32),
            pltpu.VMEM(record_piece.shape, jnp.int32),
            pltpu.VMEM(fir_taps.shape, fir_taps.dtype),
            pltpu.SMEM((1,), jnp.int32),
            pltpu.SMEM((WIN_DEV,), jnp.int32),
            pltpu.VMEM((size, OUTS), jnp.int16),
            pltpu.VMEM((size + 8, OUTS), jnp.int32),
            pltpu.SemaphoreType.DMA((6,)),
        ],
        compiler_params=pltpu.CompilerParams(vmem_limit_bytes=FILTER_VMEM),
        name="filter",
    )(records, record_channel, record_piece, fir_taps, source_slot, window_starts)

    def swap(value, step):
        return lax.ppermute(value, "chan", [(i, i ^ step) for i in range(block_total)])

    units = {0: unit}
    for step, last in LAST_HOP.items():
        units[step] = swap(units[step ^ last], last)
    rows = CH_DEV + block_total
    half_rows = block_total // span_total * CH_DEV
    half_shape = jax.ShapeDtypeStruct((half_rows, LAGS), jnp.float32)
    tables = [wide_table(), band_table(), lag_table()]
    keep, send = pl.pallas_call(
        lambda *refs: correlate_kernel(block_total, span_total, *refs),
        out_shape=(half_shape, half_shape),
        in_specs=[hbm] + [vmem] * (block_total - 1) + [hbm] * 3,
        out_specs=(vmem, vmem),
        scratch_shapes=[
            pltpu.VMEM((PIECES * rows, block_total * count), jnp.bfloat16),
            pltpu.VMEM((rows, SPAN + LANES), jnp.float32),
            pltpu.VMEM((WIN_DEV * rows, WL), jnp.float32),
            pltpu.VMEM((WIN_DEV * rows, WL), jnp.float32),
            pltpu.VMEM((block_total * CH_DEV, WL), jnp.bfloat16),
            pltpu.VMEM((block_total * CH_DEV, LAGS), jnp.float32),
            pltpu.VMEM((size, OUTS), jnp.int32),
            pltpu.SMEM((8, OUTS), jnp.int32),
        ]
        + [pltpu.VMEM(table.shape, table.dtype) for table in tables]
        + [pltpu.SemaphoreType.DMA((5,))],
        compiler_params=pltpu.CompilerParams(vmem_limit_bytes=CORRELATE_VMEM),
        name="correlate",
    )(
        local,
        *[units[step] for step in ORDER],
        *[jnp.asarray(table) for table in tables],
    )
    other = lax.ppermute(send, "win", [(i, i ^ 1) for i in range(span_total)])
    return (keep + other).reshape(block_total // span_total, CH_DEV, LAGS)


def make_filter(fir_taps):
    outputs_per = SEG // DEC
    sample_index = jnp.arange(SEG, dtype=jnp.int32)[:, None]
    column_index = jnp.arange(outputs_per + SPILL, dtype=jnp.int32)[None, :]
    tap_index = jnp.where(
        column_index < outputs_per,
        DEC * column_index + DEC - 1 - sample_index,
        DEC * (column_index - outputs_per) + DEC - 1 + SEG - sample_index,
    )
    match_table = (
        tap_index[:, :, None] == jnp.arange(TAPS, dtype=jnp.int32)[None, None, :]
    ).astype(jnp.float32)
    return jnp.sum(match_table * fir_taps.astype(jnp.float32)[None, None, :], axis=2).astype(
        jnp.bfloat16
    )


def make_fourier():
    sample_index = jnp.arange(WL, dtype=jnp.int32)[:, None]
    freq_index = jnp.arange(NF, dtype=jnp.int32)[None, :]
    phase = 2.0 * math.pi * (sample_index * freq_index % WL).astype(jnp.float32) / WL
    return jnp.concatenate([jnp.cos(phase), -jnp.sin(phase)], axis=1).astype(jnp.bfloat16)


def make_taper():
    sample_index = jnp.arange(WL, dtype=jnp.int32).astype(jnp.float32)
    return 0.5 - 0.5 * jnp.cos(2.0 * math.pi * sample_index / WL)


def make_lags():
    freq_index = jnp.arange(NF, dtype=jnp.int32)[:, None]
    lag_index = jnp.arange(LAGS, dtype=jnp.int32)[None, :] - LAGS // 2
    phase = 2.0 * math.pi * (freq_index * lag_index % WL).astype(jnp.float32) / WL
    scale = 1.0 / math.sqrt(WL * WIN_DEV)
    return (jnp.concatenate([jnp.cos(phase), -jnp.sin(phase)], axis=0) * scale).astype(jnp.bfloat16)


def whiten(spectra):
    freq_index = jnp.arange(NF, dtype=jnp.int32)
    band_table = (jnp.abs(freq_index[:, None] - freq_index[None, :]) <= BAND).astype(jnp.float32)
    band_count = jnp.sum(band_table, axis=0)
    real_part = spectra[..., :NF]
    imag_part = spectra[..., NF:]
    energy = real_part * real_part + imag_part * imag_part
    smooth = jnp.dot(energy, band_table, precision=lax.Precision.HIGHEST) / band_count[None, :]
    amplitude = jnp.sqrt(smooth + EPSILON)
    return (spectra / jnp.concatenate([amplitude, amplitude], axis=-1)).astype(jnp.bfloat16)


def cross_spectrum(source_block, local_block):
    src_real = source_block[..., :NF]
    src_imag = source_block[..., NF:]
    loc_real = local_block[..., :NF]
    loc_imag = local_block[..., NF:]
    real_sum = jnp.einsum(
        "bwf,cwf->bcf", src_real, loc_real, preferred_element_type=jnp.float32
    ) + jnp.einsum("bwf,cwf->bcf", src_imag, loc_imag, preferred_element_type=jnp.float32)
    imag_sum = jnp.einsum(
        "bwf,cwf->bcf", src_imag, loc_real, preferred_element_type=jnp.float32
    ) - jnp.einsum("bwf,cwf->bcf", src_real, loc_imag, preferred_element_type=jnp.float32)
    return jnp.concatenate([real_sum, imag_sum], axis=-1).astype(jnp.bfloat16)


def over_blocks(block_fn, sources, channel_count):
    source_count = sources.shape[0]
    block_size = math.gcd(source_count, 16)
    block_count = source_count // block_size
    grouped = sources.reshape((block_count, block_size) + sources.shape[1:])
    return lax.map(block_fn, grouped).reshape(source_count, channel_count, LAGS)


def routed_body(records, record_channel, record_piece, fir_taps, window_starts, source_slot):
    block_total = lax.axis_size("chan")
    per_device = records.shape[0]
    capacity = 2 * per_device // block_total
    outputs_per = SEG // DEC
    owner_block = record_channel // CH_DEV
    local_slot = record_channel % CH_DEV * PIECES + record_piece
    one_hot = (owner_block[:, None] == jnp.arange(block_total, dtype=jnp.int32)[None, :]).astype(
        jnp.int32
    )
    earlier_count = jnp.sum((jnp.cumsum(one_hot, axis=0) - one_hot) * one_hot, axis=1)
    position = owner_block * capacity + earlier_count
    slot_table = (
        jnp.full((block_total * capacity,), -1, jnp.int32)
        .at[position]
        .set(local_slot)
        .reshape(block_total, capacity)
    )
    filter_matrix = make_filter(fir_taps)
    row_send = (
        jnp.zeros((block_total * capacity, SEG), jnp.bfloat16)
        .at[position]
        .set(records)
        .reshape(block_total, capacity, SEG)
    )
    rows_got, slots_got = (
        lax.all_to_all(row_send, "chan", split_axis=0, concat_axis=0, tiled=True),
        lax.all_to_all(slot_table, "chan", split_axis=0, concat_axis=0, tiled=True),
    )
    flat_slots = slots_got.reshape(-1)
    target = jnp.where(flat_slots >= 0, flat_slots, per_device)
    traces = (
        jnp.zeros((per_device, SEG), jnp.bfloat16)
        .at[target]
        .set(rows_got.reshape(-1, SEG), mode="drop")
    )
    filtered = jnp.dot(traces, filter_matrix, preferred_element_type=jnp.float32)
    main_part = filtered[:, :outputs_per]
    spill_part = filtered[:, outputs_per:]
    main_part = main_part.reshape(CH_DEV, PIECES, outputs_per)
    spill_part = spill_part.reshape(CH_DEV, PIECES, SPILL)
    carried = jnp.pad(spill_part[:, :-1, :], ((0, 0), (1, 0), (0, outputs_per - SPILL)))
    decimated = (main_part + carried).reshape(CH_DEV, SPAN)

    def window_cut(window_start):
        return lax.dynamic_slice_in_dim(decimated, window_start, WL, 1)

    segments = (jax.vmap(window_cut, out_axes=1)(window_starts) * make_taper()).astype(jnp.bfloat16)
    window_count = segments.shape[1]
    spectra = jnp.dot(segments.reshape(-1, WL), make_fourier(), preferred_element_type=jnp.float32)
    whitened = whiten(spectra).reshape(CH_DEV, window_count, WL)
    source = lax.dynamic_slice_in_dim(whitened, source_slot[0], 1, 0)
    gathered = lax.all_gather(source, "chan", axis=0, tiled=True)
    lag_table = make_lags()

    def span_block(source_block):
        cross_spectra = cross_spectrum(source_block, whitened)
        return jnp.dot(
            cross_spectra.reshape(-1, WL), lag_table, preferred_element_type=jnp.float32
        ).reshape(source_block.shape[0], CH_DEV, LAGS)

    return lax.psum_scatter(
        over_blocks(span_block, gathered, CH_DEV), "win", scatter_dimension=0, tiled=True
    )


def solution(mesh):
    in_specs = (
        P(("groups", "chan", "win"), None),
        P(("groups", "chan", "win")),
        P(("groups", "chan", "win")),
        P(),
        P(("groups", "win")),
        P(("groups", "chan")),
    )
    out_specs = P(("groups", "win"), "chan", None)
    body = gathered_body if mesh.shape["chan"] == 8 else routed_body
    return jax.shard_map(body, mesh=mesh, in_specs=in_specs, out_specs=out_specs, check_vma=False)
```

```python
import math

import jax
import jax.numpy as jnp
import ml_dtypes
import numpy as np
from jax import lax
from jax.experimental import pallas as pl
from jax.experimental.pallas import tpu as pltpu
from jax.sharding import PartitionSpec as P

CH_DEV = 16
SPAN = 2048
WIN_DEV = 8
WL = 1024
NF = 512
DEC = 4
TAPS = 32
SPILL = 7
SEG = 512
PIECES = 16
BAND = 64
LAGS = 256


EPSILON = 1e-06

LANES = 128
OUTS = SEG // DEC
AUX = 16
SCALE_ROW = SPILL
KEY_ROW = SPILL + 1
SLOT_ROW = SPILL + 2
FILTER_VMEM = 56 << 20
FLOPS = 10**10
CORRELATE_VMEM = 50 << 20
LOCAL_ROWS = 16384
LAST_HOP = {1: 1, 2: 2, 4: 4, 6: 6, 3: 3, 5: 1, 7: 1}
ORDER = (3, 6, 1, 4, 2, 7, 5)
CODE = 23000.0


def fourier_table():
    sample_index = np.arange(WL)[:, None]
    freq_index = np.arange(NF)[None, :]
    phase = 2.0 * np.pi * (sample_index * freq_index % WL) / WL
    return np.concatenate([np.cos(phase), -np.sin(phase)], axis=1).astype(ml_dtypes.bfloat16)


def lag_table():
    freq_index = np.arange(NF)[:, None]
    lag_index = np.arange(LAGS)[None, :] - LAGS // 2
    phase = 2.0 * np.pi * (freq_index * lag_index % WL) / WL
    scale = 1.0 / math.sqrt(WL * WIN_DEV)
    tiles = (NF // LANES, 1, LANES, LAGS)
    parts = [np.cos(phase).reshape(tiles), -np.sin(phase).reshape(tiles)]
    return (np.concatenate(parts, axis=1).reshape(2 * NF, LAGS) * scale).astype(ml_dtypes.bfloat16)


def band_table():
    freq_index = np.arange(NF)
    return (np.abs(freq_index[:, None] - freq_index[None, :]) <= BAND).astype(ml_dtypes.bfloat16)


def split_rows(row):
    rows = []
    for _ in range(3):
        rows.append(row.astype(ml_dtypes.bfloat16))
        row = row - rows[-1].astype(np.float32)
    return rows


def wide_table():
    freq_index = np.arange(NF)
    band = np.abs(freq_index[:, None] - freq_index[None, :]) <= BAND
    taper = (0.5 - 0.5 * np.cos(2.0 * np.pi * np.arange(WL) / WL)).astype(np.float32)
    inverse = np.zeros(WL, np.float32)
    inverse[:NF] = 1.0 / band.sum(axis=0)
    empty = [np.zeros(WL, ml_dtypes.bfloat16)] * 10
    rows = np.stack(split_rows(taper) + split_rows(inverse) + empty)
    return np.concatenate([fourier_table(), rows], axis=0)


def filter_kernel(
    records_hbm, channel_hbm, piece_hbm, taps_hbm, slot_hbm, starts_hbm, unit_hbm, local_hbm, *scratch
):
    records_ref, channel_ref, piece_ref, taps_ref, slot_ref, starts_ref = scratch[:6]
    unit_ref, local_ref, arrived = scratch[6:]
    f32 = jnp.float32
    count = records_ref.shape[0]
    size = unit_ref.shape[0]
    pairs = (
        (taps_hbm, taps_ref),
        (records_hbm, records_ref),
        (channel_hbm, channel_ref),
        (piece_hbm, piece_ref),
        (slot_hbm, slot_ref),
        (starts_hbm, starts_ref),
    )
    copies = [
        pltpu.make_async_copy(source, target, arrived.at[number])
        for number, (source, target) in enumerate(pairs)
    ]
    for copy in copies:
        copy.start()
    tap = lax.broadcasted_iota(jnp.int32, (TAPS, SEG), 0)
    sample = lax.broadcasted_iota(jnp.int32, (TAPS, SEG), 1)
    place = (((DEC - 1 - tap) & (SEG - 1)) == sample).astype(f32).astype(jnp.bfloat16)
    copies[0].wait()
    taps = jnp.broadcast_to(taps_ref[...].reshape(1, TAPS), (16, TAPS))
    first = jnp.dot(taps, place, preferred_element_type=f32)
    circulant = pltpu.roll(
        jnp.broadcast_to(first[0:1], (OUTS, SEG)), 0, 1, stride=DEC, stride_axis=0
    )
    output = lax.broadcasted_iota(jnp.int32, (OUTS, SEG), 0)
    sample = lax.broadcasted_iota(jnp.int32, (OUTS, SEG), 1)
    inside = sample <= DEC * output + DEC - 1
    main_filter = jnp.where(inside, circulant, 0.0)
    spill_filter = jnp.where(inside, 0.0, circulant)[:AUX]
    filters = jnp.concatenate([main_filter, spill_filter], axis=0).astype(jnp.bfloat16)
    copies[1].wait()
    filtered = lax.dot_general(
        filters, records_ref[...], (((1,), (1,)), ((), ())), preferred_element_type=f32
    )
    absolute = jnp.abs(filtered)
    largest = jnp.maximum(jnp.max(absolute, axis=0, keepdims=True), 1e-30)
    power = jnp.minimum(jnp.floor(jnp.log2(largest)) + 1.0, 126.0)
    root = jnp.sqrt(jnp.sqrt(absolute * jnp.exp2(-power)))
    code = jnp.floor(root * CODE + 0.5)
    code = jnp.where(filtered < 0.0, -code, code)
    main = jnp.transpose(code[:OUTS]).astype(jnp.int32)
    local_ref[:count] = main
    unit_ref[:count] = main.astype(jnp.int16)
    for copy in copies[2:]:
        copy.wait()
    row = lax.broadcasted_iota(jnp.int32, (AUX, count), 0)
    key = channel_ref[...].reshape(1, count) * PIECES + piece_ref[...].reshape(1, count)
    side = jnp.where(row < SPILL, code[OUTS:].astype(jnp.int32), 0)
    side = jnp.where(row == SCALE_ROW, power.astype(jnp.int32), side)
    side = jnp.where(row == KEY_ROW, key, side)
    side = jnp.where(row == SLOT_ROW, slot_ref[0], side)
    for block in range(count // LANES):
        to = slice(count + block * AUX, count + (block + 1) * AUX)
        part = side[:, block * LANES : (block + 1) * LANES]
        local_ref[to] = part
        unit_ref[to] = part.astype(jnp.int16)
    lane = lax.broadcasted_iota(jnp.int32, (8, OUTS), 1)
    starts = jnp.zeros((8, OUTS), jnp.int32)
    for window in range(WIN_DEV):
        starts = jnp.where(lane == window, starts_ref[window], starts)
    local_ref[size:] = starts
    here = local_hbm.at[pl.ds(0, size + 8)]
    out = pltpu.make_async_copy(unit_ref, unit_hbm, arrived.at[0])
    local = pltpu.make_async_copy(local_ref, here, arrived.at[1])
    out.start()
    local.start()
    out.wait()
    local.wait()


def halves(code):
    first = (code >> 8).astype(jnp.float32).astype(jnp.bfloat16)
    return first, (code & 255).astype(jnp.float32).astype(jnp.bfloat16)


def decoded(code, scale):
    root = code * (1.0 / CODE)
    return (root * root) * (root * jnp.abs(root)) * scale


def correlate_kernel(block_total, span_total, *refs):
    local_hbm, slot_ref = refs[:2]
    units_ref = dict(zip(ORDER, refs[2 : block_total + 1]))
    wide_ref, band_ref, lags_ref, keep_ref, send_ref = refs[block_total + 1 : block_total + 6]
    pick_ref, dec_ref, seg_ref, white_ref, out_ref, unit_ref, starts_ref, arrived = refs[
        block_total + 6 :
    ]
    f32 = jnp.float32
    size = unit_ref.shape[0]
    pairs = (
        (local_hbm.at[pl.ds(0, size)], unit_ref),
        (local_hbm.at[pl.ds(size, 8)], starts_ref),
    )
    copies = [
        pltpu.make_async_copy(source, target, arrived.at[number])
        for number, (source, target) in enumerate(pairs)
    ]
    for copy in copies:
        copy.start()
    me = lax.axis_index("chan")
    half = lax.axis_index("win")
    rows = CH_DEV + block_total
    count = size * LANES // (LANES + AUX)

    def side_of(unit):
        blocks = range(count // LANES)
        parts = [unit[count + block * AUX : count + (block + 1) * AUX] for block in blocks]
        return jnp.concatenate([part.astype(jnp.int32) for part in parts], axis=1)

    sides = {step: side_of(unit) for step, unit in units_ref.items()}
    row = lax.broadcasted_iota(jnp.int32, (2 * rows, count), 0)
    odd = (row >= rows).astype(jnp.int32)
    row = row - odd * rows
    source = row - CH_DEV
    channel = me * CH_DEV + row
    channel = jnp.where(source == me, source * CH_DEV + slot_ref[0], channel)
    for step, side in sides.items():
        slot = jnp.broadcast_to(side[SLOT_ROW : SLOT_ROW + 1], (2 * rows, count))
        channel = jnp.where(source == (me ^ step), source * CH_DEV + slot, channel)
    wanted = channel * PIECES + odd

    def pick(step, side):
        key = jnp.broadcast_to(side[KEY_ROW : KEY_ROW + 1], (2 * rows, count))
        for pair in range(PIECES // 2):
            pick_ref[
                pair * 2 * rows : (pair + 1) * 2 * rows, step * count : (step + 1) * count
            ] = jnp.where(wanted + 2 * pair == key, 1.0, 0.0).astype(jnp.bfloat16)

    for step in range(1, block_total):
        pick(step, sides[step])
    copies[0].wait()
    sides[0] = side_of(unit_ref)
    pick(0, sides[0])
    units = [unit_ref] + [units_ref[step] for step in range(1, block_total)]
    codes = jnp.concatenate([unit[:count].astype(jnp.int32) for unit in units], axis=0)
    picked = jnp.dot(
        pick_ref[...], jnp.concatenate(halves(codes), axis=1), preferred_element_type=f32
    )
    side = jnp.concatenate([sides[step] for step in range(block_total)], axis=1)
    beside = lax.dot_general(
        pick_ref[...],
        jnp.concatenate(halves(side), axis=0),
        (((1,), (1,)), ((), ())),
        preferred_element_type=f32,
    )
    beside = beside[:, :AUX] * 256.0 + beside[:, AUX:]
    scale = jnp.exp2(beside[:, SCALE_ROW : SCALE_ROW + 1])
    main_part = decoded(picked[:, :OUTS] * 256.0 + picked[:, OUTS:], scale)
    column = lax.broadcasted_iota(jnp.int32, beside.shape, 1)
    spill_part = jnp.where(column < SPILL, decoded(beside, scale), 0.0)
    for piece in range(PIECES):
        dec_ref[:, piece * OUTS : (piece + 1) * OUTS] = main_part[
            piece * rows : (piece + 1) * rows
        ]
        if piece:
            dec_ref[:, piece * OUTS : piece * OUTS + AUX] += spill_part[
                (piece - 1) * rows : piece * rows
            ]
    dec_ref[:, SPAN:] = jnp.zeros((rows, LANES), f32)
    lane = lax.broadcasted_iota(jnp.int32, (rows, LANES), 1)
    extra = wide_ref[WL:].astype(f32)
    taper = extra[0:1] + extra[1:2] + extra[2:3]
    inverse = (extra[3:4] + extra[4:5] + extra[5:6])[:, :NF]
    copies[1].wait()
    for window in range(WIN_DEV):
        start = starts_ref[0, window]
        base = pl.multiple_of((start >> 7) * LANES, LANES)
        offset = start & (LANES - 1)
        shift = (LANES - offset) & (LANES - 1)
        chunks = [
            pltpu.roll(dec_ref[:, pl.ds(base + tile * LANES, LANES)], shift, 1)
            for tile in range(WL // LANES + 1)
        ]
        here = lane < LANES - offset
        for tile in range(WL // LANES):
            at = slice(tile * LANES, (tile + 1) * LANES)
            seg_ref[window * rows : (window + 1) * rows, at] = (
                jnp.where(here, chunks[tile], chunks[tile + 1]) * taper[:, at]
            )
    spectra = jnp.dot(
        seg_ref[...].astype(jnp.bfloat16), wide_ref[:WL], preferred_element_type=f32
    )
    real = spectra[:, :NF]
    imag = spectra[:, NF:]
    energy = real * real + imag * imag
    high = energy.astype(jnp.bfloat16)
    rest = energy - high.astype(f32)
    middle = rest.astype(jnp.bfloat16)
    low = (rest - middle.astype(f32)).astype(jnp.bfloat16)
    band = band_ref[...]
    smooth = (
        jnp.dot(high, band, preferred_element_type=f32)
        + jnp.dot(middle, band, preferred_element_type=f32)
        + jnp.dot(low, band, preferred_element_type=f32)
    ) * inverse
    scale = lax.rsqrt(smooth + EPSILON)
    white_ref[:, :NF] = (real * scale).astype(jnp.bfloat16).astype(f32)
    white_ref[:, NF:] = (imag * scale).astype(jnp.bfloat16).astype(f32)
    total = jnp.zeros((block_total * CH_DEV, LAGS), f32)
    for tile in range(NF // LANES):
        re = slice(tile * LANES, (tile + 1) * LANES)
        im = slice(NF + tile * LANES, NF + (tile + 1) * LANES)
        real_sums = [jnp.zeros((CH_DEV, LANES), f32)] * block_total
        imag_sums = [jnp.zeros((CH_DEV, LANES), f32)] * block_total
        for window in range(WIN_DEV):
            own = slice(window * rows, window * rows + CH_DEV)
            loc_real = white_ref[own, re]
            loc_imag = white_ref[own, im]
            for number in range(block_total):
                at = window * rows + CH_DEV + number
                src_real = jnp.broadcast_to(white_ref[at : at + 1, re], (CH_DEV, LANES))
                src_imag = jnp.broadcast_to(white_ref[at : at + 1, im], (CH_DEV, LANES))
                real_sums[number] += src_real * loc_real + src_imag * loc_imag
                imag_sums[number] += src_imag * loc_real - src_real * loc_imag
        cross = jnp.concatenate(
            [
                jnp.concatenate(real_sums, axis=0).astype(jnp.bfloat16),
                jnp.concatenate(imag_sums, axis=0).astype(jnp.bfloat16),
            ],
            axis=1,
        )
        total += jnp.dot(
            cross,
            lags_ref[2 * tile * LANES : 2 * (tile + 1) * LANES],
            preferred_element_type=f32,
        )
    out_ref[...] = total
    part = keep_ref.shape[0]
    keep_ref[...] = out_ref[pl.ds(pl.multiple_of(half * part, 8), part)]
    send_ref[...] = out_ref[pl.ds(pl.multiple_of((span_total - 1 - half) * part, 8), part)]


def gathered_body(records, record_channel, record_piece, fir_taps, window_starts, source_slot):
    block_total = lax.axis_size("chan")
    span_total = lax.axis_size("win")
    vmem = pl.BlockSpec(memory_space=pltpu.VMEM)
    smem = pl.BlockSpec(memory_space=pltpu.SMEM)
    hbm = pl.BlockSpec(memory_space=pl.ANY)
    count = records.shape[0]
    size = count + count // LANES * AUX
    unit, local = pl.pallas_call(
        filter_kernel,
        out_shape=(
            jax.ShapeDtypeStruct((size, OUTS), jnp.int16),
            jax.ShapeDtypeStruct((LOCAL_ROWS, OUTS), jnp.int32),
        ),
        in_specs=[hbm] * 6,
        out_specs=(hbm, hbm),
        scratch_shapes=[
            pltpu.VMEM(records.shape, records.dtype),
            pltpu.VMEM(record_channel.shape, jnp.int32),
            pltpu.VMEM(record_piece.shape, jnp.int32),
            pltpu.VMEM(fir_taps.shape, fir_taps.dtype),
            pltpu.SMEM((1,), jnp.int32),
            pltpu.SMEM((WIN_DEV,), jnp.int32),
            pltpu.VMEM((size, OUTS), jnp.int16),
            pltpu.VMEM((size + 8, OUTS), jnp.int32),
            pltpu.SemaphoreType.DMA((6,)),
        ],
        compiler_params=pltpu.CompilerParams(vmem_limit_bytes=FILTER_VMEM),
        cost_estimate=pl.CostEstimate(flops=FLOPS, bytes_accessed=1 << 20, transcendentals=0),
        name="filter",
    )(records, record_channel, record_piece, fir_taps, source_slot, window_starts)

    def swap(value, step):
        return lax.ppermute(value, "chan", [(i, i ^ step) for i in range(block_total)])

    units = {0: unit}
    for step, last in LAST_HOP.items():
        units[step] = swap(units[step ^ last], last)
    rows = CH_DEV + block_total
    half_rows = block_total // span_total * CH_DEV
    half_shape = jax.ShapeDtypeStruct((half_rows, LAGS), jnp.float32)
    tables = [wide_table(), band_table(), lag_table()]
    keep, send = pl.pallas_call(
        lambda *refs: correlate_kernel(block_total, span_total, *refs),
        out_shape=(half_shape, half_shape),
        in_specs=[hbm, smem] + [vmem] * (block_total + 2),
        out_specs=(vmem, vmem),
        scratch_shapes=[
            pltpu.VMEM((PIECES * rows, block_total * count), jnp.bfloat16),
            pltpu.VMEM((rows, SPAN + LANES), jnp.float32),
            pltpu.VMEM((WIN_DEV * rows, WL), jnp.float32),
            pltpu.VMEM((WIN_DEV * rows, WL), jnp.float32),
            pltpu.VMEM((block_total * CH_DEV, LAGS), jnp.float32),
            pltpu.VMEM((size, OUTS), jnp.int32),
            pltpu.SMEM((8, OUTS), jnp.int32),
            pltpu.SemaphoreType.DMA((2,)),
        ],
        compiler_params=pltpu.CompilerParams(vmem_limit_bytes=CORRELATE_VMEM),
        name="correlate",
    )(
        local,
        source_slot,
        *[units[step] for step in ORDER],
        *[jnp.asarray(table) for table in tables],
    )
    other = lax.ppermute(send, "win", [(i, i ^ 1) for i in range(span_total)])
    return (keep + other).reshape(block_total // span_total, CH_DEV, LAGS)


def make_filter(fir_taps):
    outputs_per = SEG // DEC
    sample_index = jnp.arange(SEG, dtype=jnp.int32)[:, None]
    column_index = jnp.arange(outputs_per + SPILL, dtype=jnp.int32)[None, :]
    tap_index = jnp.where(
        column_index < outputs_per,
        DEC * column_index + DEC - 1 - sample_index,
        DEC * (column_index - outputs_per) + DEC - 1 + SEG - sample_index,
    )
    match_table = (
        tap_index[:, :, None] == jnp.arange(TAPS, dtype=jnp.int32)[None, None, :]
    ).astype(jnp.float32)
    return jnp.sum(match_table * fir_taps.astype(jnp.float32)[None, None, :], axis=2).astype(
        jnp.bfloat16
    )


def make_fourier():
    sample_index = jnp.arange(WL, dtype=jnp.int32)[:, None]
    freq_index = jnp.arange(NF, dtype=jnp.int32)[None, :]
    phase = 2.0 * math.pi * (sample_index * freq_index % WL).astype(jnp.float32) / WL
    return jnp.concatenate([jnp.cos(phase), -jnp.sin(phase)], axis=1).astype(jnp.bfloat16)


def make_taper():
    sample_index = jnp.arange(WL, dtype=jnp.int32).astype(jnp.float32)
    return 0.5 - 0.5 * jnp.cos(2.0 * math.pi * sample_index / WL)


def make_lags():
    freq_index = jnp.arange(NF, dtype=jnp.int32)[:, None]
    lag_index = jnp.arange(LAGS, dtype=jnp.int32)[None, :] - LAGS // 2
    phase = 2.0 * math.pi * (freq_index * lag_index % WL).astype(jnp.float32) / WL
    scale = 1.0 / math.sqrt(WL * WIN_DEV)
    return (jnp.concatenate([jnp.cos(phase), -jnp.sin(phase)], axis=0) * scale).astype(jnp.bfloat16)


def whiten(spectra):
    freq_index = jnp.arange(NF, dtype=jnp.int32)
    band_table = (jnp.abs(freq_index[:, None] - freq_index[None, :]) <= BAND).astype(jnp.float32)
    band_count = jnp.sum(band_table, axis=0)
    real_part = spectra[..., :NF]
    imag_part = spectra[..., NF:]
    energy = real_part * real_part + imag_part * imag_part
    smooth = jnp.dot(energy, band_table, precision=lax.Precision.HIGHEST) / band_count[None, :]
    amplitude = jnp.sqrt(smooth + EPSILON)
    return (spectra / jnp.concatenate([amplitude, amplitude], axis=-1)).astype(jnp.bfloat16)


def cross_spectrum(source_block, local_block):
    src_real = source_block[..., :NF]
    src_imag = source_block[..., NF:]
    loc_real = local_block[..., :NF]
    loc_imag = local_block[..., NF:]
    real_sum = jnp.einsum(
        "bwf,cwf->bcf", src_real, loc_real, preferred_element_type=jnp.float32
    ) + jnp.einsum("bwf,cwf->bcf", src_imag, loc_imag, preferred_element_type=jnp.float32)
    imag_sum = jnp.einsum(
        "bwf,cwf->bcf", src_imag, loc_real, preferred_element_type=jnp.float32
    ) - jnp.einsum("bwf,cwf->bcf", src_real, loc_imag, preferred_element_type=jnp.float32)
    return jnp.concatenate([real_sum, imag_sum], axis=-1).astype(jnp.bfloat16)


def over_blocks(block_fn, sources, channel_count):
    source_count = sources.shape[0]
    block_size = math.gcd(source_count, 16)
    block_count = source_count // block_size
    grouped = sources.reshape((block_count, block_size) + sources.shape[1:])
    return lax.map(block_fn, grouped).reshape(source_count, channel_count, LAGS)


def routed_body(records, record_channel, record_piece, fir_taps, window_starts, source_slot):
    block_total = lax.axis_size("chan")
    per_device = records.shape[0]
    capacity = 2 * per_device // block_total
    outputs_per = SEG // DEC
    owner_block = record_channel // CH_DEV
    local_slot = record_channel % CH_DEV * PIECES + record_piece
    one_hot = (owner_block[:, None] == jnp.arange(block_total, dtype=jnp.int32)[None, :]).astype(
        jnp.int32
    )
    earlier_count = jnp.sum((jnp.cumsum(one_hot, axis=0) - one_hot) * one_hot, axis=1)
    position = owner_block * capacity + earlier_count
    slot_table = (
        jnp.full((block_total * capacity,), -1, jnp.int32)
        .at[position]
        .set(local_slot)
        .reshape(block_total, capacity)
    )
    filter_matrix = make_filter(fir_taps)
    row_send = (
        jnp.zeros((block_total * capacity, SEG), jnp.bfloat16)
        .at[position]
        .set(records)
        .reshape(block_total, capacity, SEG)
    )
    rows_got, slots_got = (
        lax.all_to_all(row_send, "chan", split_axis=0, concat_axis=0, tiled=True),
        lax.all_to_all(slot_table, "chan", split_axis=0, concat_axis=0, tiled=True),
    )
    flat_slots = slots_got.reshape(-1)
    target = jnp.where(flat_slots >= 0, flat_slots, per_device)
    traces = (
        jnp.zeros((per_device, SEG), jnp.bfloat16)
        .at[target]
        .set(rows_got.reshape(-1, SEG), mode="drop")
    )
    filtered = jnp.dot(traces, filter_matrix, preferred_element_type=jnp.float32)
    main_part = filtered[:, :outputs_per]
    spill_part = filtered[:, outputs_per:]
    main_part = main_part.reshape(CH_DEV, PIECES, outputs_per)
    spill_part = spill_part.reshape(CH_DEV, PIECES, SPILL)
    carried = jnp.pad(spill_part[:, :-1, :], ((0, 0), (1, 0), (0, outputs_per - SPILL)))
    decimated = (main_part + carried).reshape(CH_DEV, SPAN)

    def window_cut(window_start):
        return lax.dynamic_slice_in_dim(decimated, window_start, WL, 1)

    segments = (jax.vmap(window_cut, out_axes=1)(window_starts) * make_taper()).astype(jnp.bfloat16)
    window_count = segments.shape[1]
    spectra = jnp.dot(segments.reshape(-1, WL), make_fourier(), preferred_element_type=jnp.float32)
    whitened = whiten(spectra).reshape(CH_DEV, window_count, WL)
    source = lax.dynamic_slice_in_dim(whitened, source_slot[0], 1, 0)
    gathered = lax.all_gather(source, "chan", axis=0, tiled=True)
    lag_table = make_lags()

    def span_block(source_block):
        cross_spectra = cross_spectrum(source_block, whitened)
        return jnp.dot(
            cross_spectra.reshape(-1, WL), lag_table, preferred_element_type=jnp.float32
        ).reshape(source_block.shape[0], CH_DEV, LAGS)

    return lax.psum_scatter(
        over_blocks(span_block, gathered, CH_DEV), "win", scatter_dimension=0, tiled=True
    )


def solution(mesh):
    in_specs = (
        P(("groups", "chan", "win"), None),
        P(("groups", "chan", "win")),
        P(("groups", "chan", "win")),
        P(),
        P(("groups", "win")),
        P(("groups", "chan")),
    )
    out_specs = P(("groups", "win"), "chan", None)
    body = gathered_body if mesh.shape["chan"] == 8 else routed_body
    return jax.shard_map(body, mesh=mesh, in_specs=in_specs, out_specs=out_specs, check_vma=False)
```

```python
import math

import jax
import jax.numpy as jnp
import ml_dtypes
import numpy as np
from jax import lax
from jax.experimental import pallas as pl
from jax.experimental.pallas import tpu as pltpu
from jax.sharding import PartitionSpec as P

CH_DEV = 16
SPAN = 2048
WIN_DEV = 8
WL = 1024
NF = 512
DEC = 4
TAPS = 32
SPILL = 7
SEG = 512
PIECES = 16
BAND = 64
LAGS = 256


EPSILON = 1e-06

LANES = 128
OUTS = SEG // DEC
AUX = 16
SCALE_ROW = SPILL
KEY_ROW = SPILL + 1
SLOT_ROW = SPILL + 2
FILTER_VMEM = 56 << 20
FLOPS = 10**10
CORRELATE_VMEM = 50 << 20
LOCAL_ROWS = 16384
LAST_HOP = {1: 1, 2: 2, 4: 4, 6: 6, 3: 3, 5: 1, 7: 1}
ORDER = (3, 6, 1, 4, 2, 7, 5)
CODE = 23000.0


def fourier_table():
    sample_index = np.arange(WL)[:, None]
    freq_index = np.arange(NF)[None, :]
    phase = 2.0 * np.pi * (sample_index * freq_index % WL) / WL
    return np.concatenate([np.cos(phase), -np.sin(phase)], axis=1).astype(ml_dtypes.bfloat16)


def lag_table():
    freq_index = np.arange(NF)[:, None]
    lag_index = np.arange(LAGS)[None, :] - LAGS // 2
    phase = 2.0 * np.pi * (freq_index * lag_index % WL) / WL
    scale = 1.0 / math.sqrt(WL * WIN_DEV)
    tiles = (NF // LANES, 1, LANES, LAGS)
    parts = [np.cos(phase).reshape(tiles), -np.sin(phase).reshape(tiles)]
    return (np.concatenate(parts, axis=1).reshape(2 * NF, LAGS) * scale).astype(ml_dtypes.bfloat16)


def band_table():
    freq_index = np.arange(NF)
    return (np.abs(freq_index[:, None] - freq_index[None, :]) <= BAND).astype(ml_dtypes.bfloat16)


def split_rows(row):
    rows = []
    for _ in range(3):
        rows.append(row.astype(ml_dtypes.bfloat16))
        row = row - rows[-1].astype(np.float32)
    return rows


def wide_table():
    freq_index = np.arange(NF)
    band = np.abs(freq_index[:, None] - freq_index[None, :]) <= BAND
    taper = (0.5 - 0.5 * np.cos(2.0 * np.pi * np.arange(WL) / WL)).astype(np.float32)
    inverse = np.zeros(WL, np.float32)
    inverse[:NF] = 1.0 / band.sum(axis=0)
    empty = [np.zeros(WL, ml_dtypes.bfloat16)] * 10
    rows = np.stack(split_rows(taper) + split_rows(inverse) + empty)
    return np.concatenate([fourier_table(), rows], axis=0)


def filter_kernel(
    records_hbm, channel_hbm, piece_hbm, taps_hbm, slot_hbm, unit_hbm, local_hbm, *scratch
):
    records_ref, channel_ref, piece_ref, taps_ref, slot_ref, unit_ref, arrived = scratch
    f32 = jnp.float32
    count = records_ref.shape[0]
    pairs = (
        (taps_hbm, taps_ref),
        (records_hbm, records_ref),
        (channel_hbm, channel_ref),
        (piece_hbm, piece_ref),
        (slot_hbm, slot_ref),
    )
    copies = [
        pltpu.make_async_copy(source, target, arrived.at[number])
        for number, (source, target) in enumerate(pairs)
    ]
    for copy in copies:
        copy.start()
    tap = lax.broadcasted_iota(jnp.int32, (TAPS, SEG), 0)
    sample = lax.broadcasted_iota(jnp.int32, (TAPS, SEG), 1)
    place = (((DEC - 1 - tap) & (SEG - 1)) == sample).astype(f32).astype(jnp.bfloat16)
    copies[0].wait()
    taps = jnp.broadcast_to(taps_ref[...].reshape(1, TAPS), (16, TAPS))
    first = jnp.dot(taps, place, preferred_element_type=f32)
    circulant = pltpu.roll(
        jnp.broadcast_to(first[0:1], (OUTS, SEG)), 0, 1, stride=DEC, stride_axis=0
    )
    output = lax.broadcasted_iota(jnp.int32, (OUTS, SEG), 0)
    sample = lax.broadcasted_iota(jnp.int32, (OUTS, SEG), 1)
    inside = sample <= DEC * output + DEC - 1
    main_filter = jnp.where(inside, circulant, 0.0)
    spill_filter = jnp.where(inside, 0.0, circulant)[:AUX]
    filters = jnp.concatenate([main_filter, spill_filter], axis=0).astype(jnp.bfloat16)
    copies[1].wait()
    filtered = lax.dot_general(
        filters, records_ref[...], (((1,), (1,)), ((), ())), preferred_element_type=f32
    )
    absolute = jnp.abs(filtered)
    largest = jnp.maximum(jnp.max(absolute, axis=0, keepdims=True), 1e-30)
    power = jnp.minimum(jnp.floor(jnp.log2(largest)) + 1.0, 126.0)
    root = jnp.sqrt(jnp.sqrt(absolute * jnp.exp2(-power)))
    code = jnp.floor(root * CODE + 0.5)
    code = jnp.where(filtered < 0.0, -code, code)
    unit_ref[:OUTS] = code[:OUTS].astype(jnp.int32).astype(jnp.int16)
    for copy in copies[2:]:
        copy.wait()
    row = lax.broadcasted_iota(jnp.int32, (AUX, count), 0)
    key = channel_ref[...].reshape(1, count) * PIECES + piece_ref[...].reshape(1, count)
    side = jnp.where(row < SPILL, code[OUTS:].astype(jnp.int32), 0)
    side = jnp.where(row == SCALE_ROW, power.astype(jnp.int32), side)
    side = jnp.where(row == KEY_ROW, key, side)
    side = jnp.where(row == SLOT_ROW, slot_ref[0], side)
    unit_ref[OUTS:] = side.astype(jnp.int16)
    out = pltpu.make_async_copy(unit_ref, unit_hbm, arrived.at[0])
    local = pltpu.make_async_copy(unit_ref, local_hbm.at[pl.ds(0, OUTS + AUX)], arrived.at[1])
    out.start()
    local.start()
    out.wait()
    local.wait()


def halves(code):
    first = (code >> 8).astype(jnp.float32).astype(jnp.bfloat16)
    return first, (code & 255).astype(jnp.float32).astype(jnp.bfloat16)


def decoded(code, scale):
    root = code * (1.0 / CODE)
    return (root * root) * (root * jnp.abs(root)) * scale


def correlate_kernel(block_total, span_total, *refs):
    local_hbm, starts_hbm, slot_ref = refs[:3]
    refs = refs[1:]
    units_ref = dict(zip(ORDER, refs[2 : block_total + 1]))
    wide_ref, band_ref, lags_ref, keep_ref, send_ref = refs[block_total + 1 : block_total + 6]
    pick_ref, pick_sum_ref, dec_ref, seg_ref, white_ref, out_ref, unit_ref, starts_ref, arrived = refs[
        block_total + 6 :
    ]
    f32 = jnp.float32
    pairs = (
        (local_hbm.at[pl.ds(0, OUTS + AUX)], unit_ref),
        (starts_hbm, starts_ref),
    )
    copies = [
        pltpu.make_async_copy(source, target, arrived.at[number])
        for number, (source, target) in enumerate(pairs)
    ]
    for copy in copies:
        copy.start()
    me = lax.axis_index("chan")
    half = lax.axis_index("win")
    rows = CH_DEV + block_total
    count = unit_ref.shape[1]

    def side_of(unit):
        return unit[OUTS:].astype(jnp.int32)

    sides = {step: side_of(unit) for step, unit in units_ref.items()}
    row = lax.broadcasted_iota(jnp.int32, (2 * rows, count), 0)
    odd = (row >= rows).astype(jnp.int32)
    row = row - odd * rows
    source = row - CH_DEV
    channel = me * CH_DEV + row
    channel = jnp.where(source == me, source * CH_DEV + slot_ref[0], channel)
    for step, side in sides.items():
        slot = jnp.broadcast_to(side[SLOT_ROW : SLOT_ROW + 1], (2 * rows, count))
        channel = jnp.where(source == (me ^ step), source * CH_DEV + slot, channel)
    wanted = channel * PIECES + odd

    def pick(step, side):
        key = jnp.broadcast_to(side[KEY_ROW : KEY_ROW + 1], (2 * rows, count))
        for pair in range(PIECES // 2):
            pick_ref[
                pair * 2 * rows : (pair + 1) * 2 * rows, step * count : (step + 1) * count
            ] = jnp.where(wanted + 2 * pair == key, 1.0, 0.0).astype(jnp.bfloat16)

    def select(steps, units):
        for step in steps:
            pick(step, sides[step])
        codes = jnp.concatenate([units[step][...].astype(jnp.int32) for step in steps], axis=1)
        return lax.dot_general(
            jnp.concatenate(halves(codes), axis=0),
            pick_ref[:, steps[0] * count : (steps[-1] + 1) * count],
            (((1,), (1,)), ((), ())),
            preferred_element_type=f32,
        )

    pick_sum_ref[...] = select(list(range(1, block_total)), units_ref)
    copies[0].wait()
    sides[0] = side_of(unit_ref)
    picked = select([0], [unit_ref]) + pick_sum_ref[...]
    picked = picked[: OUTS + AUX] * 256.0 + picked[OUTS + AUX :]
    scale = jnp.exp2(picked[OUTS + SCALE_ROW : OUTS + SCALE_ROW + 1])
    main_part = decoded(picked[:OUTS], scale)
    spill_part = pltpu.roll(decoded(picked[OUTS:], scale), rows, 1)
    row = lax.broadcasted_iota(jnp.int32, spill_part.shape, 0)
    column = lax.broadcasted_iota(jnp.int32, spill_part.shape, 1)
    spill_part = jnp.where((row < SPILL) & (column >= rows), spill_part, 0.0)
    samples = jnp.concatenate([main_part[:AUX] + spill_part, main_part[AUX:]], axis=0)
    samples = jnp.transpose(samples)
    for piece in range(PIECES):
        dec_ref[:, piece * OUTS : (piece + 1) * OUTS] = samples[piece * rows : (piece + 1) * rows]
    dec_ref[:, SPAN:] = jnp.zeros((rows, LANES), f32)
    lane = lax.broadcasted_iota(jnp.int32, (rows, LANES), 1)
    extra = wide_ref[WL:].astype(f32)
    taper = extra[0:1] + extra[1:2] + extra[2:3]
    inverse = (extra[3:4] + extra[4:5] + extra[5:6])[:, :NF]
    copies[1].wait()
    for window in range(WIN_DEV):
        start = starts_ref[window]
        base = pl.multiple_of((start >> 7) * LANES, LANES)
        offset = start & (LANES - 1)
        shift = (LANES - offset) & (LANES - 1)
        chunks = [
            pltpu.roll(dec_ref[:, pl.ds(base + tile * LANES, LANES)], shift, 1)
            for tile in range(WL // LANES + 1)
        ]
        here = lane < LANES - offset
        for tile in range(WL // LANES):
            at = slice(tile * LANES, (tile + 1) * LANES)
            seg_ref[window * rows : (window + 1) * rows, at] = (
                jnp.where(here, chunks[tile], chunks[tile + 1]) * taper[:, at]
            )
    spectra = jnp.dot(
        seg_ref[...].astype(jnp.bfloat16), wide_ref[:WL], preferred_element_type=f32
    )
    real = spectra[:, :NF]
    imag = spectra[:, NF:]
    energy = real * real + imag * imag
    high = energy.astype(jnp.bfloat16)
    rest = energy - high.astype(f32)
    middle = rest.astype(jnp.bfloat16)
    low = (rest - middle.astype(f32)).astype(jnp.bfloat16)
    band = band_ref[...]
    smooth = (
        jnp.dot(high, band, preferred_element_type=f32)
        + jnp.dot(middle, band, preferred_element_type=f32)
        + jnp.dot(low, band, preferred_element_type=f32)
    ) * inverse
    scale = lax.rsqrt(smooth + EPSILON)
    white_ref[:, :NF] = (real * scale).astype(jnp.bfloat16).astype(f32)
    white_ref[:, NF:] = (imag * scale).astype(jnp.bfloat16).astype(f32)
    total = jnp.zeros((block_total * CH_DEV, LAGS), f32)
    for tile in range(NF // LANES):
        re = slice(tile * LANES, (tile + 1) * LANES)
        im = slice(NF + tile * LANES, NF + (tile + 1) * LANES)
        real_sums = []
        imag_sums = []
        for group in range(0, block_total, 4):
            zero = jnp.zeros((CH_DEV, LANES), f32)
            sums = [[zero, zero, zero] for _ in range(4)]
            for window in range(WIN_DEV):
                own = slice(window * rows, window * rows + CH_DEV)
                loc_real = white_ref[own, re]
                loc_imag = white_ref[own, im]
                less = loc_real - loc_imag
                more = loc_real + loc_imag
                for number in range(4):
                    at = window * rows + CH_DEV + group + number
                    src_real = jnp.broadcast_to(white_ref[at : at + 1, re], (CH_DEV, LANES))
                    src_imag = jnp.broadcast_to(white_ref[at : at + 1, im], (CH_DEV, LANES))
                    sums[number][0] += loc_real * (src_real + src_imag)
                    sums[number][1] += less * src_imag
                    sums[number][2] += more * src_real
            real_sums += [both - imag for both, imag, real in sums]
            imag_sums += [both - real for both, imag, real in sums]
        cross = jnp.concatenate(
            [
                jnp.concatenate(real_sums, axis=0).astype(jnp.bfloat16),
                jnp.concatenate(imag_sums, axis=0).astype(jnp.bfloat16),
            ],
            axis=1,
        )
        total += jnp.dot(
            cross,
            lags_ref[2 * tile * LANES : 2 * (tile + 1) * LANES],
            preferred_element_type=f32,
        )
    out_ref[...] = total
    part = keep_ref.shape[0]
    keep_ref[...] = out_ref[pl.ds(pl.multiple_of(half * part, 8), part)]
    send_ref[...] = out_ref[pl.ds(pl.multiple_of((span_total - 1 - half) * part, 8), part)]


def gathered_body(records, record_channel, record_piece, fir_taps, window_starts, source_slot):
    block_total = lax.axis_size("chan")
    span_total = lax.axis_size("win")
    vmem = pl.BlockSpec(memory_space=pltpu.VMEM)
    smem = pl.BlockSpec(memory_space=pltpu.SMEM)
    hbm = pl.BlockSpec(memory_space=pl.ANY)
    count = records.shape[0]
    unit_shape = (OUTS + AUX, count)
    unit, local = pl.pallas_call(
        filter_kernel,
        out_shape=(
            jax.ShapeDtypeStruct(unit_shape, jnp.int16),
            jax.ShapeDtypeStruct((LOCAL_ROWS, count), jnp.int16),
        ),
        in_specs=[hbm] * 5,
        out_specs=(hbm, hbm),
        scratch_shapes=[
            pltpu.VMEM(records.shape, records.dtype),
            pltpu.VMEM(record_channel.shape, jnp.int32),
            pltpu.VMEM(record_piece.shape, jnp.int32),
            pltpu.VMEM(fir_taps.shape, fir_taps.dtype),
            pltpu.SMEM((1,), jnp.int32),
            pltpu.VMEM(unit_shape, jnp.int16),
            pltpu.SemaphoreType.DMA((5,)),
        ],
        compiler_params=pltpu.CompilerParams(vmem_limit_bytes=FILTER_VMEM),
        cost_estimate=pl.CostEstimate(flops=FLOPS, bytes_accessed=1 << 20, transcendentals=0),
        name="filter",
    )(records, record_channel, record_piece, fir_taps, source_slot)

    def swap(value, step):
        return lax.ppermute(value, "chan", [(i, i ^ step) for i in range(block_total)])

    units = {0: unit}
    for step, last in LAST_HOP.items():
        units[step] = swap(units[step ^ last], last)
    rows = CH_DEV + block_total
    half_rows = block_total // span_total * CH_DEV
    half_shape = jax.ShapeDtypeStruct((half_rows, LAGS), jnp.float32)
    tables = [wide_table(), band_table(), lag_table()]
    keep, send = pl.pallas_call(
        lambda *refs: correlate_kernel(block_total, span_total, *refs),
        out_shape=(half_shape, half_shape),
        in_specs=[hbm, hbm, smem] + [vmem] * (block_total + 2),
        out_specs=(vmem, vmem),
        scratch_shapes=[
            pltpu.VMEM((PIECES * rows, block_total * count), jnp.bfloat16),
            pltpu.VMEM((2 * (OUTS + AUX), PIECES * rows), jnp.float32),
            pltpu.VMEM((rows, SPAN + LANES), jnp.float32),
            pltpu.VMEM((WIN_DEV * rows, WL), jnp.float32),
            pltpu.VMEM((WIN_DEV * rows, WL), jnp.float32),
            pltpu.VMEM((block_total * CH_DEV, LAGS), jnp.float32),
            pltpu.VMEM(unit_shape, jnp.int16),
            pltpu.SMEM((WIN_DEV,), jnp.int32),
            pltpu.SemaphoreType.DMA((2,)),
        ],
        compiler_params=pltpu.CompilerParams(vmem_limit_bytes=CORRELATE_VMEM),
        name="correlate",
    )(
        local,
        window_starts,
        source_slot,
        *[units[step] for step in ORDER],
        *[jnp.asarray(table) for table in tables],
    )
    other = lax.ppermute(send, "win", [(i, i ^ 1) for i in range(span_total)])
    return (keep + other).reshape(block_total // span_total, CH_DEV, LAGS)


def make_filter(fir_taps):
    outputs_per = SEG // DEC
    sample_index = jnp.arange(SEG, dtype=jnp.int32)[:, None]
    column_index = jnp.arange(outputs_per + SPILL, dtype=jnp.int32)[None, :]
    tap_index = jnp.where(
        column_index < outputs_per,
        DEC * column_index + DEC - 1 - sample_index,
        DEC * (column_index - outputs_per) + DEC - 1 + SEG - sample_index,
    )
    match_table = (
        tap_index[:, :, None] == jnp.arange(TAPS, dtype=jnp.int32)[None, None, :]
    ).astype(jnp.float32)
    return jnp.sum(match_table * fir_taps.astype(jnp.float32)[None, None, :], axis=2).astype(
        jnp.bfloat16
    )


def make_fourier():
    sample_index = jnp.arange(WL, dtype=jnp.int32)[:, None]
    freq_index = jnp.arange(NF, dtype=jnp.int32)[None, :]
    phase = 2.0 * math.pi * (sample_index * freq_index % WL).astype(jnp.float32) / WL
    return jnp.concatenate([jnp.cos(phase), -jnp.sin(phase)], axis=1).astype(jnp.bfloat16)


def make_taper():
    sample_index = jnp.arange(WL, dtype=jnp.int32).astype(jnp.float32)
    return 0.5 - 0.5 * jnp.cos(2.0 * math.pi * sample_index / WL)


def make_lags():
    freq_index = jnp.arange(NF, dtype=jnp.int32)[:, None]
    lag_index = jnp.arange(LAGS, dtype=jnp.int32)[None, :] - LAGS // 2
    phase = 2.0 * math.pi * (freq_index * lag_index % WL).astype(jnp.float32) / WL
    scale = 1.0 / math.sqrt(WL * WIN_DEV)
    return (jnp.concatenate([jnp.cos(phase), -jnp.sin(phase)], axis=0) * scale).astype(jnp.bfloat16)


def whiten(spectra):
    freq_index = jnp.arange(NF, dtype=jnp.int32)
    band_table = (jnp.abs(freq_index[:, None] - freq_index[None, :]) <= BAND).astype(jnp.float32)
    band_count = jnp.sum(band_table, axis=0)
    real_part = spectra[..., :NF]
    imag_part = spectra[..., NF:]
    energy = real_part * real_part + imag_part * imag_part
    smooth = jnp.dot(energy, band_table, precision=lax.Precision.HIGHEST) / band_count[None, :]
    amplitude = jnp.sqrt(smooth + EPSILON)
    return (spectra / jnp.concatenate([amplitude, amplitude], axis=-1)).astype(jnp.bfloat16)


def cross_spectrum(source_block, local_block):
    src_real = source_block[..., :NF]
    src_imag = source_block[..., NF:]
    loc_real = local_block[..., :NF]
    loc_imag = local_block[..., NF:]
    real_sum = jnp.einsum(
        "bwf,cwf->bcf", src_real, loc_real, preferred_element_type=jnp.float32
    ) + jnp.einsum("bwf,cwf->bcf", src_imag, loc_imag, preferred_element_type=jnp.float32)
    imag_sum = jnp.einsum(
        "bwf,cwf->bcf", src_imag, loc_real, preferred_element_type=jnp.float32
    ) - jnp.einsum("bwf,cwf->bcf", src_real, loc_imag, preferred_element_type=jnp.float32)
    return jnp.concatenate([real_sum, imag_sum], axis=-1).astype(jnp.bfloat16)


def over_blocks(block_fn, sources, channel_count):
    source_count = sources.shape[0]
    block_size = math.gcd(source_count, 16)
    block_count = source_count // block_size
    grouped = sources.reshape((block_count, block_size) + sources.shape[1:])
    return lax.map(block_fn, grouped).reshape(source_count, channel_count, LAGS)


def routed_body(records, record_channel, record_piece, fir_taps, window_starts, source_slot):
    block_total = lax.axis_size("chan")
    per_device = records.shape[0]
    capacity = 2 * per_device // block_total
    outputs_per = SEG // DEC
    owner_block = record_channel // CH_DEV
    local_slot = record_channel % CH_DEV * PIECES + record_piece
    one_hot = (owner_block[:, None] == jnp.arange(block_total, dtype=jnp.int32)[None, :]).astype(
        jnp.int32
    )
    earlier_count = jnp.sum((jnp.cumsum(one_hot, axis=0) - one_hot) * one_hot, axis=1)
    position = owner_block * capacity + earlier_count
    slot_table = (
        jnp.full((block_total * capacity,), -1, jnp.int32)
        .at[position]
        .set(local_slot)
        .reshape(block_total, capacity)
    )
    filter_matrix = make_filter(fir_taps)
    row_send = (
        jnp.zeros((block_total * capacity, SEG), jnp.bfloat16)
        .at[position]
        .set(records)
        .reshape(block_total, capacity, SEG)
    )
    rows_got, slots_got = (
        lax.all_to_all(row_send, "chan", split_axis=0, concat_axis=0, tiled=True),
        lax.all_to_all(slot_table, "chan", split_axis=0, concat_axis=0, tiled=True),
    )
    flat_slots = slots_got.reshape(-1)
    target = jnp.where(flat_slots >= 0, flat_slots, per_device)
    traces = (
        jnp.zeros((per_device, SEG), jnp.bfloat16)
        .at[target]
        .set(rows_got.reshape(-1, SEG), mode="drop")
    )
    filtered = jnp.dot(traces, filter_matrix, preferred_element_type=jnp.float32)
    main_part = filtered[:, :outputs_per]
    spill_part = filtered[:, outputs_per:]
    main_part = main_part.reshape(CH_DEV, PIECES, outputs_per)
    spill_part = spill_part.reshape(CH_DEV, PIECES, SPILL)
    carried = jnp.pad(spill_part[:, :-1, :], ((0, 0), (1, 0), (0, outputs_per - SPILL)))
    decimated = (main_part + carried).reshape(CH_DEV, SPAN)

    def window_cut(window_start):
        return lax.dynamic_slice_in_dim(decimated, window_start, WL, 1)

    segments = (jax.vmap(window_cut, out_axes=1)(window_starts) * make_taper()).astype(jnp.bfloat16)
    window_count = segments.shape[1]
    spectra = jnp.dot(segments.reshape(-1, WL), make_fourier(), preferred_element_type=jnp.float32)
    whitened = whiten(spectra).reshape(CH_DEV, window_count, WL)
    source = lax.dynamic_slice_in_dim(whitened, source_slot[0], 1, 0)
    gathered = lax.all_gather(source, "chan", axis=0, tiled=True)
    lag_table = make_lags()

    def span_block(source_block):
        cross_spectra = cross_spectrum(source_block, whitened)
        return jnp.dot(
            cross_spectra.reshape(-1, WL), lag_table, preferred_element_type=jnp.float32
        ).reshape(source_block.shape[0], CH_DEV, LAGS)

    return lax.psum_scatter(
        over_blocks(span_block, gathered, CH_DEV), "win", scatter_dimension=0, tiled=True
    )


def solution(mesh):
    in_specs = (
        P(("groups", "chan", "win"), None),
        P(("groups", "chan", "win")),
        P(("groups", "chan", "win")),
        P(),
        P(("groups", "win")),
        P(("groups", "chan")),
    )
    out_specs = P(("groups", "win"), "chan", None)
    body = gathered_body if mesh.shape["chan"] == 8 else routed_body
    return jax.shard_map(body, mesh=mesh, in_specs=in_specs, out_specs=out_specs, check_vma=False)
```

```python
import math

import jax
import jax.numpy as jnp
import ml_dtypes
import numpy as np
from jax import lax
from jax.experimental import pallas as pl
from jax.experimental.pallas import tpu as pltpu
from jax.sharding import PartitionSpec as P

CH_DEV = 16
SPAN = 2048
WIN_DEV = 8
WL = 1024
NF = 512
DEC = 4
TAPS = 32
SPILL = 7
SEG = 512
PIECES = 16
BAND = 64
LAGS = 256


EPSILON = 1e-06

LANES = 128
OUTS = SEG // DEC
AUX = 16
SCALE_ROW = SPILL
KEY_ROW = SPILL + 1
SLOT_ROW = SPILL + 2
FILTER_VMEM = 56 << 20
FLOPS = 10**10
CORRELATE_VMEM = 48 << 20
LOCAL_ROWS = 16384
LAST_HOP = {1: 1, 2: 2, 3: 3, 4: 4, 6: 2, 5: 1, 7: 3}
ORDER = (6, 7, 3, 2, 4, 1, 5)
CODE = 23000.0


def fourier_table():
    sample_index = np.arange(WL)[:, None]
    freq_index = np.arange(NF)[None, :]
    phase = 2.0 * np.pi * (sample_index * freq_index % WL) / WL
    return np.concatenate([np.cos(phase), -np.sin(phase)], axis=1).astype(ml_dtypes.bfloat16)


def lag_table():
    freq_index = np.arange(NF)[:, None]
    lag_index = np.arange(LAGS)[None, :] - LAGS // 2
    phase = 2.0 * np.pi * (freq_index * lag_index % WL) / WL
    scale = 1.0 / math.sqrt(WL * WIN_DEV)
    tiles = (NF // LANES, 1, LANES, LAGS)
    parts = [np.cos(phase).reshape(tiles), -np.sin(phase).reshape(tiles)]
    return (np.concatenate(parts, axis=1).reshape(2 * NF, LAGS) * scale).astype(ml_dtypes.bfloat16)


def band_table():
    freq_index = np.arange(NF)
    return (np.abs(freq_index[:, None] - freq_index[None, :]) <= BAND).astype(ml_dtypes.bfloat16)


def split_rows(row):
    rows = []
    for _ in range(3):
        rows.append(row.astype(ml_dtypes.bfloat16))
        row = row - rows[-1].astype(np.float32)
    return rows


def wide_table():
    freq_index = np.arange(NF)
    band = np.abs(freq_index[:, None] - freq_index[None, :]) <= BAND
    taper = (0.5 - 0.5 * np.cos(2.0 * np.pi * np.arange(WL) / WL)).astype(np.float32)
    inverse = np.zeros(WL, np.float32)
    inverse[:NF] = 1.0 / band.sum(axis=0)
    empty = [np.zeros(WL, ml_dtypes.bfloat16)] * 10
    rows = np.stack(split_rows(taper) + split_rows(inverse) + empty)
    return np.concatenate([fourier_table(), rows], axis=0)


def filter_kernel(
    records_hbm, channel_hbm, piece_hbm, taps_hbm, slot_hbm, unit_hbm, local_hbm, *scratch
):
    records_ref, channel_ref, piece_ref, taps_ref, slot_ref, unit_ref, arrived = scratch
    f32 = jnp.float32
    count = records_ref.shape[0]
    pairs = (
        (taps_hbm, taps_ref),
        (records_hbm, records_ref),
        (channel_hbm, channel_ref),
        (piece_hbm, piece_ref),
        (slot_hbm, slot_ref),
    )
    copies = [
        pltpu.make_async_copy(source, target, arrived.at[number])
        for number, (source, target) in enumerate(pairs)
    ]
    for copy in copies:
        copy.start()
    tap = lax.broadcasted_iota(jnp.int32, (TAPS, SEG), 0)
    sample = lax.broadcasted_iota(jnp.int32, (TAPS, SEG), 1)
    place = (((DEC - 1 - tap) & (SEG - 1)) == sample).astype(f32).astype(jnp.bfloat16)
    copies[0].wait()
    taps = jnp.broadcast_to(taps_ref[...].reshape(1, TAPS), (16, TAPS))
    first = jnp.dot(taps, place, preferred_element_type=f32)
    circulant = pltpu.roll(
        jnp.broadcast_to(first[0:1], (OUTS, SEG)), 0, 1, stride=DEC, stride_axis=0
    )
    output = lax.broadcasted_iota(jnp.int32, (OUTS, SEG), 0)
    sample = lax.broadcasted_iota(jnp.int32, (OUTS, SEG), 1)
    inside = sample <= DEC * output + DEC - 1
    main_filter = jnp.where(inside, circulant, 0.0)
    spill_filter = jnp.where(inside, 0.0, circulant)[:AUX]
    filters = jnp.concatenate([main_filter, spill_filter], axis=0).astype(jnp.bfloat16)
    copies[1].wait()
    filtered = lax.dot_general(
        filters, records_ref[...], (((1,), (1,)), ((), ())), preferred_element_type=f32
    )
    absolute = jnp.abs(filtered)
    largest = jnp.maximum(jnp.max(absolute, axis=0, keepdims=True), 1e-30)
    power = jnp.minimum(jnp.floor(jnp.log2(largest)) + 1.0, 126.0)
    root = jnp.sqrt(jnp.sqrt(absolute * jnp.exp2(-power)))
    code = jnp.floor(root * CODE + 0.5)
    code = jnp.where(filtered < 0.0, -code, code)
    unit_ref[:OUTS] = code[:OUTS].astype(jnp.int32).astype(jnp.int16)
    for copy in copies[2:]:
        copy.wait()
    row = lax.broadcasted_iota(jnp.int32, (AUX, count), 0)
    key = channel_ref[...].reshape(1, count) * PIECES + piece_ref[...].reshape(1, count)
    side = jnp.where(row < SPILL, code[OUTS:].astype(jnp.int32), 0)
    side = jnp.where(row == SCALE_ROW, power.astype(jnp.int32), side)
    side = jnp.where(row == KEY_ROW, key, side)
    side = jnp.where(row == SLOT_ROW, slot_ref[0], side)
    unit_ref[OUTS:] = side.astype(jnp.int16)
    out = pltpu.make_async_copy(unit_ref, unit_hbm, arrived.at[0])
    local = pltpu.make_async_copy(unit_ref, local_hbm.at[pl.ds(0, OUTS + AUX)], arrived.at[1])
    out.start()
    local.start()
    out.wait()
    local.wait()


def halves(code):
    first = (code >> 8).astype(jnp.float32).astype(jnp.bfloat16)
    return first, (code & 255).astype(jnp.float32).astype(jnp.bfloat16)


def decoded(code, scale):
    root = code * (1.0 / CODE)
    return (root * root) * (root * jnp.abs(root)) * scale


def lag_products(white_ref, lags_ref, rows, first, number):
    f32 = jnp.float32
    total = jnp.zeros((number * CH_DEV, LAGS), f32)
    for tile in range(NF // LANES):
        re = slice(tile * LANES, (tile + 1) * LANES)
        im = slice(NF + tile * LANES, NF + (tile + 1) * LANES)
        zero = jnp.zeros((CH_DEV, LANES), f32)
        sums = [[zero, zero, zero] for _ in range(number)]
        for window in range(WIN_DEV):
            own = slice(window * rows, window * rows + CH_DEV)
            loc_real = white_ref[own, re]
            loc_imag = white_ref[own, im]
            less = loc_real - loc_imag
            more = loc_real + loc_imag
            for source in range(number):
                at = window * rows + CH_DEV + first + source
                src_real = jnp.broadcast_to(white_ref[at : at + 1, re], (CH_DEV, LANES))
                src_imag = jnp.broadcast_to(white_ref[at : at + 1, im], (CH_DEV, LANES))
                sums[source][0] += loc_real * (src_real + src_imag)
                sums[source][1] += less * src_imag
                sums[source][2] += more * src_real
        real_sums = [both - imag for both, imag, real in sums]
        imag_sums = [both - real for both, imag, real in sums]
        cross = jnp.concatenate(
            [
                jnp.concatenate(real_sums, axis=0).astype(jnp.bfloat16),
                jnp.concatenate(imag_sums, axis=0).astype(jnp.bfloat16),
            ],
            axis=1,
        )
        total += jnp.dot(
            cross,
            lags_ref[2 * tile * LANES : 2 * (tile + 1) * LANES],
            preferred_element_type=f32,
        )
    return total


def correlate_kernel(block_total, span_total, *refs):
    local_hbm, starts_hbm, slot_ref = refs[:3]
    refs = refs[1:]
    units_ref = dict(zip(ORDER, refs[2 : block_total + 1]))
    wide_ref, band_ref, lags_ref, send_ref, white_ref = refs[block_total + 1 : block_total + 6]
    pick_ref, pick_sum_ref, dec_ref, seg_ref, unit_ref, starts_ref, arrived = refs[block_total + 6 :]
    f32 = jnp.float32
    pairs = (
        (local_hbm.at[pl.ds(0, OUTS + AUX)], unit_ref),
        (starts_hbm, starts_ref),
    )
    copies = [
        pltpu.make_async_copy(source, target, arrived.at[number])
        for number, (source, target) in enumerate(pairs)
    ]
    for copy in copies:
        copy.start()
    me = lax.axis_index("chan")
    half = lax.axis_index("win")
    rows = CH_DEV + block_total
    count = unit_ref.shape[1]

    def side_of(unit):
        return unit[OUTS:].astype(jnp.int32)

    sides = {step: side_of(unit) for step, unit in units_ref.items()}
    row = lax.broadcasted_iota(jnp.int32, (2 * rows, count), 0)
    odd = (row >= rows).astype(jnp.int32)
    row = row - odd * rows
    source = (row - CH_DEV + (1 + half) * (block_total // span_total)) % block_total
    source = jnp.where(row >= CH_DEV, source, -1)
    channel = me * CH_DEV + row
    channel = jnp.where(source == me, source * CH_DEV + slot_ref[0], channel)
    for step, side in sides.items():
        slot = jnp.broadcast_to(side[SLOT_ROW : SLOT_ROW + 1], (2 * rows, count))
        channel = jnp.where(source == (me ^ step), source * CH_DEV + slot, channel)
    wanted = channel * PIECES + odd

    def pick(step, side):
        key = jnp.broadcast_to(side[KEY_ROW : KEY_ROW + 1], (2 * rows, count))
        for pair in range(PIECES // 2):
            pick_ref[
                pair * 2 * rows : (pair + 1) * 2 * rows, step * count : (step + 1) * count
            ] = jnp.where(wanted + 2 * pair == key, 1.0, 0.0).astype(jnp.bfloat16)

    def select(steps, units):
        for step in steps:
            pick(step, sides[step])
        codes = jnp.concatenate([units[step][...].astype(jnp.int32) for step in steps], axis=1)
        return lax.dot_general(
            jnp.concatenate(halves(codes), axis=0),
            pick_ref[:, steps[0] * count : (steps[-1] + 1) * count],
            (((1,), (1,)), ((), ())),
            preferred_element_type=f32,
        )

    pick_sum_ref[...] = select(list(range(1, block_total)), units_ref)
    copies[0].wait()
    sides[0] = side_of(unit_ref)
    picked = select([0], [unit_ref]) + pick_sum_ref[...]
    picked = picked[: OUTS + AUX] * 256.0 + picked[OUTS + AUX :]
    scale = jnp.exp2(picked[OUTS + SCALE_ROW : OUTS + SCALE_ROW + 1])
    main_part = decoded(picked[:OUTS], scale)
    spill_part = pltpu.roll(decoded(picked[OUTS:], scale), rows, 1)
    row = lax.broadcasted_iota(jnp.int32, spill_part.shape, 0)
    column = lax.broadcasted_iota(jnp.int32, spill_part.shape, 1)
    spill_part = jnp.where((row < SPILL) & (column >= rows), spill_part, 0.0)
    samples = jnp.concatenate([main_part[:AUX] + spill_part, main_part[AUX:]], axis=0)
    samples = jnp.transpose(samples)
    for piece in range(PIECES):
        dec_ref[:, piece * OUTS : (piece + 1) * OUTS] = samples[piece * rows : (piece + 1) * rows]
    dec_ref[:, SPAN:] = jnp.zeros((rows, LANES), f32)
    lane = lax.broadcasted_iota(jnp.int32, (rows, LANES), 1)
    extra = wide_ref[WL:].astype(f32)
    taper = extra[0:1] + extra[1:2] + extra[2:3]
    inverse = (extra[3:4] + extra[4:5] + extra[5:6])[:, :NF]
    copies[1].wait()
    for window in range(WIN_DEV):
        start = starts_ref[window]
        base = pl.multiple_of((start >> 7) * LANES, LANES)
        offset = start & (LANES - 1)
        shift = (LANES - offset) & (LANES - 1)
        chunks = [
            pltpu.roll(dec_ref[:, pl.ds(base + tile * LANES, LANES)], shift, 1)
            for tile in range(WL // LANES + 1)
        ]
        here = lane < LANES - offset
        for tile in range(WL // LANES):
            at = slice(tile * LANES, (tile + 1) * LANES)
            seg_ref[window * rows : (window + 1) * rows, at] = (
                jnp.where(here, chunks[tile], chunks[tile + 1]) * taper[:, at]
            )
    spectra = jnp.dot(
        seg_ref[...].astype(jnp.bfloat16), wide_ref[:WL], preferred_element_type=f32
    )
    real = spectra[:, :NF]
    imag = spectra[:, NF:]
    energy = real * real + imag * imag
    high = energy.astype(jnp.bfloat16)
    rest = energy - high.astype(f32)
    middle = rest.astype(jnp.bfloat16)
    low = (rest - middle.astype(f32)).astype(jnp.bfloat16)
    band = band_ref[...]
    smooth = (
        jnp.dot(high, band, preferred_element_type=f32)
        + jnp.dot(middle, band, preferred_element_type=f32)
        + jnp.dot(low, band, preferred_element_type=f32)
    ) * inverse
    scale = lax.rsqrt(smooth + EPSILON)
    white_ref[:, :NF] = (real * scale).astype(jnp.bfloat16).astype(f32)
    white_ref[:, NF:] = (imag * scale).astype(jnp.bfloat16).astype(f32)
    send_ref[...] = lag_products(white_ref, lags_ref, rows, 0, block_total // span_total)


def keep_kernel(rows, first, number, white_ref, lags_ref, keep_ref):
    keep_ref[...] = lag_products(white_ref, lags_ref, rows, first, number)


def gathered_body(records, record_channel, record_piece, fir_taps, window_starts, source_slot):
    block_total = lax.axis_size("chan")
    span_total = lax.axis_size("win")
    vmem = pl.BlockSpec(memory_space=pltpu.VMEM)
    smem = pl.BlockSpec(memory_space=pltpu.SMEM)
    hbm = pl.BlockSpec(memory_space=pl.ANY)
    count = records.shape[0]
    unit_shape = (OUTS + AUX, count)
    unit, local = pl.pallas_call(
        filter_kernel,
        out_shape=(
            jax.ShapeDtypeStruct(unit_shape, jnp.int16),
            jax.ShapeDtypeStruct((LOCAL_ROWS, count), jnp.int16),
        ),
        in_specs=[hbm] * 5,
        out_specs=(hbm, hbm),
        scratch_shapes=[
            pltpu.VMEM(records.shape, records.dtype),
            pltpu.VMEM(record_channel.shape, jnp.int32),
            pltpu.VMEM(record_piece.shape, jnp.int32),
            pltpu.VMEM(fir_taps.shape, fir_taps.dtype),
            pltpu.SMEM((1,), jnp.int32),
            pltpu.VMEM(unit_shape, jnp.int16),
            pltpu.SemaphoreType.DMA((5,)),
        ],
        compiler_params=pltpu.CompilerParams(vmem_limit_bytes=FILTER_VMEM),
        cost_estimate=pl.CostEstimate(flops=FLOPS, bytes_accessed=1 << 20, transcendentals=0),
        name="filter",
    )(records, record_channel, record_piece, fir_taps, source_slot)

    def swap(value, step):
        return lax.ppermute(value, "chan", [(i, i ^ step) for i in range(block_total)])

    units = {0: unit}
    for step, last in LAST_HOP.items():
        units[step] = swap(units[step ^ last], last)
    rows = CH_DEV + block_total
    half_rows = block_total // span_total * CH_DEV
    half_shape = jax.ShapeDtypeStruct((half_rows, LAGS), jnp.float32)
    tables = [wide_table(), band_table(), lag_table()]
    lags = jnp.asarray(tables[2])
    half_count = block_total // span_total
    send, white = pl.pallas_call(
        lambda *refs: correlate_kernel(block_total, span_total, *refs),
        out_shape=(half_shape, jax.ShapeDtypeStruct((WIN_DEV * rows, WL), jnp.float32)),
        in_specs=[hbm, hbm, smem] + [vmem] * (block_total + 2),
        out_specs=(vmem, vmem),
        scratch_shapes=[
            pltpu.VMEM((PIECES * rows, block_total * count), jnp.bfloat16),
            pltpu.VMEM((2 * (OUTS + AUX), PIECES * rows), jnp.float32),
            pltpu.VMEM((rows, SPAN + LANES), jnp.float32),
            pltpu.VMEM((WIN_DEV * rows, WL), jnp.float32),
            pltpu.VMEM(unit_shape, jnp.int16),
            pltpu.SMEM((WIN_DEV,), jnp.int32),
            pltpu.SemaphoreType.DMA((2,)),
        ],
        compiler_params=pltpu.CompilerParams(vmem_limit_bytes=CORRELATE_VMEM),
        name="correlate",
    )(
        local,
        window_starts,
        source_slot,
        *[units[step] for step in ORDER],
        *[jnp.asarray(table) for table in tables[:2]],
        lags,
    )
    other = lax.ppermute(send, "win", [(i, i ^ 1) for i in range(span_total)])
    keep = pl.pallas_call(
        lambda *refs: keep_kernel(rows, half_count, half_count, *refs),
        out_shape=half_shape,
        in_specs=[vmem, vmem],
        out_specs=vmem,
        compiler_params=pltpu.CompilerParams(vmem_limit_bytes=32 << 20),
        name="keep",
    )(white, lags)
    return (keep + other).reshape(block_total // span_total, CH_DEV, LAGS)


def make_filter(fir_taps):
    outputs_per = SEG // DEC
    sample_index = jnp.arange(SEG, dtype=jnp.int32)[:, None]
    column_index = jnp.arange(outputs_per + SPILL, dtype=jnp.int32)[None, :]
    tap_index = jnp.where(
        column_index < outputs_per,
        DEC * column_index + DEC - 1 - sample_index,
        DEC * (column_index - outputs_per) + DEC - 1 + SEG - sample_index,
    )
    match_table = (
        tap_index[:, :, None] == jnp.arange(TAPS, dtype=jnp.int32)[None, None, :]
    ).astype(jnp.float32)
    return jnp.sum(match_table * fir_taps.astype(jnp.float32)[None, None, :], axis=2).astype(
        jnp.bfloat16
    )


def make_fourier():
    sample_index = jnp.arange(WL, dtype=jnp.int32)[:, None]
    freq_index = jnp.arange(NF, dtype=jnp.int32)[None, :]
    phase = 2.0 * math.pi * (sample_index * freq_index % WL).astype(jnp.float32) / WL
    return jnp.concatenate([jnp.cos(phase), -jnp.sin(phase)], axis=1).astype(jnp.bfloat16)


def make_taper():
    sample_index = jnp.arange(WL, dtype=jnp.int32).astype(jnp.float32)
    return 0.5 - 0.5 * jnp.cos(2.0 * math.pi * sample_index / WL)


def make_lags():
    freq_index = jnp.arange(NF, dtype=jnp.int32)[:, None]
    lag_index = jnp.arange(LAGS, dtype=jnp.int32)[None, :] - LAGS // 2
    phase = 2.0 * math.pi * (freq_index * lag_index % WL).astype(jnp.float32) / WL
    scale = 1.0 / math.sqrt(WL * WIN_DEV)
    return (jnp.concatenate([jnp.cos(phase), -jnp.sin(phase)], axis=0) * scale).astype(jnp.bfloat16)


def whiten(spectra):
    freq_index = jnp.arange(NF, dtype=jnp.int32)
    band_table = (jnp.abs(freq_index[:, None] - freq_index[None, :]) <= BAND).astype(jnp.float32)
    band_count = jnp.sum(band_table, axis=0)
    real_part = spectra[..., :NF]
    imag_part = spectra[..., NF:]
    energy = real_part * real_part + imag_part * imag_part
    smooth = jnp.dot(energy, band_table, precision=lax.Precision.HIGHEST) / band_count[None, :]
    amplitude = jnp.sqrt(smooth + EPSILON)
    return (spectra / jnp.concatenate([amplitude, amplitude], axis=-1)).astype(jnp.bfloat16)


def cross_spectrum(source_block, local_block):
    src_real = source_block[..., :NF]
    src_imag = source_block[..., NF:]
    loc_real = local_block[..., :NF]
    loc_imag = local_block[..., NF:]
    real_sum = jnp.einsum(
        "bwf,cwf->bcf", src_real, loc_real, preferred_element_type=jnp.float32
    ) + jnp.einsum("bwf,cwf->bcf", src_imag, loc_imag, preferred_element_type=jnp.float32)
    imag_sum = jnp.einsum(
        "bwf,cwf->bcf", src_imag, loc_real, preferred_element_type=jnp.float32
    ) - jnp.einsum("bwf,cwf->bcf", src_real, loc_imag, preferred_element_type=jnp.float32)
    return jnp.concatenate([real_sum, imag_sum], axis=-1).astype(jnp.bfloat16)


def over_blocks(block_fn, sources, channel_count):
    source_count = sources.shape[0]
    block_size = math.gcd(source_count, 16)
    block_count = source_count // block_size
    grouped = sources.reshape((block_count, block_size) + sources.shape[1:])
    return lax.map(block_fn, grouped).reshape(source_count, channel_count, LAGS)


def routed_body(records, record_channel, record_piece, fir_taps, window_starts, source_slot):
    block_total = lax.axis_size("chan")
    per_device = records.shape[0]
    capacity = 2 * per_device // block_total
    outputs_per = SEG // DEC
    owner_block = record_channel // CH_DEV
    local_slot = record_channel % CH_DEV * PIECES + record_piece
    one_hot = (owner_block[:, None] == jnp.arange(block_total, dtype=jnp.int32)[None, :]).astype(
        jnp.int32
    )
    earlier_count = jnp.sum((jnp.cumsum(one_hot, axis=0) - one_hot) * one_hot, axis=1)
    position = owner_block * capacity + earlier_count
    slot_table = (
        jnp.full((block_total * capacity,), -1, jnp.int32)
        .at[position]
        .set(local_slot)
        .reshape(block_total, capacity)
    )
    filter_matrix = make_filter(fir_taps)
    row_send = (
        jnp.zeros((block_total * capacity, SEG), jnp.bfloat16)
        .at[position]
        .set(records)
        .reshape(block_total, capacity, SEG)
    )
    rows_got, slots_got = (
        lax.all_to_all(row_send, "chan", split_axis=0, concat_axis=0, tiled=True),
        lax.all_to_all(slot_table, "chan", split_axis=0, concat_axis=0, tiled=True),
    )
    flat_slots = slots_got.reshape(-1)
    target = jnp.where(flat_slots >= 0, flat_slots, per_device)
    traces = (
        jnp.zeros((per_device, SEG), jnp.bfloat16)
        .at[target]
        .set(rows_got.reshape(-1, SEG), mode="drop")
    )
    filtered = jnp.dot(traces, filter_matrix, preferred_element_type=jnp.float32)
    main_part = filtered[:, :outputs_per]
    spill_part = filtered[:, outputs_per:]
    main_part = main_part.reshape(CH_DEV, PIECES, outputs_per)
    spill_part = spill_part.reshape(CH_DEV, PIECES, SPILL)
    carried = jnp.pad(spill_part[:, :-1, :], ((0, 0), (1, 0), (0, outputs_per - SPILL)))
    decimated = (main_part + carried).reshape(CH_DEV, SPAN)

    def window_cut(window_start):
        return lax.dynamic_slice_in_dim(decimated, window_start, WL, 1)

    segments = (jax.vmap(window_cut, out_axes=1)(window_starts) * make_taper()).astype(jnp.bfloat16)
    window_count = segments.shape[1]
    spectra = jnp.dot(segments.reshape(-1, WL), make_fourier(), preferred_element_type=jnp.float32)
    whitened = whiten(spectra).reshape(CH_DEV, window_count, WL)
    source = lax.dynamic_slice_in_dim(whitened, source_slot[0], 1, 0)
    gathered = lax.all_gather(source, "chan", axis=0, tiled=True)
    lag_table = make_lags()

    def span_block(source_block):
        cross_spectra = cross_spectrum(source_block, whitened)
        return jnp.dot(
            cross_spectra.reshape(-1, WL), lag_table, preferred_element_type=jnp.float32
        ).reshape(source_block.shape[0], CH_DEV, LAGS)

    return lax.psum_scatter(
        over_blocks(span_block, gathered, CH_DEV), "win", scatter_dimension=0, tiled=True
    )


def solution(mesh):
    in_specs = (
        P(("groups", "chan", "win"), None),
        P(("groups", "chan", "win")),
        P(("groups", "chan", "win")),
        P(),
        P(("groups", "win")),
        P(("groups", "chan")),
    )
    out_specs = P(("groups", "win"), "chan", None)
    body = gathered_body if mesh.shape["chan"] == 8 else routed_body
    return jax.shard_map(body, mesh=mesh, in_specs=in_specs, out_specs=out_specs, check_vma=False)
```

```python
import math

import jax
import jax.numpy as jnp
import ml_dtypes
import numpy as np
from jax import lax
from jax.experimental import pallas as pl
from jax.experimental.pallas import tpu as pltpu
from jax.sharding import PartitionSpec as P

CH_DEV = 16
SPAN = 2048
WIN_DEV = 8
WL = 1024
NF = 512
DEC = 4
TAPS = 32
SPILL = 7
SEG = 512
PIECES = 16
BAND = 64
LAGS = 256


EPSILON = 1e-06

LANES = 128
OUTS = SEG // DEC
AUX = 16
SCALE_ROW = SPILL
KEY_ROW = SPILL + 1
SLOT_ROW = SPILL + 2
FILTER_VMEM = 56 << 20
FLOPS = 10**10
EARLY_VMEM = 44 << 20
EARLY_FLOPS = 10**9
CORRELATE_VMEM = 40 << 20
LOCAL_ROWS = 32768
LAST_HOP = {1: 1, 2: 2, 3: 3, 4: 4, 6: 6, 5: 1, 7: 3}
EARLY = (0, 1, 2, 6, 3, 4)
LATE = (5, 7)
CODE = 23000.0


def fourier_table():
    sample_index = np.arange(WL)[:, None]
    freq_index = np.arange(NF)[None, :]
    phase = 2.0 * np.pi * (sample_index * freq_index % WL) / WL
    return np.concatenate([np.cos(phase), -np.sin(phase)], axis=1).astype(ml_dtypes.bfloat16)


def lag_table():
    freq_index = np.arange(NF)[:, None]
    lag_index = np.arange(LAGS)[None, :] - LAGS // 2
    phase = 2.0 * np.pi * (freq_index * lag_index % WL) / WL
    scale = 1.0 / math.sqrt(WL * WIN_DEV)
    tiles = (NF // LANES, 1, LANES, LAGS)
    parts = [np.cos(phase).reshape(tiles), -np.sin(phase).reshape(tiles)]
    return (np.concatenate(parts, axis=1).reshape(2 * NF, LAGS) * scale).astype(ml_dtypes.bfloat16)


def band_table():
    freq_index = np.arange(NF)
    return (np.abs(freq_index[:, None] - freq_index[None, :]) <= BAND).astype(ml_dtypes.bfloat16)


def split_rows(row):
    rows = []
    for _ in range(3):
        rows.append(row.astype(ml_dtypes.bfloat16))
        row = row - rows[-1].astype(np.float32)
    return rows


def wide_table():
    freq_index = np.arange(NF)
    band = np.abs(freq_index[:, None] - freq_index[None, :]) <= BAND
    taper = (0.5 - 0.5 * np.cos(2.0 * np.pi * np.arange(WL) / WL)).astype(np.float32)
    inverse = np.zeros(WL, np.float32)
    inverse[:NF] = 1.0 / band.sum(axis=0)
    empty = [np.zeros(WL, ml_dtypes.bfloat16)] * 10
    rows = np.stack(split_rows(taper) + split_rows(inverse) + empty)
    return np.concatenate([fourier_table(), rows], axis=0)


def filter_kernel(
    records_hbm, channel_hbm, piece_hbm, taps_hbm, slot_hbm, unit_hbm, local_hbm, *scratch
):
    records_ref, channel_ref, piece_ref, taps_ref, slot_ref, unit_ref, arrived = scratch
    f32 = jnp.float32
    count = records_ref.shape[0]
    pairs = (
        (taps_hbm, taps_ref),
        (records_hbm, records_ref),
        (channel_hbm, channel_ref),
        (piece_hbm, piece_ref),
        (slot_hbm, slot_ref),
    )
    copies = [
        pltpu.make_async_copy(source, target, arrived.at[number])
        for number, (source, target) in enumerate(pairs)
    ]
    for copy in copies:
        copy.start()
    tap = lax.broadcasted_iota(jnp.int32, (TAPS, SEG), 0)
    sample = lax.broadcasted_iota(jnp.int32, (TAPS, SEG), 1)
    place = (((DEC - 1 - tap) & (SEG - 1)) == sample).astype(f32).astype(jnp.bfloat16)
    copies[0].wait()
    taps = jnp.broadcast_to(taps_ref[...].reshape(1, TAPS), (16, TAPS))
    first = jnp.dot(taps, place, preferred_element_type=f32)
    circulant = pltpu.roll(
        jnp.broadcast_to(first[0:1], (OUTS, SEG)), 0, 1, stride=DEC, stride_axis=0
    )
    output = lax.broadcasted_iota(jnp.int32, (OUTS, SEG), 0)
    sample = lax.broadcasted_iota(jnp.int32, (OUTS, SEG), 1)
    inside = sample <= DEC * output + DEC - 1
    main_filter = jnp.where(inside, circulant, 0.0)
    spill_filter = jnp.where(inside, 0.0, circulant)[:AUX]
    filters = jnp.concatenate([main_filter, spill_filter], axis=0).astype(jnp.bfloat16)
    copies[1].wait()
    filtered = lax.dot_general(
        filters, records_ref[...], (((1,), (1,)), ((), ())), preferred_element_type=f32
    )
    absolute = jnp.abs(filtered)
    largest = jnp.maximum(jnp.max(absolute, axis=0, keepdims=True), 1e-30)
    power = jnp.minimum(jnp.floor(jnp.log2(largest)) + 1.0, 126.0)
    root = jnp.sqrt(jnp.sqrt(absolute * jnp.exp2(-power)))
    code = jnp.floor(root * CODE + 0.5)
    code = jnp.where(filtered < 0.0, -code, code)
    unit_ref[:OUTS] = code[:OUTS].astype(jnp.int32).astype(jnp.int16)
    for copy in copies[2:]:
        copy.wait()
    row = lax.broadcasted_iota(jnp.int32, (AUX, count), 0)
    key = channel_ref[...].reshape(1, count) * PIECES + piece_ref[...].reshape(1, count)
    side = jnp.where(row < SPILL, code[OUTS:].astype(jnp.int32), 0)
    side = jnp.where(row == SCALE_ROW, power.astype(jnp.int32), side)
    side = jnp.where(row == KEY_ROW, key, side)
    side = jnp.where(row == SLOT_ROW, slot_ref[0], side)
    unit_ref[OUTS:] = side.astype(jnp.int16)
    out = pltpu.make_async_copy(unit_ref, unit_hbm, arrived.at[0])
    local = pltpu.make_async_copy(unit_ref, local_hbm.at[pl.ds(0, OUTS + AUX)], arrived.at[1])
    out.start()
    local.start()
    out.wait()
    local.wait()


def halves(code):
    first = (code >> 8).astype(jnp.float32).astype(jnp.bfloat16)
    return first, (code & 255).astype(jnp.float32).astype(jnp.bfloat16)


def decoded(code, scale):
    root = code * (1.0 / CODE)
    return (root * root) * (root * jnp.abs(root)) * scale


def lag_products(white_ref, lags_ref, rows, first, number):
    f32 = jnp.float32
    total = jnp.zeros((number * CH_DEV, LAGS), f32)
    for tile in range(NF // LANES):
        re = slice(tile * LANES, (tile + 1) * LANES)
        im = slice(NF + tile * LANES, NF + (tile + 1) * LANES)
        zero = jnp.zeros((CH_DEV, LANES), f32)
        sums = [[zero, zero, zero] for _ in range(number)]
        for window in range(WIN_DEV):
            own = slice(window * rows, window * rows + CH_DEV)
            loc_real = white_ref[own, re]
            loc_imag = white_ref[own, im]
            less = loc_real - loc_imag
            more = loc_real + loc_imag
            for source in range(number):
                at = window * rows + CH_DEV + first + source
                src_real = jnp.broadcast_to(white_ref[at : at + 1, re], (CH_DEV, LANES))
                src_imag = jnp.broadcast_to(white_ref[at : at + 1, im], (CH_DEV, LANES))
                sums[source][0] += loc_real * (src_real + src_imag)
                sums[source][1] += less * src_imag
                sums[source][2] += more * src_real
        real_sums = [both - imag for both, imag, real in sums]
        imag_sums = [both - real for both, imag, real in sums]
        cross = jnp.concatenate(
            [
                jnp.concatenate(real_sums, axis=0).astype(jnp.bfloat16),
                jnp.concatenate(imag_sums, axis=0).astype(jnp.bfloat16),
            ],
            axis=1,
        )
        total += jnp.dot(
            cross,
            lags_ref[2 * tile * LANES : 2 * (tile + 1) * LANES],
            preferred_element_type=f32,
        )
    return total


def pick_rows(pick_ref, key, first, group, wanted):
    shape = (2 * group, key.shape[1])
    key = jnp.broadcast_to(key, shape)
    for pair in range(PIECES // 2):
        pick_ref[pair * 2 * group : (pair + 1) * 2 * group, first : first + shape[1]] = jnp.where(
            wanted + 2 * pair == key, 1.0, 0.0
        ).astype(jnp.bfloat16)


def wanted_own(me, count):
    row = lax.broadcasted_iota(jnp.int32, (2 * CH_DEV, count), 0)
    odd = (row >= CH_DEV).astype(jnp.int32)
    return (me * CH_DEV + row - odd * CH_DEV) * PIECES + odd


def selected(data, pick):
    return lax.dot_general(data, pick, (((1,), (1,)), ((), ())), preferred_element_type=jnp.float32)


def early_kernel(early_total, *refs):
    local_hbm = refs[0]
    units_ref = refs[1:early_total]
    own_ref, data_ref, side_ref, pick_ref, unit_ref, arrived = refs[early_total:]
    copy = pltpu.make_async_copy(local_hbm.at[pl.ds(0, OUTS + AUX)], unit_ref, arrived)
    copy.start()
    count = unit_ref.shape[1]
    wanted = wanted_own(lax.axis_index("chan"), count)

    def take(unit, number):
        at = slice(number * count, (number + 1) * count)
        codes = unit[...].astype(jnp.int32)
        first, second = halves(codes)
        data_ref[: OUTS + AUX, at] = first
        data_ref[OUTS + AUX :, at] = second
        side_ref[:, at] = codes[OUTS:]
        pick_rows(pick_ref, codes[OUTS + KEY_ROW : OUTS + KEY_ROW + 1], number * count, CH_DEV, wanted)

    for number in range(1, early_total):
        take(units_ref[number - 1], number)
    own_ref[...] = selected(data_ref[:, count:], pick_ref[:, count:])
    copy.wait()
    take(unit_ref, 0)
    own_ref[...] += selected(data_ref[:, :count], pick_ref[:, :count])


def samples_of(picked, group):
    code = picked[: OUTS + AUX] * 256.0 + picked[OUTS + AUX :]
    scale = jnp.exp2(code[OUTS + SCALE_ROW : OUTS + SCALE_ROW + 1])
    main_part = decoded(code[:OUTS], scale)
    spill_part = pltpu.roll(decoded(code[OUTS:], scale), group, 1)
    row = lax.broadcasted_iota(jnp.int32, spill_part.shape, 0)
    column = lax.broadcasted_iota(jnp.int32, spill_part.shape, 1)
    spill_part = jnp.where((row < SPILL) & (column >= group), spill_part, 0.0)
    return jnp.transpose(jnp.concatenate([main_part[:AUX] + spill_part, main_part[AUX:]], axis=0))


def correlate_kernel(block_total, span_total, *refs):
    f32 = jnp.float32
    own_ref, data_ref, side_ref, starts_hbm, slot_ref = refs[:5]
    refs = refs[5:]
    units_ref = dict(zip(LATE, refs))
    refs = refs[len(LATE) :]
    wide_ref, band_ref, lags_ref, send_ref, white_ref = refs[:5]
    pick_own_ref, pick_src_ref, dec_ref, seg_ref, starts_ref, arrived = refs[5:]
    copy = pltpu.make_async_copy(starts_hbm, starts_ref, arrived)
    copy.start()
    me = lax.axis_index("chan")
    half = lax.axis_index("win")
    rows = CH_DEV + block_total
    count = side_ref.shape[1] // len(EARLY)
    late = {step: unit[...].astype(jnp.int32) for step, unit in units_ref.items()}
    sides = {step: side_ref[:, n * count : (n + 1) * count] for n, step in enumerate(EARLY)}
    sides |= {step: codes[OUTS:] for step, codes in late.items()}
    row = lax.broadcasted_iota(jnp.int32, (2 * block_total, count), 0)
    odd = (row >= block_total).astype(jnp.int32)
    source = (row + (1 + half) * (block_total // span_total)) % block_total
    channel = source * CH_DEV + slot_ref[0]
    for step, side in sides.items():
        if step:
            slot = jnp.broadcast_to(side[SLOT_ROW : SLOT_ROW + 1], source.shape)
            channel = jnp.where(source == (me ^ step), source * CH_DEV + slot, channel)
    wanted = channel * PIECES + odd
    own = wanted_own(me, count)
    for number, step in enumerate(EARLY + LATE):
        key = sides[step][KEY_ROW : KEY_ROW + 1]
        pick_rows(pick_src_ref, key, number * count, block_total, wanted)
        if step in late:
            pick_rows(pick_own_ref, key, (number - len(EARLY)) * count, CH_DEV, own)
    codes = jnp.concatenate([late[step] for step in LATE], axis=1)
    late_data = jnp.concatenate(halves(codes), axis=0)
    split = len(EARLY) * count
    picked_src = selected(data_ref[...], pick_src_ref[:, :split])
    picked_src += selected(late_data, pick_src_ref[:, split:])
    picked_own = own_ref[...] + selected(late_data, pick_own_ref[...])
    samples = samples_of(picked_own, CH_DEV)
    sources = samples_of(picked_src, block_total)
    for piece in range(PIECES):
        at = slice(piece * OUTS, (piece + 1) * OUTS)
        dec_ref[:CH_DEV, at] = samples[piece * CH_DEV : (piece + 1) * CH_DEV]
        dec_ref[CH_DEV:, at] = sources[piece * block_total : (piece + 1) * block_total]
    dec_ref[:, SPAN:] = jnp.zeros((rows, LANES), f32)
    lane = lax.broadcasted_iota(jnp.int32, (rows, LANES), 1)
    extra = wide_ref[WL:].astype(f32)
    taper = extra[0:1] + extra[1:2] + extra[2:3]
    inverse = (extra[3:4] + extra[4:5] + extra[5:6])[:, :NF]
    copy.wait()
    for window in range(WIN_DEV):
        start = starts_ref[window]
        base = pl.multiple_of((start >> 7) * LANES, LANES)
        offset = start & (LANES - 1)
        shift = (LANES - offset) & (LANES - 1)
        chunks = [
            pltpu.roll(dec_ref[:, pl.ds(base + tile * LANES, LANES)], shift, 1)
            for tile in range(WL // LANES + 1)
        ]
        here = lane < LANES - offset
        for tile in range(WL // LANES):
            at = slice(tile * LANES, (tile + 1) * LANES)
            seg_ref[window * rows : (window + 1) * rows, at] = (
                jnp.where(here, chunks[tile], chunks[tile + 1]) * taper[:, at]
            )
    spectra = jnp.dot(
        seg_ref[...].astype(jnp.bfloat16), wide_ref[:WL], preferred_element_type=f32
    )
    real = spectra[:, :NF]
    imag = spectra[:, NF:]
    energy = real * real + imag * imag
    high = energy.astype(jnp.bfloat16)
    rest = energy - high.astype(f32)
    middle = rest.astype(jnp.bfloat16)
    low = (rest - middle.astype(f32)).astype(jnp.bfloat16)
    band = band_ref[...]
    smooth = (
        jnp.dot(high, band, preferred_element_type=f32)
        + jnp.dot(middle, band, preferred_element_type=f32)
        + jnp.dot(low, band, preferred_element_type=f32)
    ) * inverse
    scale = lax.rsqrt(smooth + EPSILON)
    white_ref[:, :NF] = (real * scale).astype(jnp.bfloat16).astype(f32)
    white_ref[:, NF:] = (imag * scale).astype(jnp.bfloat16).astype(f32)
    send_ref[...] = lag_products(white_ref, lags_ref, rows, 0, block_total // span_total)


def keep_kernel(rows, first, number, white_ref, lags_ref, keep_ref):
    keep_ref[...] = lag_products(white_ref, lags_ref, rows, first, number)


def gathered_body(records, record_channel, record_piece, fir_taps, window_starts, source_slot):
    block_total = lax.axis_size("chan")
    span_total = lax.axis_size("win")
    vmem = pl.BlockSpec(memory_space=pltpu.VMEM)
    smem = pl.BlockSpec(memory_space=pltpu.SMEM)
    hbm = pl.BlockSpec(memory_space=pl.ANY)
    count = records.shape[0]
    unit_shape = (OUTS + AUX, count)
    unit, local = pl.pallas_call(
        filter_kernel,
        out_shape=(
            jax.ShapeDtypeStruct(unit_shape, jnp.int16),
            jax.ShapeDtypeStruct((LOCAL_ROWS, count), jnp.int16),
        ),
        in_specs=[hbm] * 5,
        out_specs=(hbm, hbm),
        scratch_shapes=[
            pltpu.VMEM(records.shape, records.dtype),
            pltpu.VMEM(record_channel.shape, jnp.int32),
            pltpu.VMEM(record_piece.shape, jnp.int32),
            pltpu.VMEM(fir_taps.shape, fir_taps.dtype),
            pltpu.SMEM((1,), jnp.int32),
            pltpu.VMEM(unit_shape, jnp.int16),
            pltpu.SemaphoreType.DMA((5,)),
        ],
        compiler_params=pltpu.CompilerParams(vmem_limit_bytes=FILTER_VMEM),
        cost_estimate=pl.CostEstimate(flops=FLOPS, bytes_accessed=1 << 20, transcendentals=0),
        name="filter",
    )(records, record_channel, record_piece, fir_taps, source_slot)

    def swap(value, step):
        return lax.ppermute(value, "chan", [(i, i ^ step) for i in range(block_total)])

    units = {0: unit}
    for step, last in LAST_HOP.items():
        units[step] = swap(units[step ^ last], last)
    rows = CH_DEV + block_total
    half_rows = block_total // span_total * CH_DEV
    half_shape = jax.ShapeDtypeStruct((half_rows, LAGS), jnp.float32)
    tables = [wide_table(), band_table(), lag_table()]
    lags = jnp.asarray(tables[2])
    half_count = block_total // span_total
    data_shape = (2 * unit_shape[0], len(EARLY) * count)
    own, data, side = pl.pallas_call(
        lambda *refs: early_kernel(len(EARLY), *refs),
        out_shape=(
            jax.ShapeDtypeStruct((2 * unit_shape[0], PIECES * CH_DEV), jnp.float32),
            jax.ShapeDtypeStruct(data_shape, jnp.bfloat16),
            jax.ShapeDtypeStruct((AUX, len(EARLY) * count), jnp.int32),
        ),
        in_specs=[hbm] + [vmem] * (len(EARLY) - 1),
        out_specs=(vmem, vmem, vmem),
        scratch_shapes=[
            pltpu.VMEM((PIECES * CH_DEV, len(EARLY) * count), jnp.bfloat16),
            pltpu.VMEM(unit_shape, jnp.int16),
            pltpu.SemaphoreType.DMA,
        ],
        compiler_params=pltpu.CompilerParams(vmem_limit_bytes=EARLY_VMEM),
        cost_estimate=pl.CostEstimate(flops=EARLY_FLOPS, bytes_accessed=1 << 20, transcendentals=0),
        name="early",
    )(local, *[units[step] for step in EARLY[1:]])
    send, white = pl.pallas_call(
        lambda *refs: correlate_kernel(block_total, span_total, *refs),
        out_shape=(half_shape, jax.ShapeDtypeStruct((WIN_DEV * rows, WL), jnp.float32)),
        in_specs=[vmem, vmem, vmem, hbm, smem] + [vmem] * (len(LATE) + 3),
        out_specs=(vmem, vmem),
        scratch_shapes=[
            pltpu.VMEM((PIECES * CH_DEV, len(LATE) * count), jnp.bfloat16),
            pltpu.VMEM((PIECES * block_total, block_total * count), jnp.bfloat16),
            pltpu.VMEM((rows, SPAN + LANES), jnp.float32),
            pltpu.VMEM((WIN_DEV * rows, WL), jnp.float32),
            pltpu.SMEM((WIN_DEV,), jnp.int32),
            pltpu.SemaphoreType.DMA,
        ],
        compiler_params=pltpu.CompilerParams(vmem_limit_bytes=CORRELATE_VMEM),
        name="correlate",
    )(
        own,
        data,
        side,
        window_starts,
        source_slot,
        *[units[step] for step in LATE],
        *[jnp.asarray(table) for table in tables[:2]],
        lags,
    )
    other = lax.ppermute(send, "win", [(i, i ^ 1) for i in range(span_total)])
    keep = pl.pallas_call(
        lambda *refs: keep_kernel(rows, half_count, half_count, *refs),
        out_shape=half_shape,
        in_specs=[vmem, vmem],
        out_specs=vmem,
        compiler_params=pltpu.CompilerParams(vmem_limit_bytes=32 << 20),
        name="keep",
    )(white, lags)
    return (keep + other).reshape(block_total // span_total, CH_DEV, LAGS)


def make_filter(fir_taps):
    outputs_per = SEG // DEC
    sample_index = jnp.arange(SEG, dtype=jnp.int32)[:, None]
    column_index = jnp.arange(outputs_per + SPILL, dtype=jnp.int32)[None, :]
    tap_index = jnp.where(
        column_index < outputs_per,
        DEC * column_index + DEC - 1 - sample_index,
        DEC * (column_index - outputs_per) + DEC - 1 + SEG - sample_index,
    )
    match_table = (
        tap_index[:, :, None] == jnp.arange(TAPS, dtype=jnp.int32)[None, None, :]
    ).astype(jnp.float32)
    return jnp.sum(match_table * fir_taps.astype(jnp.float32)[None, None, :], axis=2).astype(
        jnp.bfloat16
    )


def make_fourier():
    sample_index = jnp.arange(WL, dtype=jnp.int32)[:, None]
    freq_index = jnp.arange(NF, dtype=jnp.int32)[None, :]
    phase = 2.0 * math.pi * (sample_index * freq_index % WL).astype(jnp.float32) / WL
    return jnp.concatenate([jnp.cos(phase), -jnp.sin(phase)], axis=1).astype(jnp.bfloat16)


def make_taper():
    sample_index = jnp.arange(WL, dtype=jnp.int32).astype(jnp.float32)
    return 0.5 - 0.5 * jnp.cos(2.0 * math.pi * sample_index / WL)


def make_lags():
    freq_index = jnp.arange(NF, dtype=jnp.int32)[:, None]
    lag_index = jnp.arange(LAGS, dtype=jnp.int32)[None, :] - LAGS // 2
    phase = 2.0 * math.pi * (freq_index * lag_index % WL).astype(jnp.float32) / WL
    scale = 1.0 / math.sqrt(WL * WIN_DEV)
    return (jnp.concatenate([jnp.cos(phase), -jnp.sin(phase)], axis=0) * scale).astype(jnp.bfloat16)


def whiten(spectra):
    freq_index = jnp.arange(NF, dtype=jnp.int32)
    band_table = (jnp.abs(freq_index[:, None] - freq_index[None, :]) <= BAND).astype(jnp.float32)
    band_count = jnp.sum(band_table, axis=0)
    real_part = spectra[..., :NF]
    imag_part = spectra[..., NF:]
    energy = real_part * real_part + imag_part * imag_part
    smooth = jnp.dot(energy, band_table, precision=lax.Precision.HIGHEST) / band_count[None, :]
    amplitude = jnp.sqrt(smooth + EPSILON)
    return (spectra / jnp.concatenate([amplitude, amplitude], axis=-1)).astype(jnp.bfloat16)


def cross_spectrum(source_block, local_block):
    src_real = source_block[..., :NF]
    src_imag = source_block[..., NF:]
    loc_real = local_block[..., :NF]
    loc_imag = local_block[..., NF:]
    real_sum = jnp.einsum(
        "bwf,cwf->bcf", src_real, loc_real, preferred_element_type=jnp.float32
    ) + jnp.einsum("bwf,cwf->bcf", src_imag, loc_imag, preferred_element_type=jnp.float32)
    imag_sum = jnp.einsum(
        "bwf,cwf->bcf", src_imag, loc_real, preferred_element_type=jnp.float32
    ) - jnp.einsum("bwf,cwf->bcf", src_real, loc_imag, preferred_element_type=jnp.float32)
    return jnp.concatenate([real_sum, imag_sum], axis=-1).astype(jnp.bfloat16)


def over_blocks(block_fn, sources, channel_count):
    source_count = sources.shape[0]
    block_size = math.gcd(source_count, 16)
    block_count = source_count // block_size
    grouped = sources.reshape((block_count, block_size) + sources.shape[1:])
    return lax.map(block_fn, grouped).reshape(source_count, channel_count, LAGS)


def routed_body(records, record_channel, record_piece, fir_taps, window_starts, source_slot):
    block_total = lax.axis_size("chan")
    per_device = records.shape[0]
    capacity = 2 * per_device // block_total
    outputs_per = SEG // DEC
    owner_block = record_channel // CH_DEV
    local_slot = record_channel % CH_DEV * PIECES + record_piece
    one_hot = (owner_block[:, None] == jnp.arange(block_total, dtype=jnp.int32)[None, :]).astype(
        jnp.int32
    )
    earlier_count = jnp.sum((jnp.cumsum(one_hot, axis=0) - one_hot) * one_hot, axis=1)
    position = owner_block * capacity + earlier_count
    slot_table = (
        jnp.full((block_total * capacity,), -1, jnp.int32)
        .at[position]
        .set(local_slot)
        .reshape(block_total, capacity)
    )
    filter_matrix = make_filter(fir_taps)
    row_send = (
        jnp.zeros((block_total * capacity, SEG), jnp.bfloat16)
        .at[position]
        .set(records)
        .reshape(block_total, capacity, SEG)
    )
    rows_got, slots_got = (
        lax.all_to_all(row_send, "chan", split_axis=0, concat_axis=0, tiled=True),
        lax.all_to_all(slot_table, "chan", split_axis=0, concat_axis=0, tiled=True),
    )
    flat_slots = slots_got.reshape(-1)
    target = jnp.where(flat_slots >= 0, flat_slots, per_device)
    traces = (
        jnp.zeros((per_device, SEG), jnp.bfloat16)
        .at[target]
        .set(rows_got.reshape(-1, SEG), mode="drop")
    )
    filtered = jnp.dot(traces, filter_matrix, preferred_element_type=jnp.float32)
    main_part = filtered[:, :outputs_per]
    spill_part = filtered[:, outputs_per:]
    main_part = main_part.reshape(CH_DEV, PIECES, outputs_per)
    spill_part = spill_part.reshape(CH_DEV, PIECES, SPILL)
    carried = jnp.pad(spill_part[:, :-1, :], ((0, 0), (1, 0), (0, outputs_per - SPILL)))
    decimated = (main_part + carried).reshape(CH_DEV, SPAN)

    def window_cut(window_start):
        return lax.dynamic_slice_in_dim(decimated, window_start, WL, 1)

    segments = (jax.vmap(window_cut, out_axes=1)(window_starts) * make_taper()).astype(jnp.bfloat16)
    window_count = segments.shape[1]
    spectra = jnp.dot(segments.reshape(-1, WL), make_fourier(), preferred_element_type=jnp.float32)
    whitened = whiten(spectra).reshape(CH_DEV, window_count, WL)
    source = lax.dynamic_slice_in_dim(whitened, source_slot[0], 1, 0)
    gathered = lax.all_gather(source, "chan", axis=0, tiled=True)
    lag_table = make_lags()

    def span_block(source_block):
        cross_spectra = cross_spectrum(source_block, whitened)
        return jnp.dot(
            cross_spectra.reshape(-1, WL), lag_table, preferred_element_type=jnp.float32
        ).reshape(source_block.shape[0], CH_DEV, LAGS)

    return lax.psum_scatter(
        over_blocks(span_block, gathered, CH_DEV), "win", scatter_dimension=0, tiled=True
    )


def solution(mesh):
    in_specs = (
        P(("groups", "chan", "win"), None),
        P(("groups", "chan", "win")),
        P(("groups", "chan", "win")),
        P(),
        P(("groups", "win")),
        P(("groups", "chan")),
    )
    out_specs = P(("groups", "win"), "chan", None)
    body = gathered_body if mesh.shape["chan"] == 8 else routed_body
    return jax.shard_map(body, mesh=mesh, in_specs=in_specs, out_specs=out_specs, check_vma=False)
```

```python
import math

import jax
import jax.numpy as jnp
import ml_dtypes
import numpy as np
from jax import lax
from jax.experimental import pallas as pl
from jax.experimental.pallas import tpu as pltpu
from jax.sharding import PartitionSpec as P

CH_DEV = 16
SPAN = 2048
WIN_DEV = 8
WL = 1024
NF = 512
DEC = 4
TAPS = 32
SPILL = 7
SEG = 512
PIECES = 16
BAND = 64
LAGS = 256


EPSILON = 1e-06

LANES = 128
OUTS = SEG // DEC
AUX = 16
SCALE_ROW = SPILL
KEY_ROW = SPILL + 1
SLOT_ROW = SPILL + 2
FILTER_VMEM = 56 << 20
FLOPS = 10**10
EARLY_VMEM = 44 << 20
EARLY_FLOPS = 10**9
CORRELATE_VMEM = 40 << 20
LOCAL_ROWS = 32768
LAST_HOP = {1: 1, 2: 2, 3: 3, 4: 4, 6: 6, 5: 1, 7: 3}
EARLY = (0, 1, 2, 6, 3, 4)
LATE = (5, 7)
CODE = 23000.0


def fourier_table():
    sample_index = np.arange(WL)[:, None]
    freq_index = np.arange(NF)[None, :]
    phase = 2.0 * np.pi * (sample_index * freq_index % WL) / WL
    return np.concatenate([np.cos(phase), -np.sin(phase)], axis=1).astype(ml_dtypes.bfloat16)


def lag_table():
    freq_index = np.arange(NF)[:, None]
    lag_index = np.arange(LAGS)[None, :] - LAGS // 2
    phase = 2.0 * np.pi * (freq_index * lag_index % WL) / WL
    scale = 1.0 / math.sqrt(WL * WIN_DEV)
    tiles = (NF // LANES, 1, LANES, LAGS)
    parts = [np.cos(phase).reshape(tiles), -np.sin(phase).reshape(tiles)]
    return (np.concatenate(parts, axis=1).reshape(2 * NF, LAGS) * scale).astype(ml_dtypes.bfloat16)


def band_table():
    freq_index = np.arange(NF)
    return (np.abs(freq_index[:, None] - freq_index[None, :]) <= BAND).astype(ml_dtypes.bfloat16)


def split_rows(row):
    rows = []
    for _ in range(3):
        rows.append(row.astype(ml_dtypes.bfloat16))
        row = row - rows[-1].astype(np.float32)
    return rows


def wide_table():
    freq_index = np.arange(NF)
    band = np.abs(freq_index[:, None] - freq_index[None, :]) <= BAND
    taper = (0.5 - 0.5 * np.cos(2.0 * np.pi * np.arange(WL) / WL)).astype(np.float32)
    inverse = np.zeros(WL, np.float32)
    inverse[:NF] = 1.0 / band.sum(axis=0)
    empty = [np.zeros(WL, ml_dtypes.bfloat16)] * 10
    rows = np.stack(split_rows(taper) + split_rows(inverse) + empty)
    return np.concatenate([fourier_table(), rows], axis=0)


def filter_kernel(
    records_hbm, channel_hbm, piece_hbm, taps_hbm, slot_hbm, unit_hbm, *scratch
):
    records_ref, channel_ref, piece_ref, taps_ref, slot_ref, unit_ref, arrived = scratch
    f32 = jnp.float32
    count = records_ref.shape[0]
    pairs = (
        (taps_hbm, taps_ref),
        (records_hbm, records_ref),
        (channel_hbm, channel_ref),
        (piece_hbm, piece_ref),
        (slot_hbm, slot_ref),
    )
    copies = [
        pltpu.make_async_copy(source, target, arrived.at[number])
        for number, (source, target) in enumerate(pairs)
    ]
    for copy in copies:
        copy.start()
    tap = lax.broadcasted_iota(jnp.int32, (TAPS, SEG), 0)
    sample = lax.broadcasted_iota(jnp.int32, (TAPS, SEG), 1)
    place = (((DEC - 1 - tap) & (SEG - 1)) == sample).astype(f32).astype(jnp.bfloat16)
    copies[0].wait()
    taps = jnp.broadcast_to(taps_ref[...].reshape(1, TAPS), (16, TAPS))
    first = jnp.dot(taps, place, preferred_element_type=f32)
    circulant = pltpu.roll(
        jnp.broadcast_to(first[0:1], (OUTS, SEG)), 0, 1, stride=DEC, stride_axis=0
    )
    output = lax.broadcasted_iota(jnp.int32, (OUTS, SEG), 0)
    sample = lax.broadcasted_iota(jnp.int32, (OUTS, SEG), 1)
    inside = sample <= DEC * output + DEC - 1
    main_filter = jnp.where(inside, circulant, 0.0)
    spill_filter = jnp.where(inside, 0.0, circulant)[:AUX]
    filters = jnp.concatenate([main_filter, spill_filter], axis=0).astype(jnp.bfloat16)
    copies[1].wait()
    filtered = lax.dot_general(
        filters, records_ref[...], (((1,), (1,)), ((), ())), preferred_element_type=f32
    )
    absolute = jnp.abs(filtered)
    largest = jnp.maximum(jnp.max(absolute, axis=0, keepdims=True), 1e-30)
    power = jnp.minimum(jnp.floor(jnp.log2(largest)) + 1.0, 126.0)
    root = jnp.sqrt(jnp.sqrt(absolute * jnp.exp2(-power)))
    code = jnp.floor(root * CODE + 0.5)
    code = jnp.where(filtered < 0.0, -code, code)
    unit_ref[:OUTS] = code[:OUTS].astype(jnp.int32).astype(jnp.int16)
    for copy in copies[2:]:
        copy.wait()
    row = lax.broadcasted_iota(jnp.int32, (AUX, count), 0)
    key = channel_ref[...].reshape(1, count) * PIECES + piece_ref[...].reshape(1, count)
    side = jnp.where(row < SPILL, code[OUTS:].astype(jnp.int32), 0)
    side = jnp.where(row == SCALE_ROW, power.astype(jnp.int32), side)
    side = jnp.where(row == KEY_ROW, key, side)
    side = jnp.where(row == SLOT_ROW, slot_ref[0], side)
    unit_ref[OUTS:] = side.astype(jnp.int16)
    out = pltpu.make_async_copy(unit_ref, unit_hbm, arrived.at[0])
    out.start()
    out.wait()


def halves(code):
    first = (code >> 8).astype(jnp.float32).astype(jnp.bfloat16)
    return first, (code & 255).astype(jnp.float32).astype(jnp.bfloat16)


def decoded(code, scale):
    root = code * (1.0 / CODE)
    return (root * root) * (root * jnp.abs(root)) * scale


def lag_products(white_ref, lags_ref, rows, first, number):
    f32 = jnp.float32
    total = jnp.zeros((number * CH_DEV, LAGS), f32)
    for tile in range(NF // LANES):
        re = slice(tile * LANES, (tile + 1) * LANES)
        im = slice(NF + tile * LANES, NF + (tile + 1) * LANES)
        zero = jnp.zeros((CH_DEV, LANES), f32)
        sums = [[zero, zero, zero] for _ in range(number)]
        for window in range(WIN_DEV):
            own = slice(window * rows, window * rows + CH_DEV)
            loc_real = white_ref[own, re]
            loc_imag = white_ref[own, im]
            less = loc_real - loc_imag
            more = loc_real + loc_imag
            for source in range(number):
                at = window * rows + CH_DEV + first + source
                src_real = jnp.broadcast_to(white_ref[at : at + 1, re], (CH_DEV, LANES))
                src_imag = jnp.broadcast_to(white_ref[at : at + 1, im], (CH_DEV, LANES))
                sums[source][0] += loc_real * (src_real + src_imag)
                sums[source][1] += less * src_imag
                sums[source][2] += more * src_real
        real_sums = [both - imag for both, imag, real in sums]
        imag_sums = [both - real for both, imag, real in sums]
        cross = jnp.concatenate(
            [
                jnp.concatenate(real_sums, axis=0).astype(jnp.bfloat16),
                jnp.concatenate(imag_sums, axis=0).astype(jnp.bfloat16),
            ],
            axis=1,
        )
        total += jnp.dot(
            cross,
            lags_ref[2 * tile * LANES : 2 * (tile + 1) * LANES],
            preferred_element_type=f32,
        )
    return total


def pick_rows(pick_ref, key, first, group, wanted):
    shape = (2 * group, key.shape[1])
    key = jnp.broadcast_to(key, shape)
    for pair in range(PIECES // 2):
        pick_ref[pair * 2 * group : (pair + 1) * 2 * group, first : first + shape[1]] = jnp.where(
            wanted + 2 * pair == key, 1.0, 0.0
        ).astype(jnp.bfloat16)


def wanted_own(me, count):
    row = lax.broadcasted_iota(jnp.int32, (2 * CH_DEV, count), 0)
    odd = (row >= CH_DEV).astype(jnp.int32)
    return (me * CH_DEV + row - odd * CH_DEV) * PIECES + odd


def selected(data, pick):
    return lax.dot_general(data, pick, (((1,), (1,)), ((), ())), preferred_element_type=jnp.float32)


def early_kernel(early_total, *refs):
    unit_hbm = refs[0]
    units_ref = refs[1:early_total]
    own_ref, data_ref, side_ref, pick_ref, unit_ref, arrived = refs[early_total:]
    copy = pltpu.make_async_copy(unit_hbm, unit_ref, arrived)
    copy.start()
    count = unit_ref.shape[1]
    wanted = wanted_own(lax.axis_index("chan"), count)

    def take(unit, number):
        at = slice(number * count, (number + 1) * count)
        codes = unit[...].astype(jnp.int32)
        first, second = halves(codes)
        data_ref[: OUTS + AUX, at] = first
        data_ref[OUTS + AUX :, at] = second
        side_ref[:, at] = codes[OUTS:]
        pick_rows(pick_ref, codes[OUTS + KEY_ROW : OUTS + KEY_ROW + 1], number * count, CH_DEV, wanted)

    for number in range(1, early_total):
        take(units_ref[number - 1], number)
    own_ref[...] = selected(data_ref[:, count:], pick_ref[:, count:])
    copy.wait()
    take(unit_ref, 0)
    own_ref[...] += selected(data_ref[:, :count], pick_ref[:, :count])


def samples_of(picked, group):
    code = picked[: OUTS + AUX] * 256.0 + picked[OUTS + AUX :]
    scale = jnp.exp2(code[OUTS + SCALE_ROW : OUTS + SCALE_ROW + 1])
    main_part = decoded(code[:OUTS], scale)
    spill_part = pltpu.roll(decoded(code[OUTS:], scale), group, 1)
    row = lax.broadcasted_iota(jnp.int32, spill_part.shape, 0)
    column = lax.broadcasted_iota(jnp.int32, spill_part.shape, 1)
    spill_part = jnp.where((row < SPILL) & (column >= group), spill_part, 0.0)
    return jnp.transpose(jnp.concatenate([main_part[:AUX] + spill_part, main_part[AUX:]], axis=0))


def correlate_kernel(block_total, span_total, *refs):
    f32 = jnp.float32
    own_ref, data_ref, side_ref, starts_hbm, slot_ref = refs[:5]
    refs = refs[5:]
    units_ref = dict(zip(LATE, refs))
    refs = refs[len(LATE) :]
    wide_ref, band_ref, lags_ref, send_ref, white_ref = refs[:5]
    pick_own_ref, pick_src_ref, dec_ref, seg_ref, starts_ref, arrived = refs[5:]
    copy = pltpu.make_async_copy(starts_hbm, starts_ref, arrived)
    copy.start()
    me = lax.axis_index("chan")
    half = lax.axis_index("win")
    rows = CH_DEV + block_total
    count = side_ref.shape[1] // len(EARLY)
    late = {step: unit[...].astype(jnp.int32) for step, unit in units_ref.items()}
    sides = {step: side_ref[:, n * count : (n + 1) * count] for n, step in enumerate(EARLY)}
    sides |= {step: codes[OUTS:] for step, codes in late.items()}
    row = lax.broadcasted_iota(jnp.int32, (2 * block_total, count), 0)
    odd = (row >= block_total).astype(jnp.int32)
    source = (row + (1 + half) * (block_total // span_total)) % block_total
    channel = source * CH_DEV + slot_ref[0]
    for step, side in sides.items():
        if step:
            slot = jnp.broadcast_to(side[SLOT_ROW : SLOT_ROW + 1], source.shape)
            channel = jnp.where(source == (me ^ step), source * CH_DEV + slot, channel)
    wanted = channel * PIECES + odd
    own = wanted_own(me, count)
    for number, step in enumerate(EARLY + LATE):
        key = sides[step][KEY_ROW : KEY_ROW + 1]
        pick_rows(pick_src_ref, key, number * count, block_total, wanted)
        if step in late:
            pick_rows(pick_own_ref, key, (number - len(EARLY)) * count, CH_DEV, own)
    codes = jnp.concatenate([late[step] for step in LATE], axis=1)
    late_data = jnp.concatenate(halves(codes), axis=0)
    split = len(EARLY) * count
    picked_src = selected(data_ref[...], pick_src_ref[:, :split])
    picked_src += selected(late_data, pick_src_ref[:, split:])
    picked_own = own_ref[...] + selected(late_data, pick_own_ref[...])
    samples = samples_of(picked_own, CH_DEV)
    sources = samples_of(picked_src, block_total)
    for piece in range(PIECES):
        at = slice(piece * OUTS, (piece + 1) * OUTS)
        dec_ref[:CH_DEV, at] = samples[piece * CH_DEV : (piece + 1) * CH_DEV]
        dec_ref[CH_DEV:, at] = sources[piece * block_total : (piece + 1) * block_total]
    dec_ref[:, SPAN:] = jnp.zeros((rows, LANES), f32)
    lane = lax.broadcasted_iota(jnp.int32, (rows, LANES), 1)
    extra = wide_ref[WL:].astype(f32)
    taper = extra[0:1] + extra[1:2] + extra[2:3]
    inverse = (extra[3:4] + extra[4:5] + extra[5:6])[:, :NF]
    copy.wait()
    for window in range(WIN_DEV):
        start = starts_ref[window]
        base = pl.multiple_of((start >> 7) * LANES, LANES)
        offset = start & (LANES - 1)
        shift = (LANES - offset) & (LANES - 1)
        chunks = [
            pltpu.roll(dec_ref[:, pl.ds(base + tile * LANES, LANES)], shift, 1)
            for tile in range(WL // LANES + 1)
        ]
        here = lane < LANES - offset
        for tile in range(WL // LANES):
            at = slice(tile * LANES, (tile + 1) * LANES)
            seg_ref[window * rows : (window + 1) * rows, at] = (
                jnp.where(here, chunks[tile], chunks[tile + 1]) * taper[:, at]
            )
    spectra = jnp.dot(
        seg_ref[...].astype(jnp.bfloat16), wide_ref[:WL], preferred_element_type=f32
    )
    real = spectra[:, :NF]
    imag = spectra[:, NF:]
    energy = real * real + imag * imag
    high = energy.astype(jnp.bfloat16)
    low = (energy - high.astype(f32)).astype(jnp.bfloat16)
    sums = jnp.dot(
        jnp.concatenate([high, low], axis=0), band_ref[...], preferred_element_type=f32
    )
    smooth = (sums[: energy.shape[0]] + sums[energy.shape[0] :]) * inverse
    scale = lax.rsqrt(smooth + EPSILON)
    white_ref[:, :NF] = (real * scale).astype(jnp.bfloat16).astype(f32)
    white_ref[:, NF:] = (imag * scale).astype(jnp.bfloat16).astype(f32)
    send_ref[...] = lag_products(white_ref, lags_ref, rows, 0, block_total // span_total)


def keep_kernel(rows, first, number, white_ref, lags_ref, keep_ref):
    keep_ref[...] = lag_products(white_ref, lags_ref, rows, first, number)


def gathered_body(records, record_channel, record_piece, fir_taps, window_starts, source_slot):
    block_total = lax.axis_size("chan")
    span_total = lax.axis_size("win")
    vmem = pl.BlockSpec(memory_space=pltpu.VMEM)
    smem = pl.BlockSpec(memory_space=pltpu.SMEM)
    hbm = pl.BlockSpec(memory_space=pl.ANY)
    count = records.shape[0]
    unit_shape = (OUTS + AUX, count)
    unit = pl.pallas_call(
        filter_kernel,
        out_shape=(
            jax.ShapeDtypeStruct(unit_shape, jnp.int16)
        ),
        in_specs=[hbm] * 5,
        out_specs=hbm,
        scratch_shapes=[
            pltpu.VMEM(records.shape, records.dtype),
            pltpu.VMEM(record_channel.shape, jnp.int32),
            pltpu.VMEM(record_piece.shape, jnp.int32),
            pltpu.VMEM(fir_taps.shape, fir_taps.dtype),
            pltpu.SMEM((1,), jnp.int32),
            pltpu.VMEM(unit_shape, jnp.int16),
            pltpu.SemaphoreType.DMA((5,)),
        ],
        compiler_params=pltpu.CompilerParams(vmem_limit_bytes=FILTER_VMEM),
        cost_estimate=pl.CostEstimate(flops=FLOPS, bytes_accessed=1 << 20, transcendentals=0),
        name="filter",
    )(records, record_channel, record_piece, fir_taps, source_slot)

    def swap(value, step):
        return lax.ppermute(value, "chan", [(i, i ^ step) for i in range(block_total)])

    units = {0: unit}
    for step, last in LAST_HOP.items():
        units[step] = swap(units[step ^ last], last)
    rows = CH_DEV + block_total
    half_rows = block_total // span_total * CH_DEV
    half_shape = jax.ShapeDtypeStruct((half_rows, LAGS), jnp.float32)
    tables = [wide_table(), band_table(), lag_table()]
    lags = jnp.asarray(tables[2])
    half_count = block_total // span_total
    data_shape = (2 * unit_shape[0], len(EARLY) * count)
    own, data, side = pl.pallas_call(
        lambda *refs: early_kernel(len(EARLY), *refs),
        out_shape=(
            jax.ShapeDtypeStruct((2 * unit_shape[0], PIECES * CH_DEV), jnp.float32),
            jax.ShapeDtypeStruct(data_shape, jnp.bfloat16),
            jax.ShapeDtypeStruct((AUX, len(EARLY) * count), jnp.int32),
        ),
        in_specs=[hbm] + [vmem] * (len(EARLY) - 1),
        out_specs=(vmem, vmem, vmem),
        scratch_shapes=[
            pltpu.VMEM((PIECES * CH_DEV, len(EARLY) * count), jnp.bfloat16),
            pltpu.VMEM(unit_shape, jnp.int16),
            pltpu.SemaphoreType.DMA,
        ],
        compiler_params=pltpu.CompilerParams(vmem_limit_bytes=EARLY_VMEM),
        cost_estimate=pl.CostEstimate(flops=EARLY_FLOPS, bytes_accessed=1 << 20, transcendentals=0),
        name="early",
    )(unit, *[units[step] for step in EARLY[1:]])
    send, white = pl.pallas_call(
        lambda *refs: correlate_kernel(block_total, span_total, *refs),
        out_shape=(half_shape, jax.ShapeDtypeStruct((WIN_DEV * rows, WL), jnp.float32)),
        in_specs=[vmem, vmem, vmem, hbm, smem] + [vmem] * (len(LATE) + 3),
        out_specs=(vmem, vmem),
        scratch_shapes=[
            pltpu.VMEM((PIECES * CH_DEV, len(LATE) * count), jnp.bfloat16),
            pltpu.VMEM((PIECES * block_total, block_total * count), jnp.bfloat16),
            pltpu.VMEM((rows, SPAN + LANES), jnp.float32),
            pltpu.VMEM((WIN_DEV * rows, WL), jnp.float32),
            pltpu.SMEM((WIN_DEV,), jnp.int32),
            pltpu.SemaphoreType.DMA,
        ],
        compiler_params=pltpu.CompilerParams(vmem_limit_bytes=CORRELATE_VMEM),
        name="correlate",
    )(
        own,
        data,
        side,
        window_starts,
        source_slot,
        *[units[step] for step in LATE],
        *[jnp.asarray(table) for table in tables[:2]],
        lags,
    )
    other = lax.ppermute(send, "win", [(i, i ^ 1) for i in range(span_total)])
    keep = pl.pallas_call(
        lambda *refs: keep_kernel(rows, half_count, half_count, *refs),
        out_shape=half_shape,
        in_specs=[vmem, vmem],
        out_specs=vmem,
        compiler_params=pltpu.CompilerParams(vmem_limit_bytes=32 << 20),
        name="keep",
    )(white, lags)
    return (keep + other).reshape(block_total // span_total, CH_DEV, LAGS)


def make_filter(fir_taps):
    outputs_per = SEG // DEC
    sample_index = jnp.arange(SEG, dtype=jnp.int32)[:, None]
    column_index = jnp.arange(outputs_per + SPILL, dtype=jnp.int32)[None, :]
    tap_index = jnp.where(
        column_index < outputs_per,
        DEC * column_index + DEC - 1 - sample_index,
        DEC * (column_index - outputs_per) + DEC - 1 + SEG - sample_index,
    )
    match_table = (
        tap_index[:, :, None] == jnp.arange(TAPS, dtype=jnp.int32)[None, None, :]
    ).astype(jnp.float32)
    return jnp.sum(match_table * fir_taps.astype(jnp.float32)[None, None, :], axis=2).astype(
        jnp.bfloat16
    )


def make_fourier():
    sample_index = jnp.arange(WL, dtype=jnp.int32)[:, None]
    freq_index = jnp.arange(NF, dtype=jnp.int32)[None, :]
    phase = 2.0 * math.pi * (sample_index * freq_index % WL).astype(jnp.float32) / WL
    return jnp.concatenate([jnp.cos(phase), -jnp.sin(phase)], axis=1).astype(jnp.bfloat16)


def make_taper():
    sample_index = jnp.arange(WL, dtype=jnp.int32).astype(jnp.float32)
    return 0.5 - 0.5 * jnp.cos(2.0 * math.pi * sample_index / WL)


def make_lags():
    freq_index = jnp.arange(NF, dtype=jnp.int32)[:, None]
    lag_index = jnp.arange(LAGS, dtype=jnp.int32)[None, :] - LAGS // 2
    phase = 2.0 * math.pi * (freq_index * lag_index % WL).astype(jnp.float32) / WL
    scale = 1.0 / math.sqrt(WL * WIN_DEV)
    return (jnp.concatenate([jnp.cos(phase), -jnp.sin(phase)], axis=0) * scale).astype(jnp.bfloat16)


def whiten(spectra):
    freq_index = jnp.arange(NF, dtype=jnp.int32)
    band_table = (jnp.abs(freq_index[:, None] - freq_index[None, :]) <= BAND).astype(jnp.float32)
    band_count = jnp.sum(band_table, axis=0)
    real_part = spectra[..., :NF]
    imag_part = spectra[..., NF:]
    energy = real_part * real_part + imag_part * imag_part
    smooth = jnp.dot(energy, band_table, precision=lax.Precision.HIGHEST) / band_count[None, :]
    amplitude = jnp.sqrt(smooth + EPSILON)
    return (spectra / jnp.concatenate([amplitude, amplitude], axis=-1)).astype(jnp.bfloat16)


def cross_spectrum(source_block, local_block):
    src_real = source_block[..., :NF]
    src_imag = source_block[..., NF:]
    loc_real = local_block[..., :NF]
    loc_imag = local_block[..., NF:]
    real_sum = jnp.einsum(
        "bwf,cwf->bcf", src_real, loc_real, preferred_element_type=jnp.float32
    ) + jnp.einsum("bwf,cwf->bcf", src_imag, loc_imag, preferred_element_type=jnp.float32)
    imag_sum = jnp.einsum(
        "bwf,cwf->bcf", src_imag, loc_real, preferred_element_type=jnp.float32
    ) - jnp.einsum("bwf,cwf->bcf", src_real, loc_imag, preferred_element_type=jnp.float32)
    return jnp.concatenate([real_sum, imag_sum], axis=-1).astype(jnp.bfloat16)


def over_blocks(block_fn, sources, channel_count):
    source_count = sources.shape[0]
    block_size = math.gcd(source_count, 16)
    block_count = source_count // block_size
    grouped = sources.reshape((block_count, block_size) + sources.shape[1:])
    return lax.map(block_fn, grouped).reshape(source_count, channel_count, LAGS)


def routed_body(records, record_channel, record_piece, fir_taps, window_starts, source_slot):
    block_total = lax.axis_size("chan")
    per_device = records.shape[0]
    capacity = 2 * per_device // block_total
    outputs_per = SEG // DEC
    owner_block = record_channel // CH_DEV
    local_slot = record_channel % CH_DEV * PIECES + record_piece
    one_hot = (owner_block[:, None] == jnp.arange(block_total, dtype=jnp.int32)[None, :]).astype(
        jnp.int32
    )
    earlier_count = jnp.sum((jnp.cumsum(one_hot, axis=0) - one_hot) * one_hot, axis=1)
    position = owner_block * capacity + earlier_count
    slot_table = (
        jnp.full((block_total * capacity,), -1, jnp.int32)
        .at[position]
        .set(local_slot)
        .reshape(block_total, capacity)
    )
    filter_matrix = make_filter(fir_taps)
    row_send = (
        jnp.zeros((block_total * capacity, SEG), jnp.bfloat16)
        .at[position]
        .set(records)
        .reshape(block_total, capacity, SEG)
    )
    rows_got, slots_got = (
        lax.all_to_all(row_send, "chan", split_axis=0, concat_axis=0, tiled=True),
        lax.all_to_all(slot_table, "chan", split_axis=0, concat_axis=0, tiled=True),
    )
    flat_slots = slots_got.reshape(-1)
    target = jnp.where(flat_slots >= 0, flat_slots, per_device)
    traces = (
        jnp.zeros((per_device, SEG), jnp.bfloat16)
        .at[target]
        .set(rows_got.reshape(-1, SEG), mode="drop")
    )
    filtered = jnp.dot(traces, filter_matrix, preferred_element_type=jnp.float32)
    main_part = filtered[:, :outputs_per]
    spill_part = filtered[:, outputs_per:]
    main_part = main_part.reshape(CH_DEV, PIECES, outputs_per)
    spill_part = spill_part.reshape(CH_DEV, PIECES, SPILL)
    carried = jnp.pad(spill_part[:, :-1, :], ((0, 0), (1, 0), (0, outputs_per - SPILL)))
    decimated = (main_part + carried).reshape(CH_DEV, SPAN)

    def window_cut(window_start):
        return lax.dynamic_slice_in_dim(decimated, window_start, WL, 1)

    segments = (jax.vmap(window_cut, out_axes=1)(window_starts) * make_taper()).astype(jnp.bfloat16)
    window_count = segments.shape[1]
    spectra = jnp.dot(segments.reshape(-1, WL), make_fourier(), preferred_element_type=jnp.float32)
    whitened = whiten(spectra).reshape(CH_DEV, window_count, WL)
    source = lax.dynamic_slice_in_dim(whitened, source_slot[0], 1, 0)
    gathered = lax.all_gather(source, "chan", axis=0, tiled=True)
    lag_table = make_lags()

    def span_block(source_block):
        cross_spectra = cross_spectrum(source_block, whitened)
        return jnp.dot(
            cross_spectra.reshape(-1, WL), lag_table, preferred_element_type=jnp.float32
        ).reshape(source_block.shape[0], CH_DEV, LAGS)

    return lax.psum_scatter(
        over_blocks(span_block, gathered, CH_DEV), "win", scatter_dimension=0, tiled=True
    )


def solution(mesh):
    in_specs = (
        P(("groups", "chan", "win"), None),
        P(("groups", "chan", "win")),
        P(("groups", "chan", "win")),
        P(),
        P(("groups", "win")),
        P(("groups", "chan")),
    )
    out_specs = P(("groups", "win"), "chan", None)
    body = gathered_body if mesh.shape["chan"] == 8 else routed_body
    return jax.shard_map(body, mesh=mesh, in_specs=in_specs, out_specs=out_specs, check_vma=False)
```

```python
import math

import jax
import jax.numpy as jnp
import ml_dtypes
import numpy as np
from jax import lax
from jax.experimental import pallas as pl
from jax.experimental.pallas import tpu as pltpu
from jax.sharding import PartitionSpec as P

CH_DEV = 16
SPAN = 2048
WIN_DEV = 8
WL = 1024
NF = 512
DEC = 4
TAPS = 32
SPILL = 7
SEG = 512
PIECES = 16
BAND = 64
LAGS = 256


EPSILON = 1e-06

LANES = 128
OUTS = SEG // DEC
AUX = 16
SCALE_ROW = SPILL
KEY_ROW = SPILL + 1
SLOT_ROW = SPILL + 2
FILTER_VMEM = 56 << 20
FLOPS = 10**10
EARLY_VMEM = 44 << 20
EARLY_FLOPS = 10**9
CORRELATE_VMEM = 40 << 20
LOCAL_ROWS = 32768
LAST_HOP = {1: 1, 2: 2, 3: 3, 4: 4, 6: 6, 5: 1, 7: 3}
EARLY = (0, 2, 1, 4)
LATE = (6, 5, 3, 7)
CODE = 23000.0


def fourier_table():
    sample_index = np.arange(WL)[:, None]
    freq_index = np.arange(NF)[None, :]
    phase = 2.0 * np.pi * (sample_index * freq_index % WL) / WL
    return np.concatenate([np.cos(phase), -np.sin(phase)], axis=1).astype(ml_dtypes.bfloat16)


def lag_table():
    freq_index = np.arange(NF)[:, None]
    lag_index = np.arange(LAGS)[None, :] - LAGS // 2
    phase = 2.0 * np.pi * (freq_index * lag_index % WL) / WL
    scale = 1.0 / math.sqrt(WL * WIN_DEV)
    tiles = (NF // LANES, 1, LANES, LAGS)
    parts = [np.cos(phase).reshape(tiles), -np.sin(phase).reshape(tiles)]
    return (np.concatenate(parts, axis=1).reshape(2 * NF, LAGS) * scale).astype(ml_dtypes.bfloat16)


def band_table():
    freq_index = np.arange(NF)
    return (np.abs(freq_index[:, None] - freq_index[None, :]) <= BAND).astype(ml_dtypes.bfloat16)


def split_rows(row):
    rows = []
    for _ in range(3):
        rows.append(row.astype(ml_dtypes.bfloat16))
        row = row - rows[-1].astype(np.float32)
    return rows


def wide_table():
    freq_index = np.arange(NF)
    band = np.abs(freq_index[:, None] - freq_index[None, :]) <= BAND
    taper = (0.5 - 0.5 * np.cos(2.0 * np.pi * np.arange(WL) / WL)).astype(np.float32)
    inverse = np.zeros(WL, np.float32)
    inverse[:NF] = 1.0 / band.sum(axis=0)
    empty = [np.zeros(WL, ml_dtypes.bfloat16)] * 10
    rows = np.stack(split_rows(taper) + split_rows(inverse) + empty)
    return np.concatenate([fourier_table(), rows], axis=0)


def filter_kernel(
    records_hbm, channel_hbm, piece_hbm, taps_hbm, slot_hbm, unit_hbm, *scratch
):
    records_ref, channel_ref, piece_ref, taps_ref, slot_ref, unit_ref, arrived = scratch
    f32 = jnp.float32
    count = records_ref.shape[0]
    pairs = (
        (taps_hbm, taps_ref),
        (records_hbm, records_ref),
        (channel_hbm, channel_ref),
        (piece_hbm, piece_ref),
        (slot_hbm, slot_ref),
    )
    copies = [
        pltpu.make_async_copy(source, target, arrived.at[number])
        for number, (source, target) in enumerate(pairs)
    ]
    for copy in copies:
        copy.start()
    tap = lax.broadcasted_iota(jnp.int32, (TAPS, SEG), 0)
    sample = lax.broadcasted_iota(jnp.int32, (TAPS, SEG), 1)
    place = (((DEC - 1 - tap) & (SEG - 1)) == sample).astype(f32).astype(jnp.bfloat16)
    copies[0].wait()
    taps = jnp.broadcast_to(taps_ref[...].reshape(1, TAPS), (16, TAPS))
    first = jnp.dot(taps, place, preferred_element_type=f32)
    circulant = pltpu.roll(
        jnp.broadcast_to(first[0:1], (OUTS, SEG)), 0, 1, stride=DEC, stride_axis=0
    )
    output = lax.broadcasted_iota(jnp.int32, (OUTS, SEG), 0)
    sample = lax.broadcasted_iota(jnp.int32, (OUTS, SEG), 1)
    inside = sample <= DEC * output + DEC - 1
    main_filter = jnp.where(inside, circulant, 0.0)
    spill_filter = jnp.where(inside, 0.0, circulant)[:AUX]
    filters = jnp.concatenate([main_filter, spill_filter], axis=0).astype(jnp.bfloat16)
    copies[1].wait()
    filtered = lax.dot_general(
        filters, records_ref[...], (((1,), (1,)), ((), ())), preferred_element_type=f32
    )
    absolute = jnp.abs(filtered)
    largest = jnp.maximum(jnp.max(absolute, axis=0, keepdims=True), 1e-30)
    power = jnp.minimum(jnp.floor(jnp.log2(largest)) + 1.0, 126.0)
    root = jnp.sqrt(jnp.sqrt(absolute * jnp.exp2(-power)))
    code = jnp.floor(root * CODE + 0.5)
    code = jnp.where(filtered < 0.0, -code, code)
    unit_ref[:OUTS] = code[:OUTS].astype(jnp.int32).astype(jnp.int16)
    for copy in copies[2:]:
        copy.wait()
    row = lax.broadcasted_iota(jnp.int32, (AUX, count), 0)
    key = channel_ref[...].reshape(1, count) * PIECES + piece_ref[...].reshape(1, count)
    side = jnp.where(row < SPILL, code[OUTS:].astype(jnp.int32), 0)
    side = jnp.where(row == SCALE_ROW, power.astype(jnp.int32), side)
    side = jnp.where(row == KEY_ROW, key, side)
    side = jnp.where(row == SLOT_ROW, slot_ref[0], side)
    unit_ref[OUTS:] = side.astype(jnp.int16)
    out = pltpu.make_async_copy(unit_ref, unit_hbm, arrived.at[0])
    out.start()
    out.wait()


def halves(code):
    first = (code >> 8).astype(jnp.float32).astype(jnp.bfloat16)
    return first, (code & 255).astype(jnp.float32).astype(jnp.bfloat16)


def decoded(code, scale):
    root = code * (1.0 / CODE)
    return (root * root) * (root * jnp.abs(root)) * scale


def lag_products(white_ref, lags_ref, rows, first, number):
    f32 = jnp.float32
    total = jnp.zeros((number * CH_DEV, LAGS), f32)
    for tile in range(NF // LANES):
        re = slice(tile * LANES, (tile + 1) * LANES)
        im = slice(NF + tile * LANES, NF + (tile + 1) * LANES)
        zero = jnp.zeros((CH_DEV, LANES), f32)
        sums = [[zero, zero, zero] for _ in range(number)]
        for window in range(WIN_DEV):
            own = slice(window * rows, window * rows + CH_DEV)
            loc_real = white_ref[own, re]
            loc_imag = white_ref[own, im]
            less = loc_real - loc_imag
            more = loc_real + loc_imag
            for source in range(number):
                at = window * rows + CH_DEV + first + source
                src_real = jnp.broadcast_to(white_ref[at : at + 1, re], (CH_DEV, LANES))
                src_imag = jnp.broadcast_to(white_ref[at : at + 1, im], (CH_DEV, LANES))
                sums[source][0] += loc_real * (src_real + src_imag)
                sums[source][1] += less * src_imag
                sums[source][2] += more * src_real
        real_sums = [both - imag for both, imag, real in sums]
        imag_sums = [both - real for both, imag, real in sums]
        cross = jnp.concatenate(
            [
                jnp.concatenate(real_sums, axis=0).astype(jnp.bfloat16),
                jnp.concatenate(imag_sums, axis=0).astype(jnp.bfloat16),
            ],
            axis=1,
        )
        total += jnp.dot(
            cross,
            lags_ref[2 * tile * LANES : 2 * (tile + 1) * LANES],
            preferred_element_type=f32,
        )
    return total


def pick_rows(pick_ref, key, first, group, wanted):
    shape = (2 * group, key.shape[1])
    key = jnp.broadcast_to(key, shape)
    for pair in range(PIECES // 2):
        pick_ref[pair * 2 * group : (pair + 1) * 2 * group, first : first + shape[1]] = jnp.where(
            wanted + 2 * pair == key, 1.0, 0.0
        ).astype(jnp.bfloat16)


def wanted_own(me, count):
    row = lax.broadcasted_iota(jnp.int32, (2 * CH_DEV, count), 0)
    odd = (row >= CH_DEV).astype(jnp.int32)
    return (me * CH_DEV + row - odd * CH_DEV) * PIECES + odd


def selected(data, pick):
    return lax.dot_general(data, pick, (((1,), (1,)), ((), ())), preferred_element_type=jnp.float32)


def early_kernel(early_total, *refs):
    unit_hbm = refs[0]
    units_ref = refs[1:early_total]
    own_ref, data_ref, side_ref, pick_ref, unit_ref, arrived = refs[early_total:]
    copy = pltpu.make_async_copy(unit_hbm, unit_ref, arrived)
    copy.start()
    count = unit_ref.shape[1]
    wanted = wanted_own(lax.axis_index("chan"), count)

    def take(unit, number):
        at = slice(number * count, (number + 1) * count)
        codes = unit[...].astype(jnp.int32)
        first, second = halves(codes)
        data_ref[: OUTS + AUX, at] = first
        data_ref[OUTS + AUX :, at] = second
        side_ref[:, at] = codes[OUTS:]
        pick_rows(pick_ref, codes[OUTS + KEY_ROW : OUTS + KEY_ROW + 1], number * count, CH_DEV, wanted)

    for number in range(1, early_total):
        take(units_ref[number - 1], number)
    own_ref[...] = selected(data_ref[:, count:], pick_ref[:, count:])
    copy.wait()
    take(unit_ref, 0)
    own_ref[...] += selected(data_ref[:, :count], pick_ref[:, :count])


def samples_of(picked, group):
    code = picked[: OUTS + AUX] * 256.0 + picked[OUTS + AUX :]
    scale = jnp.exp2(code[OUTS + SCALE_ROW : OUTS + SCALE_ROW + 1])
    main_part = decoded(code[:OUTS], scale)
    spill_part = pltpu.roll(decoded(code[OUTS:], scale), group, 1)
    row = lax.broadcasted_iota(jnp.int32, spill_part.shape, 0)
    column = lax.broadcasted_iota(jnp.int32, spill_part.shape, 1)
    spill_part = jnp.where((row < SPILL) & (column >= group), spill_part, 0.0)
    return jnp.transpose(jnp.concatenate([main_part[:AUX] + spill_part, main_part[AUX:]], axis=0))


def correlate_kernel(block_total, span_total, *refs):
    f32 = jnp.float32
    own_ref, data_ref, side_ref, starts_hbm, slot_ref = refs[:5]
    refs = refs[5:]
    units_ref = dict(zip(LATE, refs))
    refs = refs[len(LATE) :]
    wide_ref, band_ref, lags_ref, send_ref, white_ref = refs[:5]
    pick_own_ref, pick_src_ref, dec_ref, seg_ref, starts_ref, arrived = refs[5:]
    copy = pltpu.make_async_copy(starts_hbm, starts_ref, arrived)
    copy.start()
    me = lax.axis_index("chan")
    half = lax.axis_index("win")
    rows = CH_DEV + block_total
    count = side_ref.shape[1] // len(EARLY)
    late = {step: unit[...].astype(jnp.int32) for step, unit in units_ref.items()}
    sides = {step: side_ref[:, n * count : (n + 1) * count] for n, step in enumerate(EARLY)}
    sides |= {step: codes[OUTS:] for step, codes in late.items()}
    row = lax.broadcasted_iota(jnp.int32, (2 * block_total, count), 0)
    odd = (row >= block_total).astype(jnp.int32)
    source = (row + (1 + half) * (block_total // span_total)) % block_total
    channel = source * CH_DEV + slot_ref[0]
    for step, side in sides.items():
        if step:
            slot = jnp.broadcast_to(side[SLOT_ROW : SLOT_ROW + 1], source.shape)
            channel = jnp.where(source == (me ^ step), source * CH_DEV + slot, channel)
    wanted = channel * PIECES + odd
    own = wanted_own(me, count)
    for number, step in enumerate(EARLY + LATE):
        key = sides[step][KEY_ROW : KEY_ROW + 1]
        pick_rows(pick_src_ref, key, number * count, block_total, wanted)
        if step in late:
            pick_rows(pick_own_ref, key, (number - len(EARLY)) * count, CH_DEV, own)
    codes = jnp.concatenate([late[step] for step in LATE], axis=1)
    late_data = jnp.concatenate(halves(codes), axis=0)
    split = len(EARLY) * count
    picked_src = selected(data_ref[...], pick_src_ref[:, :split])
    picked_src += selected(late_data, pick_src_ref[:, split:])
    picked_own = own_ref[...] + selected(late_data, pick_own_ref[...])
    samples = samples_of(picked_own, CH_DEV)
    sources = samples_of(picked_src, block_total)
    for piece in range(PIECES):
        at = slice(piece * OUTS, (piece + 1) * OUTS)
        dec_ref[:CH_DEV, at] = samples[piece * CH_DEV : (piece + 1) * CH_DEV]
        dec_ref[CH_DEV:, at] = sources[piece * block_total : (piece + 1) * block_total]
    dec_ref[:, SPAN:] = jnp.zeros((rows, LANES), f32)
    lane = lax.broadcasted_iota(jnp.int32, (rows, LANES), 1)
    extra = wide_ref[WL:].astype(f32)
    taper = extra[0:1] + extra[1:2] + extra[2:3]
    inverse = (extra[3:4] + extra[4:5] + extra[5:6])[:, :NF]
    copy.wait()
    for window in range(WIN_DEV):
        start = starts_ref[window]
        base = pl.multiple_of((start >> 7) * LANES, LANES)
        offset = start & (LANES - 1)
        shift = (LANES - offset) & (LANES - 1)
        chunks = [
            pltpu.roll(dec_ref[:, pl.ds(base + tile * LANES, LANES)], shift, 1)
            for tile in range(WL // LANES + 1)
        ]
        here = lane < LANES - offset
        for tile in range(WL // LANES):
            at = slice(tile * LANES, (tile + 1) * LANES)
            seg_ref[window * rows : (window + 1) * rows, at] = (
                jnp.where(here, chunks[tile], chunks[tile + 1]) * taper[:, at]
            )
    spectra = jnp.dot(
        seg_ref[...].astype(jnp.bfloat16), wide_ref[:WL], preferred_element_type=f32
    )
    real = spectra[:, :NF]
    imag = spectra[:, NF:]
    energy = real * real + imag * imag
    high = energy.astype(jnp.bfloat16)
    low = (energy - high.astype(f32)).astype(jnp.bfloat16)
    sums = jnp.dot(
        jnp.concatenate([high, low], axis=0), band_ref[...], preferred_element_type=f32
    )
    smooth = (sums[: energy.shape[0]] + sums[energy.shape[0] :]) * inverse
    scale = lax.rsqrt(smooth + EPSILON)
    white_ref[:, :NF] = (real * scale).astype(jnp.bfloat16).astype(f32)
    white_ref[:, NF:] = (imag * scale).astype(jnp.bfloat16).astype(f32)
    send_ref[...] = lag_products(white_ref, lags_ref, rows, 0, block_total // span_total)


def keep_kernel(rows, first, number, white_ref, lags_ref, keep_ref):
    keep_ref[...] = lag_products(white_ref, lags_ref, rows, first, number)


def gathered_body(records, record_channel, record_piece, fir_taps, window_starts, source_slot):
    block_total = lax.axis_size("chan")
    span_total = lax.axis_size("win")
    vmem = pl.BlockSpec(memory_space=pltpu.VMEM)
    smem = pl.BlockSpec(memory_space=pltpu.SMEM)
    hbm = pl.BlockSpec(memory_space=pl.ANY)
    count = records.shape[0]
    unit_shape = (OUTS + AUX, count)
    unit = pl.pallas_call(
        filter_kernel,
        out_shape=(
            jax.ShapeDtypeStruct(unit_shape, jnp.int16)
        ),
        in_specs=[hbm] * 5,
        out_specs=hbm,
        scratch_shapes=[
            pltpu.VMEM(records.shape, records.dtype),
            pltpu.VMEM(record_channel.shape, jnp.int32),
            pltpu.VMEM(record_piece.shape, jnp.int32),
            pltpu.VMEM(fir_taps.shape, fir_taps.dtype),
            pltpu.SMEM((1,), jnp.int32),
            pltpu.VMEM(unit_shape, jnp.int16),
            pltpu.SemaphoreType.DMA((5,)),
        ],
        compiler_params=pltpu.CompilerParams(vmem_limit_bytes=FILTER_VMEM),
        cost_estimate=pl.CostEstimate(flops=FLOPS, bytes_accessed=1 << 20, transcendentals=0),
        name="filter",
    )(records, record_channel, record_piece, fir_taps, source_slot)

    def swap(value, step):
        return lax.ppermute(value, "chan", [(i, i ^ step) for i in range(block_total)])

    units = {0: unit}
    for step, last in LAST_HOP.items():
        units[step] = swap(units[step ^ last], last)
    rows = CH_DEV + block_total
    half_rows = block_total // span_total * CH_DEV
    half_shape = jax.ShapeDtypeStruct((half_rows, LAGS), jnp.float32)
    tables = [wide_table(), band_table(), lag_table()]
    lags = jnp.asarray(tables[2])
    half_count = block_total // span_total
    data_shape = (2 * unit_shape[0], len(EARLY) * count)
    own, data, side = pl.pallas_call(
        lambda *refs: early_kernel(len(EARLY), *refs),
        out_shape=(
            jax.ShapeDtypeStruct((2 * unit_shape[0], PIECES * CH_DEV), jnp.float32),
            jax.ShapeDtypeStruct(data_shape, jnp.bfloat16),
            jax.ShapeDtypeStruct((AUX, len(EARLY) * count), jnp.int32),
        ),
        in_specs=[hbm] + [vmem] * (len(EARLY) - 1),
        out_specs=(vmem, vmem, vmem),
        scratch_shapes=[
            pltpu.VMEM((PIECES * CH_DEV, len(EARLY) * count), jnp.bfloat16),
            pltpu.VMEM(unit_shape, jnp.int16),
            pltpu.SemaphoreType.DMA,
        ],
        compiler_params=pltpu.CompilerParams(vmem_limit_bytes=EARLY_VMEM),
        cost_estimate=pl.CostEstimate(flops=EARLY_FLOPS, bytes_accessed=1 << 20, transcendentals=0),
        name="early",
    )(unit, *[units[step] for step in EARLY[1:]])
    send, white = pl.pallas_call(
        lambda *refs: correlate_kernel(block_total, span_total, *refs),
        out_shape=(half_shape, jax.ShapeDtypeStruct((WIN_DEV * rows, WL), jnp.float32)),
        in_specs=[vmem, vmem, vmem, hbm, smem] + [vmem] * (len(LATE) + 3),
        out_specs=(vmem, vmem),
        scratch_shapes=[
            pltpu.VMEM((PIECES * CH_DEV, len(LATE) * count), jnp.bfloat16),
            pltpu.VMEM((PIECES * block_total, block_total * count), jnp.bfloat16),
            pltpu.VMEM((rows, SPAN + LANES), jnp.float32),
            pltpu.VMEM((WIN_DEV * rows, WL), jnp.float32),
            pltpu.SMEM((WIN_DEV,), jnp.int32),
            pltpu.SemaphoreType.DMA,
        ],
        compiler_params=pltpu.CompilerParams(vmem_limit_bytes=CORRELATE_VMEM),
        name="correlate",
    )(
        own,
        data,
        side,
        window_starts,
        source_slot,
        *[units[step] for step in LATE],
        *[jnp.asarray(table) for table in tables[:2]],
        lags,
    )
    other = lax.ppermute(send, "win", [(i, i ^ 1) for i in range(span_total)])
    keep = pl.pallas_call(
        lambda *refs: keep_kernel(rows, half_count, half_count, *refs),
        out_shape=half_shape,
        in_specs=[vmem, vmem],
        out_specs=vmem,
        compiler_params=pltpu.CompilerParams(vmem_limit_bytes=32 << 20),
        name="keep",
    )(white, lags)
    return (keep + other).reshape(block_total // span_total, CH_DEV, LAGS)


def make_filter(fir_taps):
    outputs_per = SEG // DEC
    sample_index = jnp.arange(SEG, dtype=jnp.int32)[:, None]
    column_index = jnp.arange(outputs_per + SPILL, dtype=jnp.int32)[None, :]
    tap_index = jnp.where(
        column_index < outputs_per,
        DEC * column_index + DEC - 1 - sample_index,
        DEC * (column_index - outputs_per) + DEC - 1 + SEG - sample_index,
    )
    match_table = (
        tap_index[:, :, None] == jnp.arange(TAPS, dtype=jnp.int32)[None, None, :]
    ).astype(jnp.float32)
    return jnp.sum(match_table * fir_taps.astype(jnp.float32)[None, None, :], axis=2).astype(
        jnp.bfloat16
    )


def make_fourier():
    sample_index = jnp.arange(WL, dtype=jnp.int32)[:, None]
    freq_index = jnp.arange(NF, dtype=jnp.int32)[None, :]
    phase = 2.0 * math.pi * (sample_index * freq_index % WL).astype(jnp.float32) / WL
    return jnp.concatenate([jnp.cos(phase), -jnp.sin(phase)], axis=1).astype(jnp.bfloat16)


def make_taper():
    sample_index = jnp.arange(WL, dtype=jnp.int32).astype(jnp.float32)
    return 0.5 - 0.5 * jnp.cos(2.0 * math.pi * sample_index / WL)


def make_lags():
    freq_index = jnp.arange(NF, dtype=jnp.int32)[:, None]
    lag_index = jnp.arange(LAGS, dtype=jnp.int32)[None, :] - LAGS // 2
    phase = 2.0 * math.pi * (freq_index * lag_index % WL).astype(jnp.float32) / WL
    scale = 1.0 / math.sqrt(WL * WIN_DEV)
    return (jnp.concatenate([jnp.cos(phase), -jnp.sin(phase)], axis=0) * scale).astype(jnp.bfloat16)


def whiten(spectra):
    freq_index = jnp.arange(NF, dtype=jnp.int32)
    band_table = (jnp.abs(freq_index[:, None] - freq_index[None, :]) <= BAND).astype(jnp.float32)
    band_count = jnp.sum(band_table, axis=0)
    real_part = spectra[..., :NF]
    imag_part = spectra[..., NF:]
    energy = real_part * real_part + imag_part * imag_part
    smooth = jnp.dot(energy, band_table, precision=lax.Precision.HIGHEST) / band_count[None, :]
    amplitude = jnp.sqrt(smooth + EPSILON)
    return (spectra / jnp.concatenate([amplitude, amplitude], axis=-1)).astype(jnp.bfloat16)


def cross_spectrum(source_block, local_block):
    src_real = source_block[..., :NF]
    src_imag = source_block[..., NF:]
    loc_real = local_block[..., :NF]
    loc_imag = local_block[..., NF:]
    real_sum = jnp.einsum(
        "bwf,cwf->bcf", src_real, loc_real, preferred_element_type=jnp.float32
    ) + jnp.einsum("bwf,cwf->bcf", src_imag, loc_imag, preferred_element_type=jnp.float32)
    imag_sum = jnp.einsum(
        "bwf,cwf->bcf", src_imag, loc_real, preferred_element_type=jnp.float32
    ) - jnp.einsum("bwf,cwf->bcf", src_real, loc_imag, preferred_element_type=jnp.float32)
    return jnp.concatenate([real_sum, imag_sum], axis=-1).astype(jnp.bfloat16)


def over_blocks(block_fn, sources, channel_count):
    source_count = sources.shape[0]
    block_size = math.gcd(source_count, 16)
    block_count = source_count // block_size
    grouped = sources.reshape((block_count, block_size) + sources.shape[1:])
    return lax.map(block_fn, grouped).reshape(source_count, channel_count, LAGS)


def routed_body(records, record_channel, record_piece, fir_taps, window_starts, source_slot):
    block_total = lax.axis_size("chan")
    per_device = records.shape[0]
    capacity = 2 * per_device // block_total
    outputs_per = SEG // DEC
    owner_block = record_channel // CH_DEV
    local_slot = record_channel % CH_DEV * PIECES + record_piece
    one_hot = (owner_block[:, None] == jnp.arange(block_total, dtype=jnp.int32)[None, :]).astype(
        jnp.int32
    )
    earlier_count = jnp.sum((jnp.cumsum(one_hot, axis=0) - one_hot) * one_hot, axis=1)
    position = owner_block * capacity + earlier_count
    slot_table = (
        jnp.full((block_total * capacity,), -1, jnp.int32)
        .at[position]
        .set(local_slot)
        .reshape(block_total, capacity)
    )
    filter_matrix = make_filter(fir_taps)
    row_send = (
        jnp.zeros((block_total * capacity, SEG), jnp.bfloat16)
        .at[position]
        .set(records)
        .reshape(block_total, capacity, SEG)
    )
    rows_got, slots_got = (
        lax.all_to_all(row_send, "chan", split_axis=0, concat_axis=0, tiled=True),
        lax.all_to_all(slot_table, "chan", split_axis=0, concat_axis=0, tiled=True),
    )
    flat_slots = slots_got.reshape(-1)
    target = jnp.where(flat_slots >= 0, flat_slots, per_device)
    traces = (
        jnp.zeros((per_device, SEG), jnp.bfloat16)
        .at[target]
        .set(rows_got.reshape(-1, SEG), mode="drop")
    )
    filtered = jnp.dot(traces, filter_matrix, preferred_element_type=jnp.float32)
    main_part = filtered[:, :outputs_per]
    spill_part = filtered[:, outputs_per:]
    main_part = main_part.reshape(CH_DEV, PIECES, outputs_per)
    spill_part = spill_part.reshape(CH_DEV, PIECES, SPILL)
    carried = jnp.pad(spill_part[:, :-1, :], ((0, 0), (1, 0), (0, outputs_per - SPILL)))
    decimated = (main_part + carried).reshape(CH_DEV, SPAN)

    def window_cut(window_start):
        return lax.dynamic_slice_in_dim(decimated, window_start, WL, 1)

    segments = (jax.vmap(window_cut, out_axes=1)(window_starts) * make_taper()).astype(jnp.bfloat16)
    window_count = segments.shape[1]
    spectra = jnp.dot(segments.reshape(-1, WL), make_fourier(), preferred_element_type=jnp.float32)
    whitened = whiten(spectra).reshape(CH_DEV, window_count, WL)
    source = lax.dynamic_slice_in_dim(whitened, source_slot[0], 1, 0)
    gathered = lax.all_gather(source, "chan", axis=0, tiled=True)
    lag_table = make_lags()

    def span_block(source_block):
        cross_spectra = cross_spectrum(source_block, whitened)
        return jnp.dot(
            cross_spectra.reshape(-1, WL), lag_table, preferred_element_type=jnp.float32
        ).reshape(source_block.shape[0], CH_DEV, LAGS)

    return lax.psum_scatter(
        over_blocks(span_block, gathered, CH_DEV), "win", scatter_dimension=0, tiled=True
    )


def solution(mesh):
    in_specs = (
        P(("groups", "chan", "win"), None),
        P(("groups", "chan", "win")),
        P(("groups", "chan", "win")),
        P(),
        P(("groups", "win")),
        P(("groups", "chan")),
    )
    out_specs = P(("groups", "win"), "chan", None)
    body = gathered_body if mesh.shape["chan"] == 8 else routed_body
    return jax.shard_map(body, mesh=mesh, in_specs=in_specs, out_specs=out_specs, check_vma=False)
```

```python
import math

import jax
import jax.numpy as jnp
import ml_dtypes
import numpy as np
from jax import lax
from jax.experimental import pallas as pl
from jax.experimental.pallas import tpu as pltpu
from jax.sharding import PartitionSpec as P

CH_DEV = 16
SPAN = 2048
WIN_DEV = 8
WL = 1024
NF = 512
DEC = 4
TAPS = 32
SPILL = 7
SEG = 512
PIECES = 16
BAND = 64
LAGS = 256


EPSILON = 1e-06

LANES = 128
OUTS = SEG // DEC
AUX = 16
SCALE_ROW = SPILL
KEY_ROW = SPILL + 1
SLOT_ROW = SPILL + 2
FILTER_VMEM = 56 << 20
FLOPS = 10**10
EARLY_VMEM = 44 << 20
EARLY_FLOPS = 10**9
CORRELATE_VMEM = 40 << 20
LOCAL_ROWS = 32768
LAST_HOP = {1: 1, 2: 2, 3: 3, 4: 4, 6: 6, 5: 1, 7: 3}
EARLY = (0, 2, 1)
LATE = (4, 6, 5, 3, 7)
CODE = 23000.0


def fourier_table():
    sample_index = np.arange(WL)[:, None]
    freq_index = np.arange(NF)[None, :]
    phase = 2.0 * np.pi * (sample_index * freq_index % WL) / WL
    return np.concatenate([np.cos(phase), -np.sin(phase)], axis=1).astype(ml_dtypes.bfloat16)


def lag_table():
    freq_index = np.arange(NF)[:, None]
    lag_index = np.arange(LAGS)[None, :] - LAGS // 2
    phase = 2.0 * np.pi * (freq_index * lag_index % WL) / WL
    scale = 1.0 / math.sqrt(WL * WIN_DEV)
    tiles = (NF // LANES, 1, LANES, LAGS)
    parts = [np.cos(phase).reshape(tiles), -np.sin(phase).reshape(tiles)]
    return (np.concatenate(parts, axis=1).reshape(2 * NF, LAGS) * scale).astype(ml_dtypes.bfloat16)


def band_table():
    freq_index = np.arange(NF)
    return (np.abs(freq_index[:, None] - freq_index[None, :]) <= BAND).astype(ml_dtypes.bfloat16)


def split_rows(row):
    rows = []
    for _ in range(3):
        rows.append(row.astype(ml_dtypes.bfloat16))
        row = row - rows[-1].astype(np.float32)
    return rows


def wide_table():
    freq_index = np.arange(NF)
    band = np.abs(freq_index[:, None] - freq_index[None, :]) <= BAND
    taper = (0.5 - 0.5 * np.cos(2.0 * np.pi * np.arange(WL) / WL)).astype(np.float32)
    inverse = np.zeros(WL, np.float32)
    inverse[:NF] = 1.0 / band.sum(axis=0)
    empty = [np.zeros(WL, ml_dtypes.bfloat16)] * 10
    rows = np.stack(split_rows(taper) + split_rows(inverse) + empty)
    return np.concatenate([fourier_table(), rows], axis=0)


def filter_kernel(
    records_hbm, channel_hbm, piece_hbm, taps_hbm, slot_hbm, unit_hbm, *scratch
):
    records_ref, channel_ref, piece_ref, taps_ref, slot_ref, unit_ref, arrived = scratch
    f32 = jnp.float32
    count = records_ref.shape[0]
    pairs = (
        (taps_hbm, taps_ref),
        (records_hbm, records_ref),
        (channel_hbm, channel_ref),
        (piece_hbm, piece_ref),
        (slot_hbm, slot_ref),
    )
    copies = [
        pltpu.make_async_copy(source, target, arrived.at[number])
        for number, (source, target) in enumerate(pairs)
    ]
    for copy in copies:
        copy.start()
    tap = lax.broadcasted_iota(jnp.int32, (TAPS, SEG), 0)
    sample = lax.broadcasted_iota(jnp.int32, (TAPS, SEG), 1)
    place = (((DEC - 1 - tap) & (SEG - 1)) == sample).astype(f32).astype(jnp.bfloat16)
    copies[0].wait()
    taps = jnp.broadcast_to(taps_ref[...].reshape(1, TAPS), (16, TAPS))
    first = jnp.dot(taps, place, preferred_element_type=f32)
    circulant = pltpu.roll(
        jnp.broadcast_to(first[0:1], (OUTS, SEG)), 0, 1, stride=DEC, stride_axis=0
    )
    output = lax.broadcasted_iota(jnp.int32, (OUTS, SEG), 0)
    sample = lax.broadcasted_iota(jnp.int32, (OUTS, SEG), 1)
    inside = sample <= DEC * output + DEC - 1
    main_filter = jnp.where(inside, circulant, 0.0)
    spill_filter = jnp.where(inside, 0.0, circulant)[:AUX]
    filters = jnp.concatenate([main_filter, spill_filter], axis=0).astype(jnp.bfloat16)
    copies[1].wait()
    filtered = lax.dot_general(
        filters, records_ref[...], (((1,), (1,)), ((), ())), preferred_element_type=f32
    )
    absolute = jnp.abs(filtered)
    largest = jnp.maximum(jnp.max(absolute, axis=0, keepdims=True), 1e-30)
    power = jnp.minimum(jnp.floor(jnp.log2(largest)) + 1.0, 126.0)
    root = jnp.sqrt(jnp.sqrt(absolute * jnp.exp2(-power)))
    code = jnp.floor(root * CODE + 0.5)
    code = jnp.where(filtered < 0.0, -code, code)
    unit_ref[:OUTS] = code[:OUTS].astype(jnp.int32).astype(jnp.int16)
    for copy in copies[2:]:
        copy.wait()
    row = lax.broadcasted_iota(jnp.int32, (AUX, count), 0)
    key = channel_ref[...].reshape(1, count) * PIECES + piece_ref[...].reshape(1, count)
    side = jnp.where(row < SPILL, code[OUTS:].astype(jnp.int32), 0)
    side = jnp.where(row == SCALE_ROW, power.astype(jnp.int32), side)
    side = jnp.where(row == KEY_ROW, key, side)
    side = jnp.where(row == SLOT_ROW, slot_ref[0], side)
    unit_ref[OUTS:] = side.astype(jnp.int16)
    out = pltpu.make_async_copy(unit_ref, unit_hbm, arrived.at[0])
    out.start()
    out.wait()


def halves(code):
    first = (code >> 8).astype(jnp.float32).astype(jnp.bfloat16)
    return first, (code & 255).astype(jnp.float32).astype(jnp.bfloat16)


def decoded(code, scale):
    root = code * (1.0 / CODE)
    return (root * root) * (root * jnp.abs(root)) * scale


def lag_products(white_ref, lags_ref, rows, first, number):
    f32 = jnp.float32
    total = jnp.zeros((number * CH_DEV, LAGS), f32)
    for tile in range(NF // LANES):
        re = slice(tile * LANES, (tile + 1) * LANES)
        im = slice(NF + tile * LANES, NF + (tile + 1) * LANES)
        zero = jnp.zeros((CH_DEV, LANES), f32)
        sums = [[zero, zero, zero] for _ in range(number)]
        for window in range(WIN_DEV):
            own = slice(window * rows, window * rows + CH_DEV)
            loc_real = white_ref[own, re]
            loc_imag = white_ref[own, im]
            less = loc_real - loc_imag
            more = loc_real + loc_imag
            for source in range(number):
                at = window * rows + CH_DEV + first + source
                src_real = jnp.broadcast_to(white_ref[at : at + 1, re], (CH_DEV, LANES))
                src_imag = jnp.broadcast_to(white_ref[at : at + 1, im], (CH_DEV, LANES))
                sums[source][0] += loc_real * (src_real + src_imag)
                sums[source][1] += less * src_imag
                sums[source][2] += more * src_real
        real_sums = [both - imag for both, imag, real in sums]
        imag_sums = [both - real for both, imag, real in sums]
        cross = jnp.concatenate(
            [
                jnp.concatenate(real_sums, axis=0).astype(jnp.bfloat16),
                jnp.concatenate(imag_sums, axis=0).astype(jnp.bfloat16),
            ],
            axis=1,
        )
        total += jnp.dot(
            cross,
            lags_ref[2 * tile * LANES : 2 * (tile + 1) * LANES],
            preferred_element_type=f32,
        )
    return total


def pick_rows(pick_ref, key, first, group, wanted):
    shape = (2 * group, key.shape[1])
    key = jnp.broadcast_to(key, shape)
    for pair in range(PIECES // 2):
        pick_ref[pair * 2 * group : (pair + 1) * 2 * group, first : first + shape[1]] = jnp.where(
            wanted + 2 * pair == key, 1.0, 0.0
        ).astype(jnp.bfloat16)


def wanted_own(me, count):
    row = lax.broadcasted_iota(jnp.int32, (2 * CH_DEV, count), 0)
    odd = (row >= CH_DEV).astype(jnp.int32)
    return (me * CH_DEV + row - odd * CH_DEV) * PIECES + odd


def selected(data, pick):
    return lax.dot_general(data, pick, (((1,), (1,)), ((), ())), preferred_element_type=jnp.float32)


def early_kernel(early_total, *refs):
    unit_hbm = refs[0]
    units_ref = refs[1:early_total]
    own_ref, data_ref, side_ref, pick_ref, unit_ref, arrived = refs[early_total:]
    copy = pltpu.make_async_copy(unit_hbm, unit_ref, arrived)
    copy.start()
    count = unit_ref.shape[1]
    wanted = wanted_own(lax.axis_index("chan"), count)

    def take(unit, number):
        at = slice(number * count, (number + 1) * count)
        codes = unit[...].astype(jnp.int32)
        first, second = halves(codes)
        data_ref[: OUTS + AUX, at] = first
        data_ref[OUTS + AUX :, at] = second
        side_ref[:, at] = codes[OUTS:]
        pick_rows(pick_ref, codes[OUTS + KEY_ROW : OUTS + KEY_ROW + 1], number * count, CH_DEV, wanted)

    for number in range(1, early_total):
        take(units_ref[number - 1], number)
    own_ref[...] = selected(data_ref[:, count:], pick_ref[:, count:])
    copy.wait()
    take(unit_ref, 0)
    own_ref[...] += selected(data_ref[:, :count], pick_ref[:, :count])


def samples_of(picked, group):
    code = picked[: OUTS + AUX] * 256.0 + picked[OUTS + AUX :]
    scale = jnp.exp2(code[OUTS + SCALE_ROW : OUTS + SCALE_ROW + 1])
    main_part = decoded(code[:OUTS], scale)
    spill_part = pltpu.roll(decoded(code[OUTS:], scale), group, 1)
    row = lax.broadcasted_iota(jnp.int32, spill_part.shape, 0)
    column = lax.broadcasted_iota(jnp.int32, spill_part.shape, 1)
    spill_part = jnp.where((row < SPILL) & (column >= group), spill_part, 0.0)
    return jnp.transpose(jnp.concatenate([main_part[:AUX] + spill_part, main_part[AUX:]], axis=0))


def correlate_kernel(block_total, span_total, *refs):
    f32 = jnp.float32
    own_ref, data_ref, side_ref, starts_hbm, slot_ref = refs[:5]
    refs = refs[5:]
    units_ref = dict(zip(LATE, refs))
    refs = refs[len(LATE) :]
    wide_ref, band_ref, lags_ref, send_ref, white_ref = refs[:5]
    pick_own_ref, pick_src_ref, dec_ref, seg_ref, starts_ref, arrived = refs[5:]
    copy = pltpu.make_async_copy(starts_hbm, starts_ref, arrived)
    copy.start()
    me = lax.axis_index("chan")
    half = lax.axis_index("win")
    rows = CH_DEV + block_total
    count = side_ref.shape[1] // len(EARLY)
    late = {step: unit[...].astype(jnp.int32) for step, unit in units_ref.items()}
    sides = {step: side_ref[:, n * count : (n + 1) * count] for n, step in enumerate(EARLY)}
    sides |= {step: codes[OUTS:] for step, codes in late.items()}
    row = lax.broadcasted_iota(jnp.int32, (2 * block_total, count), 0)
    odd = (row >= block_total).astype(jnp.int32)
    source = (row + (1 + half) * (block_total // span_total)) % block_total
    channel = source * CH_DEV + slot_ref[0]
    for step, side in sides.items():
        if step:
            slot = jnp.broadcast_to(side[SLOT_ROW : SLOT_ROW + 1], source.shape)
            channel = jnp.where(source == (me ^ step), source * CH_DEV + slot, channel)
    wanted = channel * PIECES + odd
    own = wanted_own(me, count)
    for number, step in enumerate(EARLY + LATE):
        key = sides[step][KEY_ROW : KEY_ROW + 1]
        pick_rows(pick_src_ref, key, number * count, block_total, wanted)
        if step in late:
            pick_rows(pick_own_ref, key, (number - len(EARLY)) * count, CH_DEV, own)
    codes = jnp.concatenate([late[step] for step in LATE], axis=1)
    late_data = jnp.concatenate(halves(codes), axis=0)
    split = len(EARLY) * count
    picked_src = selected(data_ref[...], pick_src_ref[:, :split])
    picked_src += selected(late_data, pick_src_ref[:, split:])
    picked_own = own_ref[...] + selected(late_data, pick_own_ref[...])
    samples = samples_of(picked_own, CH_DEV)
    sources = samples_of(picked_src, block_total)
    for piece in range(PIECES):
        at = slice(piece * OUTS, (piece + 1) * OUTS)
        dec_ref[:CH_DEV, at] = samples[piece * CH_DEV : (piece + 1) * CH_DEV]
        dec_ref[CH_DEV:, at] = sources[piece * block_total : (piece + 1) * block_total]
    dec_ref[:, SPAN:] = jnp.zeros((rows, LANES), f32)
    lane = lax.broadcasted_iota(jnp.int32, (rows, LANES), 1)
    extra = wide_ref[WL:].astype(f32)
    taper = extra[0:1] + extra[1:2] + extra[2:3]
    inverse = (extra[3:4] + extra[4:5] + extra[5:6])[:, :NF]
    copy.wait()
    for window in range(WIN_DEV):
        start = starts_ref[window]
        base = pl.multiple_of((start >> 7) * LANES, LANES)
        offset = start & (LANES - 1)
        shift = (LANES - offset) & (LANES - 1)
        chunks = [
            pltpu.roll(dec_ref[:, pl.ds(base + tile * LANES, LANES)], shift, 1)
            for tile in range(WL // LANES + 1)
        ]
        here = lane < LANES - offset
        for tile in range(WL // LANES):
            at = slice(tile * LANES, (tile + 1) * LANES)
            seg_ref[window * rows : (window + 1) * rows, at] = (
                jnp.where(here, chunks[tile], chunks[tile + 1]) * taper[:, at]
            )
    spectra = jnp.dot(
        seg_ref[...].astype(jnp.bfloat16), wide_ref[:WL], preferred_element_type=f32
    )
    real = spectra[:, :NF]
    imag = spectra[:, NF:]
    energy = real * real + imag * imag
    high = energy.astype(jnp.bfloat16)
    low = (energy - high.astype(f32)).astype(jnp.bfloat16)
    sums = jnp.dot(
        jnp.concatenate([high, low], axis=0), band_ref[...], preferred_element_type=f32
    )
    smooth = (sums[: energy.shape[0]] + sums[energy.shape[0] :]) * inverse
    scale = lax.rsqrt(smooth + EPSILON)
    white_ref[:, :NF] = (real * scale).astype(jnp.bfloat16).astype(f32)
    white_ref[:, NF:] = (imag * scale).astype(jnp.bfloat16).astype(f32)
    send_ref[...] = lag_products(white_ref, lags_ref, rows, 0, block_total // span_total)


def keep_kernel(rows, first, number, white_ref, lags_ref, keep_ref):
    keep_ref[...] = lag_products(white_ref, lags_ref, rows, first, number)


def gathered_body(records, record_channel, record_piece, fir_taps, window_starts, source_slot):
    block_total = lax.axis_size("chan")
    span_total = lax.axis_size("win")
    vmem = pl.BlockSpec(memory_space=pltpu.VMEM)
    smem = pl.BlockSpec(memory_space=pltpu.SMEM)
    hbm = pl.BlockSpec(memory_space=pl.ANY)
    count = records.shape[0]
    unit_shape = (OUTS + AUX, count)
    unit = pl.pallas_call(
        filter_kernel,
        out_shape=(
            jax.ShapeDtypeStruct(unit_shape, jnp.int16)
        ),
        in_specs=[hbm] * 5,
        out_specs=hbm,
        scratch_shapes=[
            pltpu.VMEM(records.shape, records.dtype),
            pltpu.VMEM(record_channel.shape, jnp.int32),
            pltpu.VMEM(record_piece.shape, jnp.int32),
            pltpu.VMEM(fir_taps.shape, fir_taps.dtype),
            pltpu.SMEM((1,), jnp.int32),
            pltpu.VMEM(unit_shape, jnp.int16),
            pltpu.SemaphoreType.DMA((5,)),
        ],
        compiler_params=pltpu.CompilerParams(vmem_limit_bytes=FILTER_VMEM),
        cost_estimate=pl.CostEstimate(flops=FLOPS, bytes_accessed=1 << 20, transcendentals=0),
        name="filter",
    )(records, record_channel, record_piece, fir_taps, source_slot)

    def swap(value, step):
        return lax.ppermute(value, "chan", [(i, i ^ step) for i in range(block_total)])

    units = {0: unit}
    for step, last in LAST_HOP.items():
        units[step] = swap(units[step ^ last], last)
    rows = CH_DEV + block_total
    half_rows = block_total // span_total * CH_DEV
    half_shape = jax.ShapeDtypeStruct((half_rows, LAGS), jnp.float32)
    tables = [wide_table(), band_table(), lag_table()]
    lags = jnp.asarray(tables[2])
    half_count = block_total // span_total
    data_shape = (2 * unit_shape[0], len(EARLY) * count)
    own, data, side = pl.pallas_call(
        lambda *refs: early_kernel(len(EARLY), *refs),
        out_shape=(
            jax.ShapeDtypeStruct((2 * unit_shape[0], PIECES * CH_DEV), jnp.float32),
            jax.ShapeDtypeStruct(data_shape, jnp.bfloat16),
            jax.ShapeDtypeStruct((AUX, len(EARLY) * count), jnp.int32),
        ),
        in_specs=[hbm] + [vmem] * (len(EARLY) - 1),
        out_specs=(vmem, vmem, vmem),
        scratch_shapes=[
            pltpu.VMEM((PIECES * CH_DEV, len(EARLY) * count), jnp.bfloat16),
            pltpu.VMEM(unit_shape, jnp.int16),
            pltpu.SemaphoreType.DMA,
        ],
        compiler_params=pltpu.CompilerParams(vmem_limit_bytes=EARLY_VMEM),
        cost_estimate=pl.CostEstimate(flops=EARLY_FLOPS, bytes_accessed=1 << 20, transcendentals=0),
        name="early",
    )(unit, *[units[step] for step in EARLY[1:]])
    send, white = pl.pallas_call(
        lambda *refs: correlate_kernel(block_total, span_total, *refs),
        out_shape=(half_shape, jax.ShapeDtypeStruct((WIN_DEV * rows, WL), jnp.float32)),
        in_specs=[vmem, vmem, vmem, hbm, smem] + [vmem] * (len(LATE) + 3),
        out_specs=(vmem, vmem),
        scratch_shapes=[
            pltpu.VMEM((PIECES * CH_DEV, len(LATE) * count), jnp.bfloat16),
            pltpu.VMEM((PIECES * block_total, block_total * count), jnp.bfloat16),
            pltpu.VMEM((rows, SPAN + LANES), jnp.float32),
            pltpu.VMEM((WIN_DEV * rows, WL), jnp.float32),
            pltpu.SMEM((WIN_DEV,), jnp.int32),
            pltpu.SemaphoreType.DMA,
        ],
        compiler_params=pltpu.CompilerParams(vmem_limit_bytes=CORRELATE_VMEM),
        name="correlate",
    )(
        own,
        data,
        side,
        window_starts,
        source_slot,
        *[units[step] for step in LATE],
        *[jnp.asarray(table) for table in tables[:2]],
        lags,
    )
    other = lax.ppermute(send, "win", [(i, i ^ 1) for i in range(span_total)])
    keep = pl.pallas_call(
        lambda *refs: keep_kernel(rows, half_count, half_count, *refs),
        out_shape=half_shape,
        in_specs=[vmem, vmem],
        out_specs=vmem,
        compiler_params=pltpu.CompilerParams(vmem_limit_bytes=32 << 20),
        name="keep",
    )(white, lags)
    return (keep + other).reshape(block_total // span_total, CH_DEV, LAGS)


def make_filter(fir_taps):
    outputs_per = SEG // DEC
    sample_index = jnp.arange(SEG, dtype=jnp.int32)[:, None]
    column_index = jnp.arange(outputs_per + SPILL, dtype=jnp.int32)[None, :]
    tap_index = jnp.where(
        column_index < outputs_per,
        DEC * column_index + DEC - 1 - sample_index,
        DEC * (column_index - outputs_per) + DEC - 1 + SEG - sample_index,
    )
    match_table = (
        tap_index[:, :, None] == jnp.arange(TAPS, dtype=jnp.int32)[None, None, :]
    ).astype(jnp.float32)
    return jnp.sum(match_table * fir_taps.astype(jnp.float32)[None, None, :], axis=2).astype(
        jnp.bfloat16
    )


def make_fourier():
    sample_index = jnp.arange(WL, dtype=jnp.int32)[:, None]
    freq_index = jnp.arange(NF, dtype=jnp.int32)[None, :]
    phase = 2.0 * math.pi * (sample_index * freq_index % WL).astype(jnp.float32) / WL
    return jnp.concatenate([jnp.cos(phase), -jnp.sin(phase)], axis=1).astype(jnp.bfloat16)


def make_taper():
    sample_index = jnp.arange(WL, dtype=jnp.int32).astype(jnp.float32)
    return 0.5 - 0.5 * jnp.cos(2.0 * math.pi * sample_index / WL)


def make_lags():
    freq_index = jnp.arange(NF, dtype=jnp.int32)[:, None]
    lag_index = jnp.arange(LAGS, dtype=jnp.int32)[None, :] - LAGS // 2
    phase = 2.0 * math.pi * (freq_index * lag_index % WL).astype(jnp.float32) / WL
    scale = 1.0 / math.sqrt(WL * WIN_DEV)
    return (jnp.concatenate([jnp.cos(phase), -jnp.sin(phase)], axis=0) * scale).astype(jnp.bfloat16)


def whiten(spectra):
    freq_index = jnp.arange(NF, dtype=jnp.int32)
    band_table = (jnp.abs(freq_index[:, None] - freq_index[None, :]) <= BAND).astype(jnp.float32)
    band_count = jnp.sum(band_table, axis=0)
    real_part = spectra[..., :NF]
    imag_part = spectra[..., NF:]
    energy = real_part * real_part + imag_part * imag_part
    smooth = jnp.dot(energy, band_table, precision=lax.Precision.HIGHEST) / band_count[None, :]
    amplitude = jnp.sqrt(smooth + EPSILON)
    return (spectra / jnp.concatenate([amplitude, amplitude], axis=-1)).astype(jnp.bfloat16)


def cross_spectrum(source_block, local_block):
    src_real = source_block[..., :NF]
    src_imag = source_block[..., NF:]
    loc_real = local_block[..., :NF]
    loc_imag = local_block[..., NF:]
    real_sum = jnp.einsum(
        "bwf,cwf->bcf", src_real, loc_real, preferred_element_type=jnp.float32
    ) + jnp.einsum("bwf,cwf->bcf", src_imag, loc_imag, preferred_element_type=jnp.float32)
    imag_sum = jnp.einsum(
        "bwf,cwf->bcf", src_imag, loc_real, preferred_element_type=jnp.float32
    ) - jnp.einsum("bwf,cwf->bcf", src_real, loc_imag, preferred_element_type=jnp.float32)
    return jnp.concatenate([real_sum, imag_sum], axis=-1).astype(jnp.bfloat16)


def over_blocks(block_fn, sources, channel_count):
    source_count = sources.shape[0]
    block_size = math.gcd(source_count, 16)
    block_count = source_count // block_size
    grouped = sources.reshape((block_count, block_size) + sources.shape[1:])
    return lax.map(block_fn, grouped).reshape(source_count, channel_count, LAGS)


def routed_body(records, record_channel, record_piece, fir_taps, window_starts, source_slot):
    block_total = lax.axis_size("chan")
    per_device = records.shape[0]
    capacity = 2 * per_device // block_total
    outputs_per = SEG // DEC
    owner_block = record_channel // CH_DEV
    local_slot = record_channel % CH_DEV * PIECES + record_piece
    one_hot = (owner_block[:, None] == jnp.arange(block_total, dtype=jnp.int32)[None, :]).astype(
        jnp.int32
    )
    earlier_count = jnp.sum((jnp.cumsum(one_hot, axis=0) - one_hot) * one_hot, axis=1)
    position = owner_block * capacity + earlier_count
    slot_table = (
        jnp.full((block_total * capacity,), -1, jnp.int32)
        .at[position]
        .set(local_slot)
        .reshape(block_total, capacity)
    )
    filter_matrix = make_filter(fir_taps)
    row_send = (
        jnp.zeros((block_total * capacity, SEG), jnp.bfloat16)
        .at[position]
        .set(records)
        .reshape(block_total, capacity, SEG)
    )
    rows_got, slots_got = (
        lax.all_to_all(row_send, "chan", split_axis=0, concat_axis=0, tiled=True),
        lax.all_to_all(slot_table, "chan", split_axis=0, concat_axis=0, tiled=True),
    )
    flat_slots = slots_got.reshape(-1)
    target = jnp.where(flat_slots >= 0, flat_slots, per_device)
    traces = (
        jnp.zeros((per_device, SEG), jnp.bfloat16)
        .at[target]
        .set(rows_got.reshape(-1, SEG), mode="drop")
    )
    filtered = jnp.dot(traces, filter_matrix, preferred_element_type=jnp.float32)
    main_part = filtered[:, :outputs_per]
    spill_part = filtered[:, outputs_per:]
    main_part = main_part.reshape(CH_DEV, PIECES, outputs_per)
    spill_part = spill_part.reshape(CH_DEV, PIECES, SPILL)
    carried = jnp.pad(spill_part[:, :-1, :], ((0, 0), (1, 0), (0, outputs_per - SPILL)))
    decimated = (main_part + carried).reshape(CH_DEV, SPAN)

    def window_cut(window_start):
        return lax.dynamic_slice_in_dim(decimated, window_start, WL, 1)

    segments = (jax.vmap(window_cut, out_axes=1)(window_starts) * make_taper()).astype(jnp.bfloat16)
    window_count = segments.shape[1]
    spectra = jnp.dot(segments.reshape(-1, WL), make_fourier(), preferred_element_type=jnp.float32)
    whitened = whiten(spectra).reshape(CH_DEV, window_count, WL)
    source = lax.dynamic_slice_in_dim(whitened, source_slot[0], 1, 0)
    gathered = lax.all_gather(source, "chan", axis=0, tiled=True)
    lag_table = make_lags()

    def span_block(source_block):
        cross_spectra = cross_spectrum(source_block, whitened)
        return jnp.dot(
            cross_spectra.reshape(-1, WL), lag_table, preferred_element_type=jnp.float32
        ).reshape(source_block.shape[0], CH_DEV, LAGS)

    return lax.psum_scatter(
        over_blocks(span_block, gathered, CH_DEV), "win", scatter_dimension=0, tiled=True
    )


def solution(mesh):
    in_specs = (
        P(("groups", "chan", "win"), None),
        P(("groups", "chan", "win")),
        P(("groups", "chan", "win")),
        P(),
        P(("groups", "win")),
        P(("groups", "chan")),
    )
    out_specs = P(("groups", "win"), "chan", None)
    body = gathered_body if mesh.shape["chan"] == 8 else routed_body
    return jax.shard_map(body, mesh=mesh, in_specs=in_specs, out_specs=out_specs, check_vma=False)
```
